32 devices in a mesh: bins: 4 (over y, x), batch: 4 (over z), fsdp: 2 (over core).
Axes of the slice: x: 2, y: 2, z: 4, core: 2. Of those that a mesh axis runs over, the one named last changes fastest.
Arguments:
- track_in: bfloat16 [64, 1024, 768], P(('batch', 'fsdp'), 'bins'), may hold values from -6 to 6
- black_mask: int32 [64, 1024], P(('batch', 'fsdp'), 'bins'), may hold values 0 or 1
- unmap_mask: int32 [64, 1024], P(('batch', 'fsdp'), 'bins'), may hold values 0 or 1
- seq_valid: int32 [64], P(('batch', 'fsdp')), may hold values from 256 to 1024
- dilated_weight: float32 [2304, 384], P(('batch', 'fsdp')), may hold values from -0.125 to 0.125
- point_weight: float32 [384, 768], P(('batch', 'fsdp')), may hold values from -0.30618622 to 0.30618622
- point_bias: float32 [768], P(('batch', 'fsdp')), may hold values from -3 to 3
- gain_first: float32 [768], P(('batch', 'fsdp')), may hold values from 0.5 to 2
- shift_first: float32 [768], P(('batch', 'fsdp')), may hold values from -3 to 3
- gain_second: float32 [384], P(('batch', 'fsdp')), may hold values from 0.5 to 2
- shift_second: float32 [384], P(('batch', 'fsdp')), may hold values from -3 to 3
- out_grad: bfloat16 [64, 1024, 768], P(('batch', 'fsdp'), 'bins'), may hold values from -8 to 8
Outputs:
- block_out: bfloat16 [64, 1024, 768], P(('batch', 'fsdp'), 'bins')
- input_grad: bfloat16 [64, 1024, 768], P(('batch', 'fsdp'), 'bins')
- dilated_grad: float32 [2304, 384], P(('batch', 'fsdp'))
- point_grad: float32 [384, 768], P(('batch', 'fsdp'))
- bias_grad: float32 [768], P(('batch', 'fsdp'))
- gain_first_grad: float32 [768], P(('batch', 'fsdp'))
- shift_first_grad: float32 [768], P(('batch', 'fsdp'))
- gain_second_grad: float32 [384], P(('batch', 'fsdp'))
- shift_second_grad: float32 [384], P(('batch', 'fsdp'))
The draws below stay inside these ranges and needn't reach their ends.
All inputs are finite; a program needn't handle non-finite values. No bound on the sum of `black_mask` or of `unmap_mask` on one device may be relied on, other than what follows from the above.
Results may differ from the reference program's by a relative error of at most 0.0074.
Values may be sent and summed in bfloat16 or wider, within the bound.
A program may use at most 128 MiB of HBM per device.

```python
import math
import jax
import jax.numpy as jnp
from jax import lax

D = 768
H = 384
DILATION_STEP = 26
SEQ_DEV = 8
LEN = 1024
SEQS = 64


def stream_noise(key):
    shape = (SEQS, LEN, D)
    return jax.random.normal(jax.random.fold_in(key, 101), shape, jnp.float32)


def input_values(key):
    offset = jax.random.normal(jax.random.fold_in(key, 103), (D,), jnp.float32)
    return jnp.clip(stream_noise(key) + offset, -6.0, 6.0)


def point_base(key):
    values = jax.random.normal(jax.random.fold_in(key, 106), (H, D), jnp.float32)
    return jnp.clip(values, -6.0, 6.0) * H ** (-0.5)


def draw_track_in(key, part):
    return input_values(key).astype(jnp.bfloat16)


def draw_out_grad(key, part):
    groups = SEQS // SEQ_DEV
    width = D // groups
    noise = jax.random.normal(jax.random.fold_in(key, 104), (SEQS, LEN, D), jnp.float32)
    ramp = 0.5 + jnp.arange(SEQS, dtype=jnp.float32) / (SEQS - 1)
    pairing = jax.random.permutation(jax.random.fold_in(key, 105), groups)
    owner = pairing[jnp.arange(SEQS) // SEQ_DEV]
    block = jnp.arange(D) // width
    spike = 1.0 + 1.5 * (block[None, :] == owner[:, None]).astype(jnp.float32)
    values = (0.5 * noise + input_values(key)) * ramp[:, None, None] * spike[:, None, :]
    return jnp.clip(values, -8.0, 8.0).astype(jnp.bfloat16)


def draw_point_weight(key, part):
    return point_base(key)


def draw_dilated_weight(key, part):
    outer = jnp.clip(jax.random.normal(jax.random.fold_in(key, 107), (2, D, H), jnp.float32), -6.0, 6.0) * (3 * D) ** (-0.5)
    middle = 0.4 * jnp.transpose(point_base(key))
    return jnp.concatenate([outer[0], middle, outer[1]], axis=0)


def place_ends(entries, key, smallest, top_value):
    longest = entries.shape.index(max(entries.shape))
    spots = []
    for shift in (0, 1):
        where = [jax.random.randint(jax.random.fold_in(key, axis), (), 0, length) for axis, length in enumerate(entries.shape)]
        where[longest] = (where[longest] + shift) % entries.shape[longest]
        spots.append(tuple(where))
    return entries.at[spots[0]].set(smallest).at[spots[1]].set(top_value)


def block_scale(key, extent, split, least, largest):
    def one(position, parts):
        draws = jax.random.uniform(jax.random.fold_in(jax.random.fold_in(key, 6), position), (parts,), jnp.float32, least / len(split), largest / len(split))
        return jnp.repeat(jnp.exp(draws), extent[position] // parts).reshape((-1,) + (1,) * (len(extent) - position - 1))

    loudness = one(*split[0])
    for cut in split[1:]:
        loudness = loudness * one(*cut)
    return loudness


def gaussian(own_key, extent, deviation, limit, pieces=(), kind=jnp.bfloat16):
    level = block_scale(own_key, extent, pieces, -0.22, 0.18) if pieces else 1.0
    values = jax.random.normal(own_key, extent, jnp.float32) * deviation * level
    return jnp.minimum(jnp.maximum(values, -limit), limit).astype(kind)


def setup_inputs(seed: int = 0) -> dict:
    keys = jax.random.split(jax.random.key(seed), 13)
    track_in = draw_track_in(jax.random.fold_in(keys[12], 71), 0)
    black_mask = place_ends((jax.random.randint(keys[1], (SEQS, LEN), 0, 16) < 1).astype(jnp.int32), jax.random.fold_in(keys[1], 1), 0, 1)
    unmap_mask = place_ends((jax.random.randint(keys[2], (SEQS, LEN), 0, 8) < 1).astype(jnp.int32), jax.random.fold_in(keys[2], 1), 0, 1)
    seq_valid = place_ends(jax.random.randint(keys[3], (SEQS,), LEN // 4, LEN + 1), jax.random.fold_in(keys[3], 1), LEN // 4, LEN).astype(jnp.int32)
    dilated_weight = draw_dilated_weight(jax.random.fold_in(keys[12], 71), 0)
    point_weight = draw_point_weight(jax.random.fold_in(keys[12], 71), 0)
    point_bias = gaussian(keys[6], (D,), 0.5, 3.0, ((0, 8),), jnp.float32)
    gain_first = jnp.clip(jnp.exp(math.log(2.0) - 1.3862944 * jax.random.uniform(keys[7], (D,), jnp.float32) ** block_scale(keys[7], (D,), ((0, 8),), -0.2, 0.2)), 0.5, 2.0)
    shift_first = gaussian(keys[8], (D,), 0.5, 3.0, ((0, 8),), jnp.float32)
    gain_second = jnp.clip(jnp.exp(math.log(2.0) - 1.3862944 * jax.random.uniform(keys[9], (H,), jnp.float32) ** block_scale(keys[9], (H,), ((0, 8),), -0.2, 0.2)), 0.5, 2.0)
    shift_second = gaussian(keys[10], (H,), 0.5, 3.0, ((0, 8),), jnp.float32)
    out_grad = draw_out_grad(jax.random.fold_in(keys[12], 71), 0)
    return {"track_in": track_in, "black_mask": black_mask, "unmap_mask": unmap_mask, "seq_valid": seq_valid, "dilated_weight": dilated_weight, "point_weight": point_weight, "point_bias": point_bias, "gain_first": gain_first, "shift_first": shift_first, "gain_second": gain_second, "shift_second": shift_second, "out_grad": out_grad}


@jax.custom_vjp
def lower_bound(v):
    return lax.optimization_barrier(v.astype(jnp.bfloat16)).astype(jnp.float32)

@jax.custom_vjp
def lower_backward(v):
    return v

def low_keep(v):
    return (lower_bound(v), None)

def low_pass(kept, grad):
    return (grad,)

def back_keep(v):
    return (v, None)

def back_low(kept, grad):
    return (lower_bound(grad),)
lower_bound.defvjp(low_keep, low_pass)
lower_backward.defvjp(back_keep, back_low)

def activate(values):
    return values * jax.nn.sigmoid(1.702 * values)

def normalize(values, valid, count, gain, shift):
    mean = lax.optimization_barrier(jnp.sum(values * valid, axis=(0, 1))) / count
    centred = values - mean
    variance = lax.optimization_barrier(jnp.sum(centred * centred * valid, axis=(0, 1))) / count
    return centred * lax.rsqrt(variance + 1e-05) * gain + shift

def dilated_output(first_hidden, weight):
    bins_total_count = first_hidden.shape[1]
    channel_count = first_hidden.shape[2]
    padded_input = jnp.pad(first_hidden, ((0, 0), (DILATION_STEP, DILATION_STEP), (0, 0)))
    total = jnp.zeros((first_hidden.shape[0], bins_total_count, weight.shape[1]), jnp.float32)
    for kernel_tap_index in range(3):
        sliding_window = padded_input[:, kernel_tap_index * DILATION_STEP:kernel_tap_index * DILATION_STEP + bins_total_count, :]
        kernel = weight[kernel_tap_index * channel_count:(kernel_tap_index + 1) * channel_count]
        total = total + jnp.einsum('btc,ch->bth', sliding_window, kernel, precision=lax.Precision.HIGHEST)
    return total

def reference(track_in, black_mask, unmap_mask, seq_valid, dilated_weight, point_weight, point_bias, gain_first, shift_first, gain_second, shift_second, out_grad):
    place = lax.broadcasted_iota(jnp.int32, black_mask.shape, 1)
    keep = (black_mask == 0) & (unmap_mask == 0) & (place < seq_valid[:, None])
    valid = keep.astype(jnp.float32)[:, :, None]
    count = jnp.sum(valid)

    def forward_pass(input_signal, dilation_weight, pointwise_weight, bias_vector, first_gain, first_offset, second_gain, second_offset):
        dilation_weight = lower_bound(dilation_weight)
        pointwise_weight = lower_bound(pointwise_weight)
        bias_vector = lower_bound(bias_vector)
        first_gain = lower_bound(first_gain)
        first_offset = lower_bound(first_offset)
        second_gain = lower_bound(second_gain)
        second_offset = lower_bound(second_offset)
        first_hidden = lower_bound(activate(normalize(input_signal, valid, count, first_gain, first_offset)))
        convolution_output = lower_backward(dilated_output(first_hidden, dilation_weight))
        hidden_two = lower_bound(activate(normalize(convolution_output, valid, count, second_gain, second_offset)))
        branch = lower_backward(jnp.einsum('bth,hd->btd', hidden_two, pointwise_weight, precision=lax.Precision.HIGHEST))
        return input_signal + branch + bias_vector
    primals = (track_in.astype(jnp.float32), dilated_weight, point_weight, point_bias, gain_first, shift_first, gain_second, shift_second)
    result, pull = jax.vjp(forward_pass, *primals)
    grads = pull(out_grad.astype(jnp.float32) * valid)
    return (result.astype(jnp.bfloat16), grads[0].astype(jnp.bfloat16), grads[1], grads[2], grads[3], grads[4], grads[5], grads[6], grads[7])
```

```python
import functools

import jax
import jax.numpy as jnp
from jax import lax
from jax.experimental import pallas as pl
from jax.experimental.pallas import tpu as pltpu
from jax.sharding import PartitionSpec as P

STEP = 26
EPS = 1e-5
PAD = 32
CHUNK = 32
MESH = pl.DeviceIdType.MESH
BF = jnp.bfloat16
F32 = jnp.float32


def dot(a, b, ca, cb):
    return lax.dot_general(a, b, (((ca,), (cb,)), ((), ())), preferred_element_type=F32)


def fold(v):
    rows, width = v.shape
    return jnp.sum(v.reshape(rows // 8, 8, width), axis=0)


def merge(entries):
    total = functools.reduce(jnp.add, [e[0] for e in entries])
    count = functools.reduce(jnp.add, [e[2] for e in entries])
    mean = total / jnp.maximum(count, 1.0)
    square = functools.reduce(jnp.add, [e[1] for e in entries])
    for s, _, n in entries:
        gap = s / jnp.maximum(n, 1.0) - mean
        square = square + n * gap * gap
    return total, square, count


def block(
    sizes,
    x_hbm, og_hbm, black, unmap, limit, wd, wp, par,
    out_hbm, gin_hbm, dwd, dwp, small,
    xpad, grad, vm, h1, z1, gw, h2, dz, taps, dg, stage,
    fs1, fr1, cs1, cr1, fs2, fr2, cs2, cr2, fs3, fr3, cs3, cr3, fs4, fr4, cs4, cr4,
    xsem, gsem, osem, isem, hsem, hrem, zsem, zrem, fss, frs, css, crs,
):
    nb, nz, nf = sizes
    seqs, bins, chans = grad.shape
    hid = z1.shape[2]
    wide, narrow = chans // 128, hid // 128
    pieces = bins // CHUNK
    bi, zi, fi = lax.axis_index("bins"), lax.axis_index("batch"), lax.axis_index("fsdp")

    def load_x(s):
        return pltpu.make_async_copy(x_hbm.at[s], xpad.at[s, pl.ds(PAD, bins), :], xsem.at[s])

    def load_g(s):
        return pltpu.make_async_copy(og_hbm.at[s], grad.at[s], gsem.at[s])

    for s in range(seqs):
        load_x(s).start()
    for s in range(seqs):
        load_g(s).start()

    mates = [(k,) for k in range(1, nf)]
    chips = [(b, z) for z in range(nz) for b in range(nb) if (b, z) != (0, 0)]

    def mate(k):
        return {"fsdp": lax.rem(fi + k, nf)}

    def chip(b, z):
        return {"bins": lax.rem(bi + b, nb), "batch": lax.rem(zi + z, nz)}

    barrier = pltpu.get_barrier_semaphore()
    for (k,) in mates:
        pl.semaphore_signal(barrier, inc=1, device_id=mate(k), device_id_type=MESH)
    for b, z in chips:
        pl.semaphore_signal(barrier, inc=1, device_id=chip(b, z), device_id_type=MESH)

    place = bi * bins + lax.broadcasted_iota(jnp.int32, (seqs, bins), 1)
    keep = (black[...] == 0) & (unmap[...] == 0) & (place < limit[...])
    columns = jnp.transpose(keep.astype(F32))
    tally = jnp.zeros((8, 128), F32)
    for s in range(seqs):
        lanes = jnp.broadcast_to(columns[:, s : s + 1], (bins, 128))
        vm[s] = lanes
        tally = tally + fold(lanes)
    own_count = jnp.sum(tally, axis=0, keepdims=True)

    def mask(s, r, copies):
        m = vm[s, r * CHUNK : (r + 1) * CHUNK, :]
        return jnp.concatenate([m] * copies, axis=1)

    pl.semaphore_wait(barrier, len(mates) + len(chips))

    low, high = lax.rem(bi + nb - 1, nb), lax.rem(bi + 1, nb)

    def edge_copies(src, dst, send, recv):
        to_low = pltpu.make_async_remote_copy(
            src_ref=src(0), dst_ref=dst(PAD + bins), send_sem=send.at[0], recv_sem=recv.at[0],
            device_id={"bins": low}, device_id_type=MESH,
        )
        to_high = pltpu.make_async_remote_copy(
            src_ref=src(bins - PAD), dst_ref=dst(0), send_sem=send.at[1], recv_sem=recv.at[1],
            device_id={"bins": high}, device_id_type=MESH,
        )
        return to_low, to_high

    x_low, x_high = edge_copies(
        lambda r: x_hbm.at[:, pl.ds(r, PAD), :], lambda r: xpad.at[:, pl.ds(r, PAD), :], hsem, hrem
    )

    def edge_start(to_low, to_high):
        @pl.when(bi > 0)
        def _():
            to_low.start()

        @pl.when(bi < nb - 1)
        def _():
            to_high.start()

    def edge_wait(to_low, to_high):
        @pl.when(bi < nb - 1)
        def _():
            to_low.wait_recv()
            to_high.wait_send()

        @pl.when(bi > 0)
        def _():
            to_high.wait_recv()
            to_low.wait_send()

    edge_start(x_low, x_high)

    def mate_copies(i, src, dst):
        return [
            pltpu.make_async_remote_copy(
                src_ref=src, dst_ref=dst.at[j], send_sem=fss.at[i, j], recv_sem=frs.at[i, j],
                device_id=mate(k), device_id_type=MESH,
            )
            for j, (k,) in enumerate(mates)
        ]

    def chip_copies(i, src, dst):
        return [
            pltpu.make_async_remote_copy(
                src_ref=src, dst_ref=dst.at[j], send_sem=css.at[i, j], recv_sem=crs.at[i, j],
                device_id=chip(b, z), device_id_type=MESH,
            )
            for j, (b, z) in enumerate(chips)
        ]

    def start(copies):
        for c in copies:
            c.start()

    def wait(copies):
        for c in copies:
            c.wait_recv()
        for c in copies:
            c.wait_send()

    def plain_sum(i, fs, fr, cs, cr, rows, filler):
        mine = mate_copies(i, fs, fr)
        start(mine)
        wait(mine)
        both = fs[...]
        for j in range(len(mates)):
            both = both + fr[j]
        cs[...] = both
        far = chip_copies(i, cs, cr)
        start(far)
        filler()
        wait(far)
        total = cs[...]
        for j in range(len(chips)):
            total = total + cr[j]
        return total

    def sums_x(s, acc):
        load_x(s).wait()
        for r in range(pieces):
            xx = xpad[s, PAD + r * CHUNK : PAD + (r + 1) * CHUNK, :].astype(F32)
            acc = acc + fold(xx * mask(s, r, wide))
        return acc

    acc = lax.fori_loop(0, seqs, sums_x, jnp.zeros((8, chans), F32))
    count_wide = jnp.concatenate([own_count] * wide, axis=1)
    count_narrow = jnp.concatenate([own_count] * narrow, axis=1)
    sum_one = jnp.sum(acc, axis=0, keepdims=True)
    local_one = sum_one / jnp.maximum(count_wide, 1.0)

    def squares_x(s, acc):
        for r in range(pieces):
            xx = xpad[s, PAD + r * CHUNK : PAD + (r + 1) * CHUNK, :].astype(F32) - local_one
            acc = acc + fold(xx * xx * mask(s, r, wide))
        return acc

    acc = lax.fori_loop(0, seqs, squares_x, jnp.zeros((8, chans), F32))
    fs1[0:1, :] = sum_one
    fs1[1:2, :] = jnp.sum(acc, axis=0, keepdims=True)
    fs1[2:3, :] = count_wide
    fs1[3:4, :] = count_wide

    def triple(ref):
        return ref[0:1, :], ref[1:2, :], ref[2:3, :]

    mine = mate_copies(0, fs1, fr1)
    start(mine)
    wait(mine)
    s_, q_, n_ = merge([triple(fs1)] + [triple(fr1.at[j]) for j in range(len(mates))])
    cs1[0:1, :] = s_
    cs1[1:2, :] = q_
    cs1[2:3, :] = n_
    cs1[3:4, :] = n_
    far = chip_copies(0, cs1, cr1)
    start(far)

    def mask_grad(s, acc):
        load_g(s).wait()
        for r in range(pieces):
            rows = slice(r * CHUNK, (r + 1) * CHUNK)
            g = grad[s, rows, :].astype(F32) * mask(s, r, wide)
            acc = acc + fold(g)
            grad[s, rows, :] = g.astype(BF)
        return acc

    acc = lax.fori_loop(0, seqs, mask_grad, jnp.zeros((8, chans), F32))
    own_bias = jnp.sum(acc, axis=0, keepdims=True)

    wait(far)
    s_, q_, count = merge([triple(cs1)] + [triple(cr1.at[j]) for j in range(len(chips))])
    mean_one = s_ / count
    scale_one = lax.rsqrt(q_ / count + EPS)
    gain_one = par[1:2, :] * scale_one
    shift_one = par[2:3, :]

    edge_wait(x_low, x_high)

    def first_act(s, _):
        for r in range(pieces + 2 * PAD // CHUNK):
            rows = slice(r * CHUNK, (r + 1) * CHUNK)
            v = (xpad[s, rows, :].astype(F32) - mean_one) * gain_one + shift_one
            v = 0.5 * v + (0.5 * v) * jnp.tanh(0.851 * v)
            if r * CHUNK < PAD:
                v = jnp.where(bi > 0, v, 0.0)
            if r * CHUNK >= PAD + bins:
                v = jnp.where(bi < nb - 1, v, 0.0)
            h1[s, rows, :] = v.astype(BF)
        return 0

    lax.fori_loop(0, seqs, first_act, 0)

    def conv(s, acc):
        z = None
        for k in range(3):
            first = PAD + (k - 1) * STEP
            part = dot(h1[s, first : first + bins, :], wd[k * chans : (k + 1) * chans, :], 1, 0)
            z = part if z is None else z + part
        z1[s] = z
        for r in range(pieces):
            acc = acc + fold(z1[s, r * CHUNK : (r + 1) * CHUNK, :] * mask(s, r, narrow))
        return acc

    acc = lax.fori_loop(0, seqs, conv, jnp.zeros((8, hid), F32))
    sum_two = jnp.sum(acc, axis=0, keepdims=True)
    local_two = sum_two / jnp.maximum(count_narrow, 1.0)

    def squares_z(s, acc):
        for r in range(pieces):
            z = z1[s, r * CHUNK : (r + 1) * CHUNK, :] - local_two
            acc = acc + fold(z * z * mask(s, r, narrow))
        return acc

    acc = lax.fori_loop(0, seqs, squares_z, jnp.zeros((8, hid), F32))
    fs2[0:1, :] = sum_two
    fs2[1:2, :] = jnp.sum(acc, axis=0, keepdims=True)
    fs2[2:3, :] = own_bias[:, :hid]
    fs2[3:4, :] = own_bias[:, hid:]

    def pair(ref, n):
        return ref[0:1, :], ref[1:2, :], n[2:3, :hid]

    mine = mate_copies(1, fs2, fr2)
    start(mine)
    wait(mine)
    entries = [pair(fs2, fs1)] + [pair(fr2.at[j], fr1.at[j]) for j in range(len(mates))]
    s_, q_, _ = merge(entries)
    bias_part = fs2[2:4, :]
    for j in range(len(mates)):
        bias_part = bias_part + fr2[j, 2:4, :]
    cs2[0:1, :] = s_
    cs2[1:2, :] = q_
    cs2[2:4, :] = bias_part
    far = chip_copies(1, cs2, cr2)
    start(far)

    def grad_point(s, _):
        gw[s] = dot(grad[s], wp[...], 1, 1)
        return 0

    lax.fori_loop(0, seqs, grad_point, 0)

    wait(far)
    entries = [pair(cs2, cs1)] + [pair(cr2.at[j], cr1.at[j]) for j in range(len(chips))]
    s_, q_, _ = merge(entries)
    for j in range(len(chips)):
        bias_part = bias_part + cr2[j, 2:4, :]
    small[0:1, :hid] = bias_part[0:1, :]
    small[0:1, hid:] = bias_part[1:2, :]
    mean_two = s_ / count[:, :hid]
    scale_two = lax.rsqrt(q_ / count[:, :hid] + EPS)
    gain_two = par[3:4, :hid]
    shift_two = par[3:4, hid:]

    def second_act(s, acc):
        a, b = acc
        for r in range(pieces):
            rows = slice(r * CHUNK, (r + 1) * CHUNK)
            xh = (z1[s, rows, :] - mean_two) * scale_two
            v = xh * gain_two + shift_two
            t = jnp.tanh(0.851 * v)
            h2[s, rows, :] = (0.5 * v + (0.5 * v) * t).astype(BF)
            d = gw[s, rows, :] * (0.5 + 0.5 * t + (0.4255 * v) * (1.0 - t * t))
            z1[s, rows, :] = xh
            gw[s, rows, :] = d
            a = a + fold(d)
            b = b + fold(d * xh)
        return a, b

    zero = jnp.zeros((8, hid), F32)
    a, b = lax.fori_loop(0, seqs, second_act, (zero, zero))
    fs3[0:1, :] = jnp.sum(a, axis=0, keepdims=True)
    fs3[1:2, :] = jnp.sum(b, axis=0, keepdims=True)

    def store_out(s):
        return pltpu.make_async_copy(stage.at[s], out_hbm.at[s], osem.at[s])

    def point_work():
        def branch(s, _):
            stage[s] = (
                xpad[s, PAD : PAD + bins, :].astype(F32) + dot(h2[s], wp[...], 1, 0) + par[0:1, :]
            ).astype(BF)
            store_out(s).start()
            return 0

        lax.fori_loop(0, seqs, branch, 0)
        flat = grad[...].reshape(seqs * bins, chans)
        dwp[...] = dot(h2[...].reshape(seqs * bins, hid), flat, 0, 0)

    both = plain_sum(2, fs3, fr3, cs3, cr3, 2, point_work)
    shift_total, gain_total = both[0:1, :], both[1:2, :]
    small[3:4, :hid] = gain_total
    small[3:4, hid:] = shift_total
    outer = scale_two * gain_two
    level = shift_total / count[:, :hid]
    slant = gain_total / count[:, :hid]

    def conv_grad(s, _):
        for r in range(pieces):
            rows = slice(r * CHUNK, (r + 1) * CHUNK)
            d = gw[s, rows, :] - mask(s, r, narrow) * (level + z1[s, rows, :] * slant)
            dz[s, PAD + r * CHUNK : PAD + (r + 1) * CHUNK, :] = (outer * d).astype(BF)
        return 0

    lax.fori_loop(0, seqs, conv_grad, 0)
    z_low, z_high = edge_copies(
        lambda r: dz.at[:, pl.ds(PAD + r, PAD), :], lambda r: dz.at[:, pl.ds(r, PAD), :], zsem, zrem
    )
    edge_start(z_low, z_high)

    @pl.when(bi == 0)
    def _():
        dz[:, 0:PAD, :] = jnp.zeros((seqs, PAD, hid), BF)

    @pl.when(bi == nb - 1)
    def _():
        dz[:, PAD + bins : PAD + bins + PAD, :] = jnp.zeros((seqs, PAD, hid), BF)

    edge_wait(z_low, z_high)

    def shift_taps(s, _):
        for k in range(3):
            first = PAD - (k - 1) * STEP
            taps[s, :, k * hid : (k + 1) * hid] = dz[s, first : first + bins, :]
        return 0

    lax.fori_loop(0, seqs, shift_taps, 0)

    def kernel_grad(m, _):
        cols = pl.ds(pl.multiple_of(m * 256, 256), 256)
        left = h1[:, PAD : PAD + bins, cols].reshape(seqs * bins, 256)
        for k in range(3):
            right = taps[:, :, k * hid : (k + 1) * hid].reshape(seqs * bins, hid)
            dwd[pl.ds(pl.multiple_of(k * chans + m * 256, 256), 256), :] = dot(left, right, 0, 0)
        return 0

    lax.fori_loop(0, chans // 256, kernel_grad, 0)

    def input_side(s, acc):
        a, b = acc
        d = None
        for k in range(3):
            part = dot(taps[s, :, k * hid : (k + 1) * hid], wd[k * chans : (k + 1) * chans, :], 1, 1)
            d = part if d is None else d + part
        dg[s] = d
        for r in range(pieces):
            rows = slice(r * CHUNK, (r + 1) * CHUNK)
            xc = xpad[s, PAD + r * CHUNK : PAD + (r + 1) * CHUNK, :].astype(F32) - mean_one
            v = xc * gain_one + shift_one
            t = jnp.tanh(0.851 * v)
            d = dg[s, rows, :] * (0.5 + 0.5 * t + (0.4255 * v) * (1.0 - t * t))
            dg[s, rows, :] = d
            a = a + fold(d)
            b = b + fold(d * (xc * scale_one))
        return a, b

    zero = jnp.zeros((8, chans), F32)
    a, b = lax.fori_loop(0, seqs, input_side, (zero, zero))
    fs4[0:1, :] = jnp.sum(a, axis=0, keepdims=True)
    fs4[1:2, :] = jnp.sum(b, axis=0, keepdims=True)
    both = plain_sum(3, fs4, fr4, cs4, cr4, 2, lambda: None)
    shift_total, gain_total = both[0:1, :], both[1:2, :]
    small[1:2, :] = gain_total
    small[2:3, :] = shift_total
    level = shift_total / count
    slant = gain_total / count

    def store_in(s):
        return pltpu.make_async_copy(grad.at[s], gin_hbm.at[s], isem.at[s])

    def input_grad(s, _):
        for r in range(pieces):
            rows = slice(r * CHUNK, (r + 1) * CHUNK)
            xc = xpad[s, PAD + r * CHUNK : PAD + (r + 1) * CHUNK, :].astype(F32) - mean_one
            d = dg[s, rows, :] - mask(s, r, wide) * (level + (xc * scale_one) * slant)
            grad[s, rows, :] = (grad[s, rows, :].astype(F32) + gain_one * d).astype(BF)
        store_in(s).start()
        return 0

    lax.fori_loop(0, seqs, input_grad, 0)

    def drain(s, _):
        store_out(s).wait()
        store_in(s).wait()
        return 0

    lax.fori_loop(0, seqs, drain, 0)


def local(sizes, x, black, unmap, limit, wd, wp, bias, g1, s1, g2, s2, og):
    nb, nz, nf = sizes
    seqs, bins, chans = x.shape
    hid = wd.shape[1]
    groups = ("batch", "fsdp")
    wd_all = lax.all_gather(wd.astype(BF), groups, axis=0, tiled=True)
    wp_all = lax.all_gather(wp.astype(BF), groups, axis=0, tiled=True)
    packed = jnp.concatenate([bias, g1, s1, g2, s2]).astype(BF)
    spread = lax.all_gather(packed, groups, axis=0).astype(F32)
    wide, narrow = bias.shape[0], g2.shape[0]
    rows = [spread[:, k * wide : (k + 1) * wide].reshape(1, chans) for k in range(3)]
    rest = [
        spread[:, 3 * wide + k * narrow : 3 * wide + (k + 1) * narrow].reshape(1, hid)
        for k in range(2)
    ]
    par = jnp.concatenate(rows + [jnp.concatenate(rest, axis=1)] * 5, axis=0)
    near, far = nf - 1, nb * nz - 1
    vmem = pl.BlockSpec(memory_space=pltpu.VMEM)
    hbm = pl.BlockSpec(memory_space=pl.ANY)
    dma = pltpu.SemaphoreType.DMA

    def sums(rows, width):
        return [
            pltpu.VMEM((rows, width), F32),
            pltpu.VMEM((near, rows, width), F32),
            pltpu.VMEM((rows, width), F32),
            pltpu.VMEM((far, rows, width), F32),
        ]

    tall = bins + 2 * PAD
    out, gin, dwd, dwp, small = pl.pallas_call(
        functools.partial(block, sizes),
        out_shape=(
            jax.ShapeDtypeStruct(x.shape, BF),
            jax.ShapeDtypeStruct(x.shape, BF),
            jax.ShapeDtypeStruct((3 * chans, hid), F32),
            jax.ShapeDtypeStruct((hid, chans), F32),
            jax.ShapeDtypeStruct((8, chans), F32),
        ),
        in_specs=[hbm, hbm] + [vmem] * 6,
        out_specs=(hbm, hbm, vmem, vmem, vmem),
        scratch_shapes=[
            pltpu.VMEM((seqs, tall, chans), BF),
            pltpu.VMEM((seqs, bins, chans), BF),
            pltpu.VMEM((seqs, bins, 128), F32),
            pltpu.VMEM((seqs, tall, chans), BF),
            pltpu.VMEM((seqs, bins, hid), F32),
            pltpu.VMEM((seqs, bins, hid), F32),
            pltpu.VMEM((seqs, bins, hid), BF),
            pltpu.VMEM((seqs, tall, hid), BF),
            pltpu.VMEM((seqs, bins, 3 * hid), BF),
            pltpu.VMEM((seqs, bins, chans), F32),
            pltpu.VMEM((seqs, bins, chans), BF),
        ]
        + sums(4, chans) + sums(4, hid) + sums(2, hid) + sums(2, chans)
        + [
            dma((seqs,)), dma((seqs,)), dma((seqs,)), dma((seqs,)),
            dma((2,)), dma((2,)), dma((2,)), dma((2,)),
            dma((4, near)), dma((4, near)), dma((4, far)), dma((4, far)),
        ],
        compiler_params=pltpu.CompilerParams(
            collective_id=0, has_side_effects=True, vmem_limit_bytes=60 * 2**20
        ),
    )(x, og, black, unmap, limit.reshape(seqs, 1), wd_all, wp_all, par)
    summed = lax.psum((dwd, dwp), "bins")
    owner = lax.axis_index(groups)

    def own(row, width):
        return lax.dynamic_slice_in_dim(row, owner * width, width)

    return (
        out,
        gin,
        lax.psum_scatter(summed[0], groups, scatter_dimension=0, tiled=True),
        lax.psum_scatter(summed[1], groups, scatter_dimension=0, tiled=True),
        own(small[0], wide),
        own(small[1], wide),
        own(small[2], wide),
        own(small[3, :hid], narrow),
        own(small[3, hid:], narrow),
    )


def solution(mesh):
    sizes = (mesh.shape["bins"], mesh.shape["batch"], mesh.shape["fsdp"])
    rows = P(("batch", "fsdp"))
    track = P(("batch", "fsdp"), "bins", None)
    table = P(("batch", "fsdp"), None)
    return jax.shard_map(
        functools.partial(local, sizes),
        mesh=mesh,
        in_specs=(track, P(("batch", "fsdp"), "bins"), P(("batch", "fsdp"), "bins"), rows,
                  table, table, rows, rows, rows, rows, rows, track),
        out_specs=(track, track, table, table, rows, rows, rows, rows, rows),
        check_vma=False,
    )
```

```python
import functools

import jax
import jax.numpy as jnp
from jax import lax
from jax.experimental import pallas as pl
from jax.experimental.pallas import tpu as pltpu
from jax.sharding import PartitionSpec as P

STEP = 26
EPS = 1e-5
PAD = 32
CHUNK = 32
MESH = pl.DeviceIdType.MESH
BF = jnp.bfloat16
F32 = jnp.float32


def dot(a, b, ca, cb):
    return lax.dot_general(a, b, (((ca,), (cb,)), ((), ())), preferred_element_type=F32)


def fold(v):
    rows, width = v.shape
    return jnp.sum(v.reshape(rows // 8, 8, width), axis=0)


def merge(entries):
    total = functools.reduce(jnp.add, [e[0] for e in entries])
    count = functools.reduce(jnp.add, [e[2] for e in entries])
    mean = total / jnp.maximum(count, 1.0)
    square = functools.reduce(jnp.add, [e[1] for e in entries])
    for s, _, n in entries:
        gap = s / jnp.maximum(n, 1.0) - mean
        square = square + n * gap * gap
    return total, square, count


def block(
    sizes,
    x_hbm, og_hbm, black_hbm, unmap_hbm, limit, wd_hbm, wp_hbm, bias_in, g1_in, s1_in, g2_in, s2_in,
    out_hbm, gin_hbm, dwd, dwp, bias_out, g1_out, s1_out, g2_out, s2_out,
    xin, grad, vm, h1, z1, gw, h2, dz, taps, dg, stage,
    fs1, fr1, cs1, cr1, fs2, fr2, cs2, cr2, fs3, fr3, cs3, cr3, fs4, fr4, cs4, cr4,
    black, unmap, wd_own, wp_own, wd, wp, wall, pall, par, es, er,
    xsem, gsem, osem, isem, lsem, hsem, hrem, zsem, zrem, fss, frs, css, crs,
    wzs, wzr, wcs, wcr, wfs, wfr, pzs, pzr, pfs, pfr,
):
    nb, nz, nf = sizes
    inside = wall is not None
    seqs, bins, chans = grad.shape
    hid = z1.shape[2]
    wide, narrow = chans // 128, hid // 128
    pieces = bins // CHUNK
    bi, zi, fi = lax.axis_index("bins"), lax.axis_index("batch"), lax.axis_index("fsdp")

    def load_x(s):
        return pltpu.make_async_copy(x_hbm.at[s], xin.at[s], xsem.at[s])

    def load_g(s):
        return pltpu.make_async_copy(og_hbm.at[s], grad.at[s], gsem.at[s])

    small_loads = [
        pltpu.make_async_copy(src, dst, lsem.at[i])
        for i, (src, dst) in enumerate(
            [(black_hbm, black), (unmap_hbm, unmap), (wd_hbm, wd_own), (wp_hbm, wp_own)]
        )
    ]

    mates = [(k,) for k in range(1, nf)]
    chips = [(b, z) for z in range(nz) for b in range(nb) if (b, z) != (0, 0)]

    def mate(k):
        return {"fsdp": lax.rem(fi + k, nf)}

    def chip(b, z):
        return {"bins": lax.rem(bi + b, nb), "batch": lax.rem(zi + z, nz)}

    barrier = pltpu.get_barrier_semaphore()
    for (k,) in mates:
        pl.semaphore_signal(barrier, inc=1, device_id=mate(k), device_id_type=MESH)
    for b, z in chips:
        pl.semaphore_signal(barrier, inc=1, device_id=chip(b, z), device_id_type=MESH)

    small_loads[0].start()
    small_loads[1].start()
    for s in range(seqs):
        load_x(s).start()
    small_loads[2].start()
    small_loads[3].start()
    for s in range(seqs):
        load_g(s).start()

    small_loads[0].wait()
    small_loads[1].wait()
    ends = jnp.zeros((seqs, bins), jnp.int32)
    for s in range(seqs):
        row = lax.broadcasted_iota(jnp.int32, (seqs, bins), 0)
        ends = jnp.where(row == s, limit[s], ends)
    place = bi * bins + lax.broadcasted_iota(jnp.int32, (seqs, bins), 1)
    keep = (black[...] == 0) & (unmap[...] == 0) & (place < ends)
    columns = jnp.transpose(keep.astype(F32))
    tally = jnp.zeros((8, 128), F32)
    for s in range(seqs):
        lanes = jnp.broadcast_to(columns[:, s : s + 1], (bins, 128))
        vm[s] = lanes
        tally = tally + fold(lanes)
    own_count = jnp.sum(tally, axis=0, keepdims=True)

    def mask(s, r, copies):
        m = vm[s, r * CHUNK : (r + 1) * CHUNK, :]
        return jnp.concatenate([m] * copies, axis=1)

    low, high = lax.rem(bi + nb - 1, nb), lax.rem(bi + 1, nb)

    def edge_copies(low_src, low_dst, high_src, high_dst, send, recv):
        to_low = pltpu.make_async_remote_copy(
            src_ref=low_src, dst_ref=low_dst, send_sem=send.at[0], recv_sem=recv.at[0],
            device_id={"bins": low}, device_id_type=MESH,
        )
        to_high = pltpu.make_async_remote_copy(
            src_ref=high_src, dst_ref=high_dst, send_sem=send.at[1], recv_sem=recv.at[1],
            device_id={"bins": high}, device_id_type=MESH,
        )
        return to_low, to_high

    def edge_start(to_low, to_high):
        @pl.when(bi > 0)
        def _():
            to_low.start()

        @pl.when(bi < nb - 1)
        def _():
            to_high.start()

    def edge_wait(to_low, to_high):
        @pl.when(bi < nb - 1)
        def _():
            to_low.wait_recv()
            to_high.wait_send()

        @pl.when(bi > 0)
        def _():
            to_high.wait_recv()
            to_low.wait_send()

    def mate_copies(i, src, dst):
        return [
            pltpu.make_async_remote_copy(
                src_ref=src, dst_ref=dst.at[j], send_sem=fss.at[i, j], recv_sem=frs.at[i, j],
                device_id=mate(k), device_id_type=MESH,
            )
            for j, (k,) in enumerate(mates)
        ]

    def chip_copies(i, src, dst):
        return [
            pltpu.make_async_remote_copy(
                src_ref=src, dst_ref=dst.at[j], send_sem=css.at[i, j], recv_sem=crs.at[i, j],
                device_id=chip(b, z), device_id_type=MESH,
            )
            for j, (b, z) in enumerate(chips)
        ]

    def start(copies):
        for c in copies:
            c.start()

    def wait(copies):
        for c in copies:
            c.wait_recv()
        for c in copies:
            c.wait_send()

    def plain_sum(i, fs, fr, cs, cr, rows, filler):
        mine = mate_copies(i, fs, fr)
        start(mine)
        wait(mine)
        both = fs[...]
        for j in range(len(mates)):
            both = both + fr[j]
        cs[...] = both
        far = chip_copies(i, cs, cr)
        start(far)
        filler()
        wait(far)
        total = cs[...]
        for j in range(len(chips)):
            total = total + cr[j]
        return total

    own = zi * nf + fi
    pall[own] = jnp.zeros((8, 128), F32)
    for r, ref in enumerate((bias_in, g1_in, s1_in, g2_in, s2_in)):
        n = ref.shape[0]
        pall[own, r : r + 1, 0:n] = ref[...].astype(BF).astype(F32).reshape(1, n)
    small_loads[2].wait()
    small_loads[3].wait()
    share = wp_own.shape[0]
    if inside:
        base = wd_own.shape[0]
        piece = (base + 2 * share) // nb
        wall[own, 0:base, :] = wd_own[...].astype(BF)
        wall[own, base : base + share, :] = wp_own[:, 0:hid].astype(BF)
        wall[own, base + share : base + 2 * share, :] = wp_own[:, hid:].astype(BF)

    def before(i, k, n):
        return lax.rem(i + n - k, n)

    def send(ref, ssem, rsem, where):
        return pltpu.make_async_remote_copy(
            src_ref=ref, dst_ref=ref, send_sem=ssem, recv_sem=rsem,
            device_id=where, device_id_type=MESH,
        )

    def along(k):
        return {"batch": lax.rem(zi + k, nz)}

    def slot(z, f):
        return z * nf + f

    par_far = [send(pall.at[own], pzs.at[k], pzr.at[k], along(k)) for k in range(1, nz)]
    par_near = [
        [
            send(pall.at[slot(before(zi, k, nz), fi)], pfs.at[j, k], pfr.at[j, k], mate(m))
            for j, (m,) in enumerate(mates)
        ]
        for k in range(nz)
    ]

    def part(k, b):
        rows = pl.ds(pl.multiple_of(before(bi, b, nb) * piece, 16), piece)
        return wall.at[slot(before(zi, k, nz), fi), rows, :]

    if inside:
        w_far = [send(part(0, 0), wzs.at[k], wzr.at[k], along(k)) for k in range(1, nz)]
        w_side = [
            [
                send(part(k, 0), wcs.at[k, b], wcr.at[k, b], {"bins": lax.rem(bi + b, nb)})
                for b in range(1, nb)
            ]
            for k in range(1, nz)
        ]
        w_own = [
            send(wall.at[own], wfs.at[j, 0, 0], wfr.at[j, 0, 0], mate(m))
            for j, (m,) in enumerate(mates)
        ]
        w_near = [
            [
                [send(part(k, b), wfs.at[j, k, b], wfr.at[j, k, b], mate(m)) for j, (m,) in enumerate(mates)]
                for b in range(nb)
            ]
            for k in range(1, nz)
        ]

    def sums_x(s, acc):
        load_x(s).wait()
        for r in range(pieces):
            xx = xin[s, r * CHUNK : (r + 1) * CHUNK, :].astype(F32)
            acc = acc + fold(xx * mask(s, r, wide))
        return acc

    acc = lax.fori_loop(0, seqs, sums_x, jnp.zeros((8, chans), F32))
    count_wide = jnp.concatenate([own_count] * wide, axis=1)
    count_narrow = jnp.concatenate([own_count] * narrow, axis=1)
    sum_one = jnp.sum(acc, axis=0, keepdims=True)
    local_one = sum_one / jnp.maximum(count_wide, 1.0)

    def squares_x(s, acc):
        for r in range(pieces):
            xx = xin[s, r * CHUNK : (r + 1) * CHUNK, :].astype(F32) - local_one
            acc = acc + fold(xx * xx * mask(s, r, wide))
        return acc

    acc = lax.fori_loop(0, seqs, squares_x, jnp.zeros((8, chans), F32))
    fs1[0:1, :] = sum_one
    fs1[1:2, :] = jnp.sum(acc, axis=0, keepdims=True)
    fs1[2:3, :] = count_wide
    fs1[3:4, :] = count_wide

    def triple(ref):
        return ref[0:1, :], ref[1:2, :], ref[2:3, :]

    pl.semaphore_wait(barrier, len(mates) + len(chips))
    mine = mate_copies(0, fs1, fr1)
    start(mine)
    start(par_far)
    start(par_near[0])
    if inside:
        start(w_far)
        start(w_own)
    wait(mine)
    s_, q_, n_ = merge([triple(fs1)] + [triple(fr1.at[j]) for j in range(len(mates))])
    cs1[0:1, :] = s_
    cs1[1:2, :] = q_
    cs1[2:3, :] = n_
    cs1[3:4, :] = n_
    far = chip_copies(0, cs1, cr1)
    start(far)

    def mask_grad(s, acc):
        load_g(s).wait()
        for r in range(pieces):
            rows = slice(r * CHUNK, (r + 1) * CHUNK)
            g = grad[s, rows, :].astype(F32) * mask(s, r, wide)
            acc = acc + fold(g)
            grad[s, rows, :] = g.astype(BF)
        return acc

    acc = lax.fori_loop(0, seqs, mask_grad, jnp.zeros((8, chans), F32))
    own_bias = jnp.sum(acc, axis=0, keepdims=True)

    for k in range(1, nz):
        par_far[k - 1].wait_recv()
        start(par_near[k])
        if inside:
            w_far[k - 1].wait_recv()
            start(w_side[k - 1])
            start(w_near[k - 1][0])
    for k in range(nz):
        for c in par_near[k]:
            c.wait_recv()

    rows = jnp.zeros((8, chans + 256), F32)
    cols = jnp.zeros((8, hid + 256), F32)

    def laid(into, tile, width, index):
        at = index * width
        first, turn = at // 128 * 128, at % 128
        tile = jnp.concatenate([tile, jnp.zeros((8, 128), F32)], axis=1)
        tile = pltpu.roll(tile, turn, 1) if turn else tile
        return jnp.concatenate(
            [t for t in (into[:, :first], into[:, first : first + 256] + tile, into[:, first + 256 :]) if t.shape[1]],
            axis=1,
        )

    for c in range(nz * nf):
        rows = laid(rows, pall[c], bias_in.shape[0], c)
        cols = laid(cols, pall[c], g2_in.shape[0], c)
    par[0:3, :] = rows[0:3, :chans]
    par[3:5, 0:hid] = cols[3:5, :hid]

    wait(far)
    s_, q_, count = merge([triple(cs1)] + [triple(cr1.at[j]) for j in range(len(chips))])
    mean_one = s_ / count
    scale_one = lax.rsqrt(q_ / count + EPS)
    gain_one = par[1:2, :] * scale_one
    shift_one = par[2:3, :]

    h1[:, 0:PAD, :] = jnp.zeros((seqs, PAD, chans), BF)
    h1[:, PAD + bins : PAD + bins + PAD, :] = jnp.zeros((seqs, PAD, chans), BF)

    def first_act(s, _):
        for r in range(pieces):
            rows = slice(PAD + r * CHUNK, PAD + (r + 1) * CHUNK)
            v = (xin[s, r * CHUNK : (r + 1) * CHUNK, :].astype(F32) - mean_one) * gain_one + shift_one
            h1[s, rows, :] = (0.5 * v + (0.5 * v) * jnp.tanh(0.851 * v)).astype(BF)
        return 0

    lax.fori_loop(0, seqs, first_act, 0)

    if inside:
        for k in range(1, nz):
            for b in range(1, nb):
                w_side[k - 1][b - 1].wait_recv()
                start(w_near[k - 1][b])
        for c in w_own:
            c.wait_recv()
        for k in range(1, nz):
            for b in range(nb):
                for c in w_near[k - 1][b]:
                    c.wait_recv()
        for c in range(nz * nf):
            wd[c * base : (c + 1) * base, :] = wall[c, 0:base, :]
            wp[c * share : (c + 1) * share, 0:hid] = wall[c, base : base + share, :]
            wp[c * share : (c + 1) * share, hid:] = wall[c, base + share : base + 2 * share, :]

    def tap(k):
        return wd[k * chans : (k + 1) * chans, :]

    over = h1[:, PAD + bins - STEP : PAD + bins - STEP + PAD, :].reshape(seqs * PAD, chans)
    es[1] = dot(over, tap(0), 1, 0).astype(BF).reshape(seqs, PAD, hid)
    under = h1[:, STEP : STEP + PAD, :].reshape(seqs * PAD, chans)
    es[0] = dot(under, tap(2), 1, 0).astype(BF).reshape(seqs, PAD, hid)
    e_low, e_high = edge_copies(es.at[0], er.at[0], es.at[1], er.at[1], hsem, hrem)
    edge_start(e_low, e_high)

    def conv(s, _):
        z = None
        for k in range(3):
            first = PAD + (k - 1) * STEP
            part = dot(h1[s, first : first + bins, :], tap(k), 1, 0)
            z = part if z is None else z + part
        z1[s] = z
        return 0

    lax.fori_loop(0, seqs, conv, 0)
    edge_wait(e_low, e_high)

    @pl.when(bi > 0)
    def _():
        z1[:, 0:PAD, :] = z1[:, 0:PAD, :] + er[1].astype(F32)

    @pl.when(bi < nb - 1)
    def _():
        z1[:, bins - PAD :, :] = z1[:, bins - PAD :, :] + er[0].astype(F32)

    def sums_z(s, acc):
        for r in range(pieces):
            acc = acc + fold(z1[s, r * CHUNK : (r + 1) * CHUNK, :] * mask(s, r, narrow))
        return acc

    acc = lax.fori_loop(0, seqs, sums_z, jnp.zeros((8, hid), F32))
    sum_two = jnp.sum(acc, axis=0, keepdims=True)
    local_two = sum_two / jnp.maximum(count_narrow, 1.0)

    def squares_z(s, acc):
        for r in range(pieces):
            z = z1[s, r * CHUNK : (r + 1) * CHUNK, :] - local_two
            acc = acc + fold(z * z * mask(s, r, narrow))
        return acc

    acc = lax.fori_loop(0, seqs, squares_z, jnp.zeros((8, hid), F32))
    fs2[0:1, :] = sum_two
    fs2[1:2, :] = jnp.sum(acc, axis=0, keepdims=True)
    fs2[2:3, :] = own_bias[:, :hid]
    fs2[3:4, :] = own_bias[:, hid:]

    def pair(ref, n):
        return ref[0:1, :], ref[1:2, :], n[2:3, :hid]

    mine = mate_copies(1, fs2, fr2)
    start(mine)
    wait(mine)
    entries = [pair(fs2, fs1)] + [pair(fr2.at[j], fr1.at[j]) for j in range(len(mates))]
    s_, q_, _ = merge(entries)
    bias_part = fs2[2:4, :]
    for j in range(len(mates)):
        bias_part = bias_part + fr2[j, 2:4, :]
    cs2[0:1, :] = s_
    cs2[1:2, :] = q_
    cs2[2:4, :] = bias_part
    far = chip_copies(1, cs2, cr2)
    start(far)

    def grad_point(s, _):
        gw[s] = dot(grad[s], wp[...], 1, 1)
        return 0

    lax.fori_loop(0, seqs, grad_point, 0)

    wait(far)
    entries = [pair(cs2, cs1)] + [pair(cr2.at[j], cr1.at[j]) for j in range(len(chips))]
    s_, q_, _ = merge(entries)
    for j in range(len(chips)):
        bias_part = bias_part + cr2[j, 2:4, :]
    bias_total = jnp.concatenate([bias_part[0:1, :], bias_part[1:2, :]], axis=1)

    def owned(out, row):
        n = out.shape[0]
        row = jnp.concatenate([row, jnp.zeros((1, 256), F32)], axis=1)
        row = jnp.broadcast_to(row, (8, row.shape[1]))
        mine = jnp.zeros((8, 128), F32)
        for c in range(nz * nf):
            first, turn = c * n // 128 * 128, c * n % 128
            tile = row[:, first : first + 256]
            tile = (pltpu.roll(tile, 256 - turn, 1) if turn else tile)[:, :128]
            mine = jnp.where(own == c, tile, mine)
        out[...] = mine[0:1, 0:n].reshape(n)

    owned(bias_out, bias_total)
    mean_two = s_ / count[:, :hid]
    scale_two = lax.rsqrt(q_ / count[:, :hid] + EPS)
    gain_two = par[3:4, :hid]
    shift_two = par[4:5, :hid]

    def second_act(s, acc):
        a, b = acc
        for r in range(pieces):
            rows = slice(r * CHUNK, (r + 1) * CHUNK)
            xh = (z1[s, rows, :] - mean_two) * scale_two
            v = xh * gain_two + shift_two
            t = jnp.tanh(0.851 * v)
            h2[s, rows, :] = (0.5 * v + (0.5 * v) * t).astype(BF)
            d = gw[s, rows, :] * (0.5 + 0.5 * t + (0.4255 * v) * (1.0 - t * t))
            z1[s, rows, :] = xh
            gw[s, rows, :] = d
            a = a + fold(d)
            b = b + fold(d * xh)
        return a, b

    zero = jnp.zeros((8, hid), F32)
    a, b = lax.fori_loop(0, seqs, second_act, (zero, zero))
    fs3[0:1, :] = jnp.sum(a, axis=0, keepdims=True)
    fs3[1:2, :] = jnp.sum(b, axis=0, keepdims=True)

    def store_out(s):
        return pltpu.make_async_copy(stage.at[s], out_hbm.at[s], osem.at[s])

    def point_work():
        def branch(s, _):
            stage[s] = (
                xin[s].astype(F32) + dot(h2[s], wp[...], 1, 0) + par[0:1, :]
            ).astype(BF)
            store_out(s).start()
            return 0

        lax.fori_loop(0, seqs, branch, 0)
        flat = grad[...].reshape(seqs * bins, chans)
        dwp[...] = dot(h2[...].reshape(seqs * bins, hid), flat, 0, 0)

    both = plain_sum(2, fs3, fr3, cs3, cr3, 2, point_work)
    shift_total, gain_total = both[0:1, :], both[1:2, :]
    owned(g2_out, gain_total)
    owned(s2_out, shift_total)
    outer = scale_two * gain_two
    level = shift_total / count[:, :hid]
    slant = gain_total / count[:, :hid]

    def conv_grad(s, _):
        for r in range(pieces):
            rows = slice(r * CHUNK, (r + 1) * CHUNK)
            d = gw[s, rows, :] - mask(s, r, narrow) * (level + z1[s, rows, :] * slant)
            dz[s, PAD + r * CHUNK : PAD + (r + 1) * CHUNK, :] = (outer * d).astype(BF)
        return 0

    lax.fori_loop(0, seqs, conv_grad, 0)
    z_low, z_high = edge_copies(
        dz.at[:, pl.ds(PAD, PAD), :], dz.at[:, pl.ds(PAD + bins, PAD), :],
        dz.at[:, pl.ds(bins, PAD), :], dz.at[:, pl.ds(0, PAD), :], zsem, zrem,
    )
    edge_start(z_low, z_high)

    @pl.when(bi == 0)
    def _():
        dz[:, 0:PAD, :] = jnp.zeros((seqs, PAD, hid), BF)

    @pl.when(bi == nb - 1)
    def _():
        dz[:, PAD + bins : PAD + bins + PAD, :] = jnp.zeros((seqs, PAD, hid), BF)

    edge_wait(z_low, z_high)

    def shift_taps(s, _):
        for k in range(3):
            first = PAD - (k - 1) * STEP
            taps[s, :, k * hid : (k + 1) * hid] = dz[s, first : first + bins, :]
        return 0

    lax.fori_loop(0, seqs, shift_taps, 0)

    def kernel_grad(m, _):
        cols = pl.ds(pl.multiple_of(m * 256, 256), 256)
        left = h1[:, PAD : PAD + bins, cols].reshape(seqs * bins, 256)
        for k in range(3):
            right = taps[:, :, k * hid : (k + 1) * hid].reshape(seqs * bins, hid)
            dwd[pl.ds(pl.multiple_of(k * chans + m * 256, 256), 256), :] = dot(left, right, 0, 0)
        return 0

    lax.fori_loop(0, chans // 256, kernel_grad, 0)

    def input_side(s, acc):
        a, b = acc
        d = None
        for k in range(3):
            part = dot(taps[s, :, k * hid : (k + 1) * hid], wd[k * chans : (k + 1) * chans, :], 1, 1)
            d = part if d is None else d + part
        dg[s] = d
        for r in range(pieces):
            rows = slice(r * CHUNK, (r + 1) * CHUNK)
            xc = xin[s, r * CHUNK : (r + 1) * CHUNK, :].astype(F32) - mean_one
            v = xc * gain_one + shift_one
            t = jnp.tanh(0.851 * v)
            d = dg[s, rows, :] * (0.5 + 0.5 * t + (0.4255 * v) * (1.0 - t * t))
            dg[s, rows, :] = d
            a = a + fold(d)
            b = b + fold(d * (xc * scale_one))
        return a, b

    zero = jnp.zeros((8, chans), F32)
    a, b = lax.fori_loop(0, seqs, input_side, (zero, zero))
    fs4[0:1, :] = jnp.sum(a, axis=0, keepdims=True)
    fs4[1:2, :] = jnp.sum(b, axis=0, keepdims=True)
    both = plain_sum(3, fs4, fr4, cs4, cr4, 2, lambda: None)
    shift_total, gain_total = both[0:1, :], both[1:2, :]
    owned(g1_out, gain_total)
    owned(s1_out, shift_total)
    level = shift_total / count
    slant = gain_total / count

    def store_in(s):
        return pltpu.make_async_copy(grad.at[s], gin_hbm.at[s], isem.at[s])

    def input_grad(s, _):
        for r in range(pieces):
            rows = slice(r * CHUNK, (r + 1) * CHUNK)
            xc = xin[s, r * CHUNK : (r + 1) * CHUNK, :].astype(F32) - mean_one
            d = dg[s, rows, :] - mask(s, r, wide) * (level + (xc * scale_one) * slant)
            grad[s, rows, :] = (grad[s, rows, :].astype(F32) + gain_one * d).astype(BF)
        store_in(s).start()
        return 0

    lax.fori_loop(0, seqs, input_grad, 0)

    def drain(s, _):
        store_out(s).wait()
        store_in(s).wait()
        return 0

    lax.fori_loop(0, seqs, drain, 0)
    for c in par_far:
        c.wait_send()
    for k in range(nz):
        for c in par_near[k]:
            c.wait_send()
    if inside:
        for c in w_far + w_own:
            c.wait_send()
        for k in range(1, nz):
            for c in w_side[k - 1]:
                c.wait_send()
            for b in range(nb):
                for c in w_near[k - 1][b]:
                    c.wait_send()


def call(sizes, inside, *refs):
    refs = list(refs)
    if not inside:
        first = 21 + 11 + 16 + 2
        refs[first + 2 : first + 2] = [refs[first], refs[first + 1], None]
    block(sizes, *refs)


def local(sizes, x, black, unmap, limit, wd, wp, bias, g1, s1, g2, s2, og):
    nb, nz, nf = sizes
    seqs, bins, chans = x.shape
    hid = wd.shape[1]
    groups = ("batch", "fsdp")
    inside = (
        wd.shape[0] % 16 == 0
        and wp.shape[0] % 16 == 0
        and (wd.shape[0] + 2 * wp.shape[0]) % (16 * nb) == 0
        and chans == 2 * hid
    )
    if not inside:
        wd = lax.all_gather(wd.astype(BF), groups, axis=0, tiled=True)
        wp = lax.all_gather(wp.astype(BF), groups, axis=0, tiled=True)
    near, far = nf - 1, nb * nz - 1
    vmem = pl.BlockSpec(memory_space=pltpu.VMEM)
    hbm = pl.BlockSpec(memory_space=pl.ANY)
    dma = pltpu.SemaphoreType.DMA

    def sums(rows, width):
        return [
            pltpu.VMEM((rows, width), F32),
            pltpu.VMEM((near, rows, width), F32),
            pltpu.VMEM((rows, width), F32),
            pltpu.VMEM((far, rows, width), F32),
        ]

    tall = bins + 2 * PAD
    scratch = [
        pltpu.VMEM(black.shape, jnp.int32),
        pltpu.VMEM(black.shape, jnp.int32),
        pltpu.VMEM(wd.shape, wd.dtype),
        pltpu.VMEM(wp.shape, wp.dtype),
        pltpu.VMEM((3 * chans, hid), BF) if inside else None,
        pltpu.VMEM((hid, chans), BF) if inside else None,
        pltpu.VMEM((nz * nf, wd.shape[0] + 2 * wp.shape[0], hid), BF) if inside else None,
        pltpu.VMEM((nz * nf, 8, 128), F32),
        pltpu.VMEM((8, chans), F32),
        pltpu.VMEM((2, seqs, PAD, hid), BF),
        pltpu.VMEM((2, seqs, PAD, hid), BF),
    ]
    out, gin, dwd, dwp, bias_grad, g1_grad, s1_grad, g2_grad, s2_grad = pl.pallas_call(
        functools.partial(call, sizes, inside),
        out_shape=(
            jax.ShapeDtypeStruct(x.shape, BF),
            jax.ShapeDtypeStruct(x.shape, BF),
            jax.ShapeDtypeStruct((3 * chans, hid), F32),
            jax.ShapeDtypeStruct((hid, chans), F32),
            jax.ShapeDtypeStruct(bias.shape, F32),
            jax.ShapeDtypeStruct(bias.shape, F32),
            jax.ShapeDtypeStruct(bias.shape, F32),
            jax.ShapeDtypeStruct(g2.shape, F32),
            jax.ShapeDtypeStruct(g2.shape, F32),
        ),
        in_specs=[hbm] * 4 + [pl.BlockSpec(memory_space=pltpu.SMEM)] + [hbm] * 2 + [vmem] * 5,
        out_specs=(hbm, hbm) + (vmem,) * 7,
        scratch_shapes=[
            pltpu.VMEM((seqs, bins, chans), BF),
            pltpu.VMEM((seqs, bins, chans), BF),
            pltpu.VMEM((seqs, bins, 128), F32),
            pltpu.VMEM((seqs, tall, chans), BF),
            pltpu.VMEM((seqs, bins, hid), F32),
            pltpu.VMEM((seqs, bins, hid), F32),
            pltpu.VMEM((seqs, bins, hid), BF),
            pltpu.VMEM((seqs, tall, hid), BF),
            pltpu.VMEM((seqs, bins, 3 * hid), BF),
            pltpu.VMEM((seqs, bins, chans), F32),
            pltpu.VMEM((seqs, bins, chans), BF),
        ]
        + sums(4, chans) + sums(4, hid) + sums(2, hid) + sums(2, chans)
        + [m for m in scratch if m is not None]
        + [
            dma((seqs,)), dma((seqs,)), dma((seqs,)), dma((seqs,)), dma((4,)),
            dma((2,)), dma((2,)), dma((2,)), dma((2,)),
            dma((4, near)), dma((4, near)), dma((4, far)), dma((4, far)),
            dma((nz,)), dma((nz,)), dma((nz, nb)), dma((nz, nb)),
            dma((near, nz, nb)), dma((near, nz, nb)),
            dma((nz,)), dma((nz,)), dma((near, nz)), dma((near, nz)),
        ],
        compiler_params=pltpu.CompilerParams(
            collective_id=0, has_side_effects=True, vmem_limit_bytes=60 * 2**20
        ),
    )(x, og, black, unmap, limit, wd, wp, bias, g1, s1, g2, s2)
    summed = lax.psum((dwd, dwp), "bins")
    return (
        out,
        gin,
        lax.psum_scatter(summed[0], groups, scatter_dimension=0, tiled=True),
        lax.psum_scatter(summed[1], groups, scatter_dimension=0, tiled=True),
        bias_grad,
        g1_grad,
        s1_grad,
        g2_grad,
        s2_grad,
    )


def solution(mesh):
    sizes = (mesh.shape["bins"], mesh.shape["batch"], mesh.shape["fsdp"])
    rows = P(("batch", "fsdp"))
    track = P(("batch", "fsdp"), "bins", None)
    table = P(("batch", "fsdp"), None)
    return jax.shard_map(
        functools.partial(local, sizes),
        mesh=mesh,
        in_specs=(track, P(("batch", "fsdp"), "bins"), P(("batch", "fsdp"), "bins"), rows,
                  table, table, rows, rows, rows, rows, rows, track),
        out_specs=(track, track, table, table, rows, rows, rows, rows, rows),
        check_vma=False,
    )
```

```python
import functools

import jax
import jax.numpy as jnp
from jax import lax
from jax.experimental import pallas as pl
from jax.experimental.pallas import tpu as pltpu
from jax.sharding import PartitionSpec as P

STEP = 26
EPS = 1e-5
PAD = 32
CHUNK = 32
MESH = pl.DeviceIdType.MESH
BF = jnp.bfloat16
F32 = jnp.float32


def dot(a, b, ca, cb):
    return lax.dot_general(a, b, (((ca,), (cb,)), ((), ())), preferred_element_type=F32)


def fold(v):
    rows, width = v.shape
    return jnp.sum(v.reshape(rows // 8, 8, width), axis=0)


def merge(entries):
    total = functools.reduce(jnp.add, [e[0] for e in entries])
    count = functools.reduce(jnp.add, [e[2] for e in entries])
    mean = total / jnp.maximum(count, 1.0)
    square = functools.reduce(jnp.add, [e[1] for e in entries])
    for s, _, n in entries:
        gap = s / jnp.maximum(n, 1.0) - mean
        square = square + n * gap * gap
    return total, square, count


def block(
    sizes,
    x_hbm, og_hbm, black_hbm, unmap_hbm, limit, wd_hbm, wp_hbm, bias_in, g1_in, s1_in, g2_in, s2_in,
    out_hbm, gin_hbm, dwd_out, dwp_out, bias_out, g1_out, s1_out, g2_out, s2_out,
    xin, grad, vm, h1, z1, gw, h2, dz, taps, dg, stage, upper, lower, mcol,
    fs1, fr1, cs1, cr1, fs2, fr2, cs2, cr2, fs3, fr3, cs3, cr3, fs4, fr4, cs4, cr4,
    black, unmap, wd_own, wp_own, pall, par, es, er,
    wd, wp, wall, dwd, dwp, dwd_red, dwp_red,
    xsem, gsem, osem, isem, lsem, hsem, hrem, zsem, zrem, fss, frs, css, crs,
    wzs, wzr, wcs, wcr, wfs, wfr, pzs, pzr, pfs, pfr,
    rfs, rfr, rxs, rxr, rzs, rzr, ras, rar,
):
    nb, nz, nf = sizes
    inside = wall is not None
    seqs, bins, chans = grad.shape
    hid = z1.shape[2]
    wide, narrow = chans // 128, hid // 128
    pieces = bins // CHUNK
    bi, zi, fi = lax.axis_index("bins"), lax.axis_index("batch"), lax.axis_index("fsdp")

    def load_x(s):
        return pltpu.make_async_copy(x_hbm.at[s], xin.at[s], xsem.at[s])

    def load_g(s):
        return pltpu.make_async_copy(og_hbm.at[s], grad.at[s], gsem.at[s])

    small_loads = [
        pltpu.make_async_copy(src, dst, lsem.at[i])
        for i, (src, dst) in enumerate(
            [(black_hbm, black), (unmap_hbm, unmap), (wd_hbm, wd_own), (wp_hbm, wp_own)]
        )
    ]

    mates = [(k,) for k in range(1, nf)]
    chips = [(b, z) for z in range(nz) for b in range(nb) if (b, z) != (0, 0)]

    def mate(k):
        return {"fsdp": lax.rem(fi + k, nf)}

    def chip(b, z):
        return {"bins": lax.rem(bi + b, nb), "batch": lax.rem(zi + z, nz)}

    upper[...] = jnp.zeros_like(upper)
    lower[...] = jnp.zeros_like(lower)
    dz[:, 0:PAD, :] = jnp.zeros((seqs, PAD, hid), BF)
    dz[:, PAD + bins : PAD + bins + PAD, :] = jnp.zeros((seqs, PAD, hid), BF)
    barrier = pltpu.get_barrier_semaphore()
    for (k,) in mates:
        pl.semaphore_signal(barrier, inc=1, device_id=mate(k), device_id_type=MESH)
    for b, z in chips:
        pl.semaphore_signal(barrier, inc=1, device_id=chip(b, z), device_id_type=MESH)

    small_loads[0].start()
    small_loads[1].start()
    for s in range(seqs):
        load_x(s).start()
    small_loads[2].start()
    small_loads[3].start()
    for s in range(seqs):
        load_g(s).start()

    small_loads[0].wait()
    small_loads[1].wait()
    ends = jnp.zeros((seqs, bins), jnp.int32)
    for s in range(seqs):
        row = lax.broadcasted_iota(jnp.int32, (seqs, bins), 0)
        ends = jnp.where(row == s, limit[s], ends)
    place = bi * bins + lax.broadcasted_iota(jnp.int32, (seqs, bins), 1)
    keep = (black[...] == 0) & (unmap[...] == 0) & (place < ends)
    columns = jnp.transpose(keep.astype(F32))
    tally = jnp.zeros((8, 128), F32)
    for s in range(seqs):
        lanes = jnp.broadcast_to(columns[:, s : s + 1], (bins, 128))
        vm[s] = lanes
        tally = tally + fold(lanes)
    own_count = jnp.sum(tally, axis=0, keepdims=True)

    def mask(s, r, copies):
        m = vm[s, r * CHUNK : (r + 1) * CHUNK, :]
        return jnp.concatenate([m] * copies, axis=1)

    low, high = lax.rem(bi + nb - 1, nb), lax.rem(bi + 1, nb)

    def edge_copies(low_src, low_dst, high_src, high_dst, send, recv):
        to_low = pltpu.make_async_remote_copy(
            src_ref=low_src, dst_ref=low_dst, send_sem=send.at[0], recv_sem=recv.at[0],
            device_id={"bins": low}, device_id_type=MESH,
        )
        to_high = pltpu.make_async_remote_copy(
            src_ref=high_src, dst_ref=high_dst, send_sem=send.at[1], recv_sem=recv.at[1],
            device_id={"bins": high}, device_id_type=MESH,
        )
        return to_low, to_high

    def edge_start(to_low, to_high):
        @pl.when(bi > 0)
        def _():
            to_low.start()

        @pl.when(bi < nb - 1)
        def _():
            to_high.start()

    def edge_wait(to_low, to_high):
        @pl.when(bi < nb - 1)
        def _():
            to_low.wait_recv()
            to_high.wait_send()

        @pl.when(bi > 0)
        def _():
            to_high.wait_recv()
            to_low.wait_send()

    def mate_copies(i, src, dst):
        return [
            pltpu.make_async_remote_copy(
                src_ref=src, dst_ref=dst.at[j], send_sem=fss.at[i, j], recv_sem=frs.at[i, j],
                device_id=mate(k), device_id_type=MESH,
            )
            for j, (k,) in enumerate(mates)
        ]

    def chip_copies(i, src, dst):
        return [
            pltpu.make_async_remote_copy(
                src_ref=src, dst_ref=dst.at[j], send_sem=css.at[i, j], recv_sem=crs.at[i, j],
                device_id=chip(b, z), device_id_type=MESH,
            )
            for j, (b, z) in enumerate(chips)
        ]

    def start(copies):
        for c in copies:
            c.start()

    def wait(copies):
        for c in copies:
            c.wait_recv()
        for c in copies:
            c.wait_send()

    def plain_sum(i, fs, fr, cs, cr, filler):
        mine = mate_copies(i, fs, fr)
        start(mine)
        wait(mine)
        both = fs[...]
        for j in range(len(mates)):
            both = both + fr[j]
        cs[...] = both
        far = chip_copies(i, cs, cr)
        start(far)
        filler()
        wait(far)
        total = cs[...]
        for j in range(len(chips)):
            total = total + cr[j]
        return total

    own = zi * nf + fi
    pall[own] = jnp.zeros((8, 128), F32)
    for r, ref in enumerate((bias_in, g1_in, s1_in, g2_in, s2_in)):
        n = ref.shape[0]
        pall[own, r : r + 1, 0:n] = ref[...].astype(BF).astype(F32).reshape(1, n)
    small_loads[2].wait()
    small_loads[3].wait()
    share = wp_own.shape[0]
    if inside:
        base = wd_own.shape[0]
        piece = (base + 2 * share) // nb
        wall[own, 0:base, :] = wd_own[...].astype(BF)
        wall[own, base : base + share, :] = wp_own[:, 0:hid].astype(BF)
        wall[own, base + share : base + 2 * share, :] = wp_own[:, hid:].astype(BF)

    def before(i, k, n):
        return lax.rem(i + n - k, n)

    def send_to(src, dst, ssem, rsem, where):
        return pltpu.make_async_remote_copy(
            src_ref=src, dst_ref=dst, send_sem=ssem, recv_sem=rsem,
            device_id=where, device_id_type=MESH,
        )

    def send(ref, ssem, rsem, where):
        return send_to(ref, ref, ssem, rsem, where)

    def along(k):
        return {"batch": lax.rem(zi + k, nz)}

    def slot(z, f):
        return z * nf + f

    par_far = [send(pall.at[own], pzs.at[k], pzr.at[k], along(k)) for k in range(1, nz)]
    par_near = [
        [
            send(pall.at[slot(before(zi, k, nz), fi)], pfs.at[j, k], pfr.at[j, k], mate(m))
            for j, (m,) in enumerate(mates)
        ]
        for k in range(nz)
    ]

    def part(k, b):
        rows = pl.ds(pl.multiple_of(before(bi, b, nb) * piece, 16), piece)
        return wall.at[slot(before(zi, k, nz), fi), rows, :]

    if inside:
        w_far = [send(part(0, 0), wzs.at[k], wzr.at[k], along(k)) for k in range(1, nz)]
        w_side = [
            [
                send(part(k, 0), wcs.at[k, b], wcr.at[k, b], {"bins": lax.rem(bi + b, nb)})
                for b in range(1, nb)
            ]
            for k in range(1, nz)
        ]
        w_own = [
            send(wall.at[own], wfs.at[j, 0, 0], wfr.at[j, 0, 0], mate(m))
            for j, (m,) in enumerate(mates)
        ]
        w_near = [
            [
                [send(part(k, b), wfs.at[j, k, b], wfr.at[j, k, b], mate(m)) for j, (m,) in enumerate(mates)]
                for b in range(nb)
            ]
            for k in range(1, nz)
        ]

    def reduction(i, bufs, get):
        fs, fr, xs, xr, acc, zs, zr, ga = bufs
        other = lax.rem(fi + 1, 2)

        def f_copy(d):
            return send_to(fs.at[d], fr.at[d], rfs.at[i, d], rfr.at[i, d], mate(1))

        def x_copy(d, b):
            j = lax.rem(bi + b, nb)
            return send_to(
                xs.at[d, j], xr.at[b - 1, d], rxs.at[i, b - 1, d], rxr.at[i, b - 1, d], {"bins": j}
            )

        def z_copy(d):
            return send_to(zs.at[d - 1], zr.at[d - 1], rzs.at[i, d], rzr.at[i, d], along(d))

        def a_copy(b):
            return send_to(
                ga.at[bi], ga.at[bi], ras.at[i, b], rar.at[i, b], {"bins": lax.rem(bi + b, nb)}
            )

        def f_send(d):
            z = lax.rem(zi + d, nz)
            for j in range(nb):
                fs[d, j] = get(slot(z, other), j).astype(BF)
            f_copy(d).start()

        def x_send(d):
            z = lax.rem(zi + d, nz)
            f_copy(d).wait_recv()
            for j in range(nb):
                xs[d, j] = (get(slot(z, fi), j) + fr[d, j].astype(F32)).astype(BF)
            acc[d] = get(slot(z, fi), bi) + fr[d, bi].astype(F32)
            for b in range(1, nb):
                x_copy(d, b).start()

        def z_send(d):
            total = acc[d]
            for b in range(1, nb):
                x_copy(d, b).wait_recv()
                total = total + xr[b - 1, d].astype(F32)
            if d:
                zs[d - 1] = total.astype(BF)
                z_copy(d).start()
            else:
                acc[0] = total

        def a_send(more=None):
            total = acc[0] if more is None else acc[0] + more
            for d in range(1, nz):
                z_copy(d).wait_recv()
                total = total + zr[d - 1].astype(F32)
            ga[bi] = total.astype(BF)
            for b in range(1, nb):
                a_copy(b).start()

        def finish(put):
            for b in range(1, nb):
                a_copy(b).wait_recv()
            for j in range(nb):
                put(j, ga[j].astype(F32))
            for d in range(nz):
                f_copy(d).wait_send()
                for b in range(1, nb):
                    x_copy(d, b).wait_send()
                if d:
                    z_copy(d).wait_send()
            for b in range(1, nb):
                a_copy(b).wait_send()

        return f_send, x_send, z_send, a_send, finish

    far_first = list(range(1, nz)) + [0]
    if inside:
        tall, small = base // nb, 2 * share // nb

        def dwd_get(c, j):
            return dwd[pl.ds(pl.multiple_of(c * base + j * tall, 8), tall), :]

        def dwp_get(c, j):
            rows = pl.ds(pl.multiple_of(c * share + lax.rem(j, 2) * small, 8), small)
            if isinstance(j, int):
                return dwp[rows, j // 2 * hid : (j // 2 + 1) * hid]
            return dwp[rows, pl.ds(pl.multiple_of(j // 2 * hid, 128), hid)]

        wide_f, wide_x, wide_z, wide_a, wide_end = reduction(0, dwd_red, dwd_get)
        point_f, point_x, point_z, point_a, point_end = reduction(1, dwp_red, dwp_get)

    def sums_x(s, acc):
        load_x(s).wait()
        for r in range(pieces):
            xx = xin[s, r * CHUNK : (r + 1) * CHUNK, :].astype(F32)
            acc = acc + fold(xx * mask(s, r, wide))
        return acc

    acc = lax.fori_loop(0, seqs, sums_x, jnp.zeros((8, chans), F32))
    count_wide = jnp.concatenate([own_count] * wide, axis=1)
    count_narrow = jnp.concatenate([own_count] * narrow, axis=1)
    sum_one = jnp.sum(acc, axis=0, keepdims=True)
    local_one = sum_one / jnp.maximum(count_wide, 1.0)

    def squares_x(s, acc):
        for r in range(pieces):
            xx = xin[s, r * CHUNK : (r + 1) * CHUNK, :].astype(F32) - local_one
            acc = acc + fold(xx * xx * mask(s, r, wide))
        return acc

    acc = lax.fori_loop(0, seqs, squares_x, jnp.zeros((8, chans), F32))
    fs1[0:1, :] = sum_one
    fs1[1:2, :] = jnp.sum(acc, axis=0, keepdims=True)
    fs1[2:3, :] = count_wide
    fs1[3:4, :] = count_wide

    def triple(ref):
        return ref[0:1, :], ref[1:2, :], ref[2:3, :]

    pl.semaphore_wait(barrier, len(mates) + len(chips))
    mine = mate_copies(0, fs1, fr1)
    start(mine)
    start(par_far)
    start(par_near[0])
    if inside:
        start(w_far)
        start(w_own)
    wait(mine)
    s_, q_, n_ = merge([triple(fs1)] + [triple(fr1.at[j]) for j in range(len(mates))])
    cs1[0:1, :] = s_
    cs1[1:2, :] = q_
    cs1[2:3, :] = n_
    cs1[3:4, :] = n_
    far = chip_copies(0, cs1, cr1)
    start(far)

    def mask_grad(s, acc):
        load_g(s).wait()
        for r in range(pieces):
            rows = slice(r * CHUNK, (r + 1) * CHUNK)
            g = grad[s, rows, :].astype(F32) * mask(s, r, wide)
            acc = acc + fold(g)
            grad[s, rows, :] = g.astype(BF)
        return acc

    acc = lax.fori_loop(0, seqs, mask_grad, jnp.zeros((8, chans), F32))
    own_bias = jnp.sum(acc, axis=0, keepdims=True)

    for k in range(1, nz):
        par_far[k - 1].wait_recv()
        start(par_near[k])
        if inside:
            w_far[k - 1].wait_recv()
            start(w_side[k - 1])
            start(w_near[k - 1][0])
    for k in range(nz):
        for c in par_near[k]:
            c.wait_recv()

    rows = jnp.zeros((8, chans + 256), F32)
    cols = jnp.zeros((8, hid + 256), F32)

    def laid(into, tile, width, index):
        at = index * width
        first, turn = at // 128 * 128, at % 128
        tile = jnp.concatenate([tile, jnp.zeros((8, 128), F32)], axis=1)
        tile = pltpu.roll(tile, turn, 1) if turn else tile
        return jnp.concatenate(
            [t for t in (into[:, :first], into[:, first : first + 256] + tile, into[:, first + 256 :]) if t.shape[1]],
            axis=1,
        )

    for c in range(nz * nf):
        rows = laid(rows, pall[c], bias_in.shape[0], c)
        cols = laid(cols, pall[c], g2_in.shape[0], c)
    par[0:3, :] = rows[0:3, :chans]
    par[3:5, 0:hid] = cols[3:5, :hid]

    wait(far)
    s_, q_, count = merge([triple(cs1)] + [triple(cr1.at[j]) for j in range(len(chips))])
    mean_one = s_ / count
    scale_one = lax.rsqrt(q_ / count + EPS)
    gain_one = par[1:2, :] * scale_one
    shift_one = par[2:3, :]

    h1[:, 0:PAD, :] = jnp.zeros((seqs, PAD, chans), BF)
    h1[:, PAD + bins : PAD + bins + PAD, :] = jnp.zeros((seqs, PAD, chans), BF)

    def first_act(s, acc):
        for r in range(pieces):
            rows = slice(PAD + r * CHUNK, PAD + (r + 1) * CHUNK)
            v = (xin[s, r * CHUNK : (r + 1) * CHUNK, :].astype(F32) - mean_one) * gain_one + shift_one
            v = 0.5 * v + (0.5 * v) * jnp.tanh(0.851 * v)
            h1[s, rows, :] = v.astype(BF)
            acc = acc + fold(v)
        return acc

    acc = lax.fori_loop(0, seqs, first_act, jnp.zeros((8, chans), F32))
    act_sum = jnp.sum(acc, axis=0, keepdims=True)

    if inside:
        for k in range(1, nz):
            for b in range(1, nb):
                w_side[k - 1][b - 1].wait_recv()
                start(w_near[k - 1][b])
        for c in w_own:
            c.wait_recv()
        for k in range(1, nz):
            for b in range(nb):
                for c in w_near[k - 1][b]:
                    c.wait_recv()
        for c in range(nz * nf):
            wd[c * base : (c + 1) * base, :] = wall[c, 0:base, :]
            wp[c * share : (c + 1) * share, 0:hid] = wall[c, base : base + share, :]
            wp[c * share : (c + 1) * share, hid:] = wall[c, base + share : base + 2 * share, :]

    def tap(k):
        return wd[k * chans : (k + 1) * chans, :]

    over = h1[:, PAD + bins - STEP : PAD + bins - STEP + PAD, :].reshape(seqs * PAD, chans)
    es[1] = dot(over, tap(0), 1, 0).astype(BF).reshape(seqs, PAD, hid)
    under = h1[:, STEP : STEP + PAD, :].reshape(seqs * PAD, chans)
    es[0] = dot(under, tap(2), 1, 0).astype(BF).reshape(seqs, PAD, hid)
    e_low, e_high = edge_copies(es.at[0], er.at[0], es.at[1], er.at[1], hsem, hrem)
    edge_start(e_low, e_high)

    def conv(s, _):
        z = None
        for k in range(3):
            first = PAD + (k - 1) * STEP
            part = dot(h1[s, first : first + bins, :], tap(k), 1, 0)
            z = part if z is None else z + part
        z1[s] = z
        return 0

    lax.fori_loop(0, seqs, conv, 0)
    edge_wait(e_low, e_high)

    @pl.when(bi > 0)
    def _():
        z1[:, 0:PAD, :] = z1[:, 0:PAD, :] + er[1].astype(F32)

    @pl.when(bi < nb - 1)
    def _():
        z1[:, bins - PAD :, :] = z1[:, bins - PAD :, :] + er[0].astype(F32)

    def sums_z(s, acc):
        for r in range(pieces):
            acc = acc + fold(z1[s, r * CHUNK : (r + 1) * CHUNK, :] * mask(s, r, narrow))
        return acc

    acc = lax.fori_loop(0, seqs, sums_z, jnp.zeros((8, hid), F32))
    sum_two = jnp.sum(acc, axis=0, keepdims=True)
    local_two = sum_two / jnp.maximum(count_narrow, 1.0)

    def squares_z(s, acc):
        for r in range(pieces):
            z = z1[s, r * CHUNK : (r + 1) * CHUNK, :] - local_two
            acc = acc + fold(z * z * mask(s, r, narrow))
        return acc

    acc = lax.fori_loop(0, seqs, squares_z, jnp.zeros((8, hid), F32))
    fs2[0:1, :] = sum_two
    fs2[1:2, :] = jnp.sum(acc, axis=0, keepdims=True)
    fs2[2:3, :] = own_bias[:, :hid]
    fs2[3:4, :] = own_bias[:, hid:]

    def pair(ref, n):
        return ref[0:1, :], ref[1:2, :], n[2:3, :hid]

    mine = mate_copies(1, fs2, fr2)
    start(mine)
    wait(mine)
    entries = [pair(fs2, fs1)] + [pair(fr2.at[j], fr1.at[j]) for j in range(len(mates))]
    s_, q_, _ = merge(entries)
    bias_part = fs2[2:4, :]
    for j in range(len(mates)):
        bias_part = bias_part + fr2[j, 2:4, :]
    cs2[0:1, :] = s_
    cs2[1:2, :] = q_
    cs2[2:4, :] = bias_part
    far = chip_copies(1, cs2, cr2)
    start(far)

    def grad_point(s, _):
        gw[s] = dot(grad[s], wp[...], 1, 1)
        return 0

    lax.fori_loop(0, seqs, grad_point, 0)

    wait(far)
    entries = [pair(cs2, cs1)] + [pair(cr2.at[j], cr1.at[j]) for j in range(len(chips))]
    s_, q_, _ = merge(entries)
    for j in range(len(chips)):
        bias_part = bias_part + cr2[j, 2:4, :]
    bias_total = jnp.concatenate([bias_part[0:1, :], bias_part[1:2, :]], axis=1)

    def owned(out, row):
        n = out.shape[0]
        row = jnp.concatenate([row, jnp.zeros((1, 256), F32)], axis=1)
        row = jnp.broadcast_to(row, (8, row.shape[1]))
        mine = jnp.zeros((8, 128), F32)
        for c in range(nz * nf):
            first, turn = c * n // 128 * 128, c * n % 128
            tile = row[:, first : first + 256]
            tile = (pltpu.roll(tile, 256 - turn, 1) if turn else tile)[:, :128]
            mine = jnp.where(own == c, tile, mine)
        out[...] = mine[0:1, 0:n].reshape(n)

    owned(bias_out, bias_total)
    mean_two = s_ / count[:, :hid]
    scale_two = lax.rsqrt(q_ / count[:, :hid] + EPS)
    gain_two = par[3:4, :hid]
    shift_two = par[4:5, :hid]

    def second_act(s, acc):
        a, b = acc
        for r in range(pieces):
            rows = slice(r * CHUNK, (r + 1) * CHUNK)
            xh = (z1[s, rows, :] - mean_two) * scale_two
            v = xh * gain_two + shift_two
            t = jnp.tanh(0.851 * v)
            h2[s, rows, :] = (0.5 * v + (0.5 * v) * t).astype(BF)
            d = gw[s, rows, :] * (0.5 + 0.5 * t + (0.4255 * v) * (1.0 - t * t))
            z1[s, rows, :] = xh
            gw[s, rows, :] = d
            a = a + fold(d)
            b = b + fold(d * xh)
        return a, b

    zero = jnp.zeros((8, hid), F32)
    a, b = lax.fori_loop(0, seqs, second_act, (zero, zero))
    fs3[0:1, :] = jnp.sum(a, axis=0, keepdims=True)
    fs3[1:2, :] = jnp.sum(b, axis=0, keepdims=True)
    fs3[2:3, :] = act_sum[:, :hid]
    fs3[3:4, :] = act_sum[:, hid:]

    def store_out(s):
        return pltpu.make_async_copy(stage.at[s], out_hbm.at[s], osem.at[s])

    def point_work():
        def branch(s, _):
            stage[s] = (
                xin[s].astype(F32) + dot(h2[s], wp[...], 1, 0) + par[0:1, :]
            ).astype(BF)
            store_out(s).start()
            return 0

        lax.fori_loop(0, seqs, branch, 0)
        flat = grad[...].reshape(seqs * bins, chans)
        dwp[...] = dot(h2[...].reshape(seqs * bins, hid), flat, 0, 0)

    both = plain_sum(2, fs3, fr3, cs3, cr3, point_work)
    shift_total, gain_total = both[0:1, :], both[1:2, :]
    owned(g2_out, gain_total)
    owned(s2_out, shift_total)
    if inside:
        for d in far_first:
            point_f(d)
    outer = scale_two * gain_two
    level = shift_total / count[:, :hid]
    slant = gain_total / count[:, :hid]

    typical = jnp.concatenate([both[2:3, :], both[3:4, :]], axis=1) / (nb * nz * nf * seqs * bins)
    typical = jnp.concatenate([typical, jnp.zeros((7, chans), F32)], axis=0)
    middle_act = lax.dot_general(
        typical, jnp.ones((8, 128), F32), (((0,), (0,)), ((), ())),
        precision=lax.Precision.HIGHEST, preferred_element_type=F32,
    )
    for k in range(3):
        mcol[k * chans : (k + 1) * chans, :] = middle_act

    def conv_grad(s, acc):
        for r in range(pieces):
            rows = slice(r * CHUNK, (r + 1) * CHUNK)
            d = outer * (gw[s, rows, :] - mask(s, r, narrow) * (level + z1[s, rows, :] * slant))
            dz[s, PAD + r * CHUNK : PAD + (r + 1) * CHUNK, :] = d.astype(BF)
            acc = acc + fold(d)
        return acc

    acc = lax.fori_loop(0, seqs, conv_grad, jnp.zeros((8, hid), F32))
    dz_sum = jnp.sum(acc, axis=0, keepdims=True)

    def rank_one(first, count, row):
        m = mcol[pl.ds(pl.multiple_of(first, 8), count), :]
        return jnp.concatenate([m] * narrow, axis=1) * row

    z_low, z_high = edge_copies(
        dz.at[:, pl.ds(PAD, PAD), :], upper.at[:, pl.ds(PAD, PAD), :],
        dz.at[:, pl.ds(bins, PAD), :], lower.at[:, pl.ds(0, PAD), :], zsem, zrem,
    )
    edge_start(z_low, z_high)

    def shift_taps(s, _):
        for k in range(3):
            first = PAD - (k - 1) * STEP
            taps[s, :, k * hid : (k + 1) * hid] = dz[s, first : first + bins, :]
        return 0

    lax.fori_loop(0, seqs, shift_taps, 0)
    if inside:
        for d in far_first:
            point_x(d)

    def kernel_grad(m, _):
        cols = pl.ds(pl.multiple_of(m * 256, 256), 256)
        left = h1[:, PAD : PAD + bins, cols].reshape(seqs * bins, 256)
        for k in range(3):
            right = taps[:, :, k * hid : (k + 1) * hid].reshape(seqs * bins, hid)
            g = dot(left, right, 0, 0)
            if inside:
                g = g - rank_one(m * 256, 256, dz_sum)
            dwd[pl.ds(pl.multiple_of(k * chans + m * 256, 256), 256), :] = g
        return 0

    lax.fori_loop(0, chans // 256, kernel_grad, 0)

    def middle(s, _):
        dg[s] = dot(taps[s, :, hid : 2 * hid], tap(1), 1, 1)
        return 0

    lax.fori_loop(0, seqs, middle, 0)

    edge_wait(z_low, z_high)
    after = upper[:, STEP : STEP + PAD, :]
    ahead = lower[:, PAD - STEP : 2 * PAD - STEP, :]
    taps[:, bins - PAD :, 0:hid] = taps[:, bins - PAD :, 0:hid] + after
    taps[:, 0:PAD, 2 * hid :] = taps[:, 0:PAD, 2 * hid :] + ahead
    after = after.reshape(seqs * PAD, hid)
    ahead = ahead.reshape(seqs * PAD, hid)

    def kernel_edge(m, _):
        cols = pl.ds(pl.multiple_of(m * 256, 256), 256)
        for k, rows, right in ((0, bins, after), (2, PAD, ahead)):
            left = h1[:, rows : rows + PAD, cols].reshape(seqs * PAD, 256)
            where = pl.ds(pl.multiple_of(k * chans + m * 256, 256), 256)
            dwd[where, :] = dwd[where, :] + dot(left, right, 0, 0)
        return 0

    lax.fori_loop(0, chans // 256, kernel_edge, 0)
    if inside:
        for d in far_first:
            wide_f(d)
        for d in far_first:
            point_z(d)

    def input_side(s, acc):
        a, b = acc
        d = dg[s]
        for k in (0, 2):
            d = d + dot(taps[s, :, k * hid : (k + 1) * hid], tap(k), 1, 1)
        dg[s] = d
        for r in range(pieces):
            rows = slice(r * CHUNK, (r + 1) * CHUNK)
            xc = xin[s, r * CHUNK : (r + 1) * CHUNK, :].astype(F32) - mean_one
            v = xc * gain_one + shift_one
            t = jnp.tanh(0.851 * v)
            d = dg[s, rows, :] * (0.5 + 0.5 * t + (0.4255 * v) * (1.0 - t * t))
            dg[s, rows, :] = d
            a = a + fold(d)
            b = b + fold(d * (xc * scale_one))
        return a, b

    zero = jnp.zeros((8, chans), F32)
    a, b = lax.fori_loop(0, seqs // 2, input_side, (zero, zero))
    if inside:
        for d in far_first:
            wide_x(d)
    a, b = lax.fori_loop(seqs // 2, seqs, input_side, (a, b))
    fs4[0:1, :] = jnp.sum(a, axis=0, keepdims=True)
    fs4[1:2, :] = jnp.sum(b, axis=0, keepdims=True)
    fs4[2:3, :] = jnp.concatenate([dz_sum, dz_sum], axis=1)
    fs4[3:4, :] = fs4[2:3, :]

    def weight_work():
        if inside:
            point_a()
            for d in far_first:
                wide_z(d)

    both = plain_sum(3, fs4, fr4, cs4, cr4, weight_work)
    if inside:
        wide_a(rank_one(own * base + bi * tall, tall, both[2:3, :hid]))
    shift_total, gain_total = both[0:1, :], both[1:2, :]
    owned(g1_out, gain_total)
    owned(s1_out, shift_total)
    level = shift_total / count
    slant = gain_total / count

    def store_in(s):
        return pltpu.make_async_copy(grad.at[s], gin_hbm.at[s], isem.at[s])

    def input_grad(s, _):
        for r in range(pieces):
            rows = slice(r * CHUNK, (r + 1) * CHUNK)
            xc = xin[s, r * CHUNK : (r + 1) * CHUNK, :].astype(F32) - mean_one
            d = dg[s, rows, :] - mask(s, r, wide) * (level + (xc * scale_one) * slant)
            grad[s, rows, :] = (grad[s, rows, :].astype(F32) + gain_one * d).astype(BF)
        store_in(s).start()
        return 0

    lax.fori_loop(0, seqs, input_grad, 0)

    def drain(s, _):
        store_out(s).wait()
        store_in(s).wait()
        return 0

    lax.fori_loop(0, seqs, drain, 0)
    if inside:

        def put_wide(j, v):
            dwd_out[j * tall : (j + 1) * tall, :] = v

        def put_point(j, v):
            dwp_out[j % 2 * small : (j % 2 + 1) * small, j // 2 * hid : (j // 2 + 1) * hid] = v

        point_end(put_point)
        wide_end(put_wide)
    for c in par_far:
        c.wait_send()
    for k in range(nz):
        for c in par_near[k]:
            c.wait_send()
    if inside:
        for c in w_far + w_own:
            c.wait_send()
        for k in range(1, nz):
            for c in w_side[k - 1]:
                c.wait_send()
            for b in range(nb):
                for c in w_near[k - 1][b]:
                    c.wait_send()


def call(sizes, inside, *refs):
    refs = list(refs)
    first = 21 + 14 + 16 + 8
    if inside:
        red = first + 5
        refs[red : red + 16] = [refs[red : red + 8], refs[red + 8 : red + 16]]
    else:
        refs[first:first] = [refs[first - 6], refs[first - 5], None, refs[14], refs[15], None, None]
    block(sizes, *refs)


def local(sizes, x, black, unmap, limit, wd, wp, bias, g1, s1, g2, s2, og):
    nb, nz, nf = sizes
    seqs, bins, chans = x.shape
    hid = wd.shape[1]
    groups = ("batch", "fsdp")
    inside = (
        nf == 2
        and nb == 4
        and wd.shape[0] % (8 * nb) == 0
        and wp.shape[0] % 16 == 0
        and (wd.shape[0] + 2 * wp.shape[0]) % (16 * nb) == 0
        and chans == 2 * hid
    )
    if not inside:
        wd = lax.all_gather(wd.astype(BF), groups, axis=0, tiled=True)
        wp = lax.all_gather(wp.astype(BF), groups, axis=0, tiled=True)
    near, far = nf - 1, nb * nz - 1
    vmem = pl.BlockSpec(memory_space=pltpu.VMEM)
    hbm = pl.BlockSpec(memory_space=pl.ANY)
    dma = pltpu.SemaphoreType.DMA

    def sums(rows, width):
        return [
            pltpu.VMEM((rows, width), F32),
            pltpu.VMEM((near, rows, width), F32),
            pltpu.VMEM((rows, width), F32),
            pltpu.VMEM((far, rows, width), F32),
        ]

    tall = bins + 2 * PAD
    scratch = [
        pltpu.VMEM(black.shape, jnp.int32),
        pltpu.VMEM(black.shape, jnp.int32),
        pltpu.VMEM(wd.shape, wd.dtype),
        pltpu.VMEM(wp.shape, wp.dtype),
        pltpu.VMEM((nz * nf, 8, 128), F32),
        pltpu.VMEM((8, chans), F32),
        pltpu.VMEM((2, seqs, PAD, hid), BF),
        pltpu.VMEM((2, seqs, PAD, hid), BF),
    ]
    if inside:
        scratch += [
            pltpu.VMEM((3 * chans, hid), BF),
            pltpu.VMEM((hid, chans), BF),
            pltpu.VMEM((nz * nf, wd.shape[0] + 2 * wp.shape[0], hid), BF),
            pltpu.VMEM((3 * chans, hid), F32),
            pltpu.VMEM((hid, chans), F32),
        ]
        for p in (wd.shape[0] // nb, 2 * wp.shape[0] // nb):
            scratch += [
                pltpu.VMEM((nz, nb, p, hid), BF),
                pltpu.VMEM((nz, nb, p, hid), BF),
                pltpu.VMEM((nz, nb, p, hid), BF),
                pltpu.VMEM((nb - 1, nz, p, hid), BF),
                pltpu.VMEM((nz, p, hid), F32),
                pltpu.VMEM((nz - 1, p, hid), BF),
                pltpu.VMEM((nz - 1, p, hid), BF),
                pltpu.VMEM((nb, p, hid), BF),
            ]
    out, gin, dwd, dwp, bias_grad, g1_grad, s1_grad, g2_grad, s2_grad = pl.pallas_call(
        functools.partial(call, sizes, inside),
        out_shape=(
            jax.ShapeDtypeStruct(x.shape, BF),
            jax.ShapeDtypeStruct(x.shape, BF),
            jax.ShapeDtypeStruct(wd.shape if inside else (3 * chans, hid), F32),
            jax.ShapeDtypeStruct(wp.shape if inside else (hid, chans), F32),
            jax.ShapeDtypeStruct(bias.shape, F32),
            jax.ShapeDtypeStruct(bias.shape, F32),
            jax.ShapeDtypeStruct(bias.shape, F32),
            jax.ShapeDtypeStruct(g2.shape, F32),
            jax.ShapeDtypeStruct(g2.shape, F32),
        ),
        in_specs=[hbm] * 4 + [pl.BlockSpec(memory_space=pltpu.SMEM)] + [hbm] * 2 + [vmem] * 5,
        out_specs=(hbm, hbm) + (vmem,) * 7,
        scratch_shapes=[
            pltpu.VMEM((seqs, bins, chans), BF),
            pltpu.VMEM((seqs, bins, chans), BF),
            pltpu.VMEM((seqs, bins, 128), F32),
            pltpu.VMEM((seqs, tall, chans), BF),
            pltpu.VMEM((seqs, bins, hid), F32),
            pltpu.VMEM((seqs, bins, hid), F32),
            pltpu.VMEM((seqs, bins, hid), BF),
            pltpu.VMEM((seqs, tall, hid), BF),
            pltpu.VMEM((seqs, bins, 3 * hid), BF),
            pltpu.VMEM((seqs, bins, chans), F32),
            pltpu.VMEM((seqs, bins, chans), BF),
            pltpu.VMEM((seqs, 2 * PAD, hid), BF),
            pltpu.VMEM((seqs, 2 * PAD, hid), BF),
            pltpu.VMEM((3 * chans, 128), F32),
        ]
        + sums(4, chans) + sums(4, hid) + sums(4, hid) + sums(4, chans)
        + scratch
        + [
            dma((seqs,)), dma((seqs,)), dma((seqs,)), dma((seqs,)), dma((4,)),
            dma((2,)), dma((2,)), dma((2,)), dma((2,)),
            dma((4, near)), dma((4, near)), dma((4, far)), dma((4, far)),
            dma((nz,)), dma((nz,)), dma((nz, nb)), dma((nz, nb)),
            dma((near, nz, nb)), dma((near, nz, nb)),
            dma((nz,)), dma((nz,)), dma((near, nz)), dma((near, nz)),
            dma((2, nz)), dma((2, nz)), dma((2, nb, nz)), dma((2, nb, nz)),
            dma((2, nz)), dma((2, nz)), dma((2, nb)), dma((2, nb)),
        ],
        compiler_params=pltpu.CompilerParams(
            collective_id=0, has_side_effects=True, vmem_limit_bytes=60 * 2**20
        ),
    )(x, og, black, unmap, limit, wd, wp, bias, g1, s1, g2, s2)
    if not inside:
        dwd, dwp = lax.psum((dwd, dwp), "bins")
        dwd = lax.psum_scatter(dwd, groups, scatter_dimension=0, tiled=True)
        dwp = lax.psum_scatter(dwp, groups, scatter_dimension=0, tiled=True)
    return (
        out,
        gin,
        dwd,
        dwp,
        bias_grad,
        g1_grad,
        s1_grad,
        g2_grad,
        s2_grad,
    )


def solution(mesh):
    sizes = (mesh.shape["bins"], mesh.shape["batch"], mesh.shape["fsdp"])
    rows = P(("batch", "fsdp"))
    track = P(("batch", "fsdp"), "bins", None)
    table = P(("batch", "fsdp"), None)
    return jax.shard_map(
        functools.partial(local, sizes),
        mesh=mesh,
        in_specs=(track, P(("batch", "fsdp"), "bins"), P(("batch", "fsdp"), "bins"), rows,
                  table, table, rows, rows, rows, rows, rows, track),
        out_specs=(track, track, table, table, rows, rows, rows, rows, rows),
        check_vma=False,
    )
```

```python
import functools

import jax
import jax.numpy as jnp
from jax import lax
from jax.experimental import pallas as pl
from jax.experimental.pallas import tpu as pltpu
from jax.sharding import PartitionSpec as P

STEP = 26
EPS = 1e-5
PAD = 32
CHUNK = 32
MESH = pl.DeviceIdType.MESH
BF = jnp.bfloat16
F32 = jnp.float32


def dot(a, b, ca, cb):
    return lax.dot_general(a, b, (((ca,), (cb,)), ((), ())), preferred_element_type=F32)


def fold(v):
    rows, width = v.shape
    return jnp.sum(v.reshape(rows // 8, 8, width), axis=0)


def merge(entries):
    total = functools.reduce(jnp.add, [e[0] for e in entries])
    count = functools.reduce(jnp.add, [e[2] for e in entries])
    mean = total / jnp.maximum(count, 1.0)
    square = functools.reduce(jnp.add, [e[1] for e in entries])
    for s, _, n in entries:
        gap = s / jnp.maximum(n, 1.0) - mean
        square = square + n * gap * gap
    return total, square, count


def block(
    sizes,
    x_hbm, og_hbm, black_hbm, unmap_hbm, limit, wd_hbm, wp_hbm, bias_in, g1_in, s1_in, g2_in, s2_in,
    out, gin, dwd_out, dwp_out, tile_out,
    xin, grad, vm, h1, z1, gw, h2, dz, taps, dg, zs_out, zs_in, mid_e, mid_z, upper, lower, mcol,
    fs1, fr1, cs1, cr1, fs2, fr2, cs2, cr2, fs3, fr3, cs3, cr3, fs4, fr4, cs4, cr4,
    black, unmap, wd_own, wp_own, pall, par, es, er,
    wt, wd, wp, wall, dwd, dwp, dwd_red, dwp_red,
    xsem, gsem, lsem, hsem, zsem, fss, frs, css, crs,
    wzs, wzr, wcs, wcr, wfs, wfr, pzs, pzr, pfs, pfr,
    rfs, rfr, rxs, rxr, rzs, rzr, ras, rar,
):
    nb, nz, nf = sizes
    inside = wall is not None
    seqs, bins, chans = grad.shape
    hid = z1.shape[2]
    wide, narrow = chans // 128, hid // 128
    pieces = bins // CHUNK
    bi, zi, fi = lax.axis_index("bins"), lax.axis_index("batch"), lax.axis_index("fsdp")

    def load_x(s):
        return pltpu.make_async_copy(x_hbm.at[s], xin.at[s], xsem.at[s])

    def load_g(s):
        return pltpu.make_async_copy(og_hbm.at[s], grad.at[s], gsem.at[s])

    small_loads = [
        pltpu.make_async_copy(src, dst, lsem.at[i])
        for i, (src, dst) in enumerate(
            [(black_hbm, black), (unmap_hbm, unmap), (wd_hbm, wd_own), (wp_hbm, wp_own)]
        )
    ]

    for c in small_loads:
        c.start()
    for s in range(seqs):
        load_x(s).start()
    for s in range(seqs):
        load_g(s).start()

    mates = [(k,) for k in range(1, nf)]
    chips = [(b, z) for z in range(nz) for b in range(nb) if (b, z) != (0, 0)]

    def mate(k):
        return {"fsdp": lax.rem(fi + k, nf)}

    def chip(b, z):
        return {"bins": lax.rem(bi + b, nb), "batch": lax.rem(zi + z, nz)}

    upper[...] = jnp.zeros_like(upper)
    lower[...] = jnp.zeros_like(lower)
    dz[:, 0:PAD, :] = jnp.zeros((seqs, PAD, hid), BF)
    dz[:, PAD + bins : PAD + bins + PAD, :] = jnp.zeros((seqs, PAD, hid), BF)
    barrier = pltpu.get_barrier_semaphore()
    for (k,) in mates:
        pl.semaphore_signal(barrier, inc=1, device_id=mate(k), device_id_type=MESH)
    for b, z in chips:
        pl.semaphore_signal(barrier, inc=1, device_id=chip(b, z), device_id_type=MESH)

    def start(copies):
        for c in copies:
            c.start()

    def wait(copies):
        for c in copies:
            c.wait_recv()
        for c in copies:
            c.wait_send()

    own = zi * nf + fi
    pall[own] = jnp.zeros((8, 128), F32)
    for r, ref in enumerate((bias_in, g1_in, s1_in, g2_in, s2_in)):
        n = ref.shape[0]
        pall[own, r : r + 1, 0:n] = ref[...].astype(BF).astype(F32).reshape(1, n)
    small_loads[2].wait()
    small_loads[3].wait()
    share = wp_own.shape[0]
    if inside:
        base = wd_own.shape[0]
        piece = (base + 2 * share) // nb
        wall[own, 0:base, :] = wd_own[...].astype(BF)
        wall[own, base : base + share, :] = wp_own[:, 0:hid].astype(BF)
        wall[own, base + share : base + 2 * share, :] = wp_own[:, hid:].astype(BF)

    def before(i, k, n):
        return lax.rem(i + n - k, n)

    hops = [h for k in range(1, nz) for h in (k, -k)]

    def sends(h):
        return (zi + h >= 0) & (zi + h < nz)

    def receives(h):
        return (zi - h >= 0) & (zi - h < nz)

    def send_to(src, dst, ssem, rsem, where):
        return pltpu.make_async_remote_copy(
            src_ref=src, dst_ref=dst, send_sem=ssem, recv_sem=rsem,
            device_id=where, device_id_type=MESH,
        )

    def send(ref, ssem, rsem, where):
        return send_to(ref, ref, ssem, rsem, where)

    def along(k):
        return {"batch": lax.rem(zi + k, nz)}

    def slot(z, f):
        return z * nf + f

    par_far = [send(pall.at[own], pzs.at[k], pzr.at[k], along(k)) for k in range(1, nz)]
    par_near = [
        [
            send(pall.at[slot(before(zi, k, nz), fi)], pfs.at[j, k], pfr.at[j, k], mate(m))
            for j, (m,) in enumerate(mates)
        ]
        for k in range(nz)
    ]

    def part(h, b):
        rows = pl.ds(pl.multiple_of(before(bi, b, nb) * piece, 16), piece)
        return wall.at[slot(zi - h, fi), rows, :]

    if inside:
        w_far = {
            h: send(part(0, 0), wzs.at[i], wzr.at[i], {"batch": zi + h}) for i, h in enumerate(hops)
        }
        w_side = {
            h: [
                send(part(h, 0), wcs.at[i, b], wcr.at[i, b], {"bins": lax.rem(bi + b, nb)})
                for b in range(1, nb)
            ]
            for i, h in enumerate(hops)
        }
        w_own = [send(wall.at[own], wfs.at[len(hops), 0], wfr.at[len(hops), 0], mate(1))]
        w_near = {
            h: [send(part(h, b), wfs.at[i, b], wfr.at[i, b], mate(1)) for b in range(nb)]
            for i, h in enumerate(hops)
        }

    def for_hops(test, do):
        for h in hops if inside else ():
            pl.when(test(h))(functools.partial(do, h))

    pl.semaphore_wait(barrier, len(mates) + len(chips))
    for_hops(sends, lambda h: w_far[h].start())
    if inside:
        start(w_own)
    start(par_far)
    start(par_near[0])

    small_loads[0].wait()
    small_loads[1].wait()
    ends = jnp.zeros((seqs, bins), jnp.int32)
    for s in range(seqs):
        row = lax.broadcasted_iota(jnp.int32, (seqs, bins), 0)
        ends = jnp.where(row == s, limit[s], ends)
    place = bi * bins + lax.broadcasted_iota(jnp.int32, (seqs, bins), 1)
    keep = (black[...] == 0) & (unmap[...] == 0) & (place < ends)
    columns = jnp.transpose(keep.astype(F32))
    tally = jnp.zeros((8, 128), F32)
    for s in range(seqs):
        lanes = jnp.broadcast_to(columns[:, s : s + 1], (bins, 128))
        vm[s] = lanes
        tally = tally + fold(lanes)
    own_count = jnp.sum(tally, axis=0, keepdims=True)

    def mask(s, r, copies):
        m = vm[s, r * CHUNK : (r + 1) * CHUNK, :]
        return jnp.concatenate([m] * copies, axis=1)

    low, high = lax.rem(bi + nb - 1, nb), lax.rem(bi + 1, nb)

    relay = nb == 4
    half = seqs // 2

    def edge_copy(src, dst, sems, i, where):
        return pltpu.make_async_remote_copy(
            src_ref=src, dst_ref=dst, send_sem=sems.at[0, i], recv_sem=sems.at[1, i],
            device_id={"bins": where}, device_id_type=MESH,
        )

    def edges(src, dst, mid, sems):
        to_low = [edge_copy(src.at[0, i], dst.at[0, i], sems, i, low) for i in range(2)]
        to_high = [edge_copy(src.at[1, i], dst.at[1, i], sems, 2 + i, high) for i in range(2)]
        by_0 = [edge_copy(src.at[0, 1], mid, sems, 4, 0), edge_copy(mid, dst.at[0, 1], sems, 1, 1)]
        by_3 = [edge_copy(src.at[1, 1], mid, sems, 4, nb - 1), edge_copy(mid, dst.at[1, 1], sems, 3, nb - 2)]

        def sides(do_low, do_high):
            pl.when(bi > 0)(do_low)
            pl.when(bi < nb - 1)(do_high)

        def first():
            def _low():
                to_low[0].start()
                if not relay:
                    to_low[1].start()

            def _high():
                to_high[0].start()
                if not relay:
                    to_high[1].start()

            sides(_low, _high)
            if relay:
                pl.when((bi == 1) | (bi == 3))(to_low[1].start)
                pl.when((bi == 0) | (bi == 2))(to_high[1].start)
                pl.when(bi == 2)(by_0[0].start)
                pl.when(bi == 1)(by_3[0].start)

        def onward():
            def _pass(copies):
                copies[0].wait_recv()
                copies[1].start()

            if relay:
                pl.when(bi == 0)(functools.partial(_pass, by_0))
                pl.when(bi == nb - 1)(functools.partial(_pass, by_3))

        def last():
            def _from_low():
                for c in to_high:
                    c.wait_recv()
                to_low[0].wait_send()
                if not relay:
                    to_low[1].wait_send()

            def _from_high():
                for c in to_low:
                    c.wait_recv()
                to_high[0].wait_send()
                if not relay:
                    to_high[1].wait_send()

            sides(_from_low, _from_high)
            if relay:
                pl.when((bi == 1) | (bi == 3))(to_low[1].wait_send)
                pl.when((bi == 0) | (bi == 2))(to_high[1].wait_send)
                pl.when(bi == 2)(by_0[0].wait_send)
                pl.when(bi == 1)(by_3[0].wait_send)
                pl.when(bi == 0)(by_0[1].wait_send)
                pl.when(bi == nb - 1)(by_3[1].wait_send)

        return first, onward, last

    def packed(s):
        first = s % half * STEP
        return s // half, slice(first, first + STEP), slice(None)

    def mate_copies(i, src, dst):
        return [
            pltpu.make_async_remote_copy(
                src_ref=src, dst_ref=dst.at[j], send_sem=fss.at[i, j], recv_sem=frs.at[i, j],
                device_id=mate(k), device_id_type=MESH,
            )
            for j, (k,) in enumerate(mates)
        ]

    def chip_copies(i, src, dst):
        return [
            pltpu.make_async_remote_copy(
                src_ref=src, dst_ref=dst.at[j], send_sem=css.at[i, j], recv_sem=crs.at[i, j],
                device_id=chip(b, z), device_id_type=MESH,
            )
            for j, (b, z) in enumerate(chips)
        ]

    def plain_sum(i, fs, fr, cs, cr, filler):
        mine = mate_copies(i, fs, fr)
        start(mine)
        wait(mine)
        both = fs[...]
        for j in range(len(mates)):
            both = both + fr[j]
        cs[...] = both
        far = chip_copies(i, cs, cr)
        start(far)
        filler()
        wait(far)
        total = cs[...]
        for j in range(len(chips)):
            total = total + cr[j]
        return total

    def reduction(i, bufs, get):
        fs, fr, xr, acc, zs, zr, ga = bufs
        xs = fs
        other = lax.rem(fi + 1, 2)

        def f_copy(d):
            return send_to(fs.at[d], fr.at[d], rfs.at[i, d], rfr.at[i, d], mate(1))

        def x_copy(d, b):
            j = lax.rem(bi + b, nb)
            return send_to(
                xs.at[d, j], xr.at[b - 1, d], rxs.at[i, b - 1, d], rxr.at[i, b - 1, d], {"bins": j}
            )

        def z_copy(d):
            return send_to(zs.at[d - 1], zr.at[d - 1], rzs.at[i, d], rzr.at[i, d], along(d))

        def a_copy(b):
            return send_to(
                ga.at[bi], ga.at[bi], ras.at[i, b], rar.at[i, b], {"bins": lax.rem(bi + b, nb)}
            )

        def f_send(d):
            z = lax.rem(zi + d, nz)
            for j in range(nb):
                fs[d, j] = get(slot(z, other), j).astype(BF)
            f_copy(d).start()

        def x_send(d):
            z = lax.rem(zi + d, nz)
            f_copy(d).wait()
            for j in range(nb):
                xs[d, j] = (get(slot(z, fi), j) + fr[d, j].astype(F32)).astype(BF)
            acc[d] = get(slot(z, fi), bi) + fr[d, bi].astype(F32)
            for b in range(1, nb):
                x_copy(d, b).start()

        def z_send(d):
            total = acc[d]
            for b in range(1, nb):
                x_copy(d, b).wait_recv()
                total = total + xr[b - 1, d].astype(F32)
            if d:
                zs[d - 1] = total.astype(BF)
                z_copy(d).start()
            else:
                acc[0] = total

        def a_send():
            total = acc[0]
            for d in range(1, nz):
                z_copy(d).wait_recv()
                total = total + zr[d - 1].astype(F32)
            ga[bi] = total.astype(BF)
            for b in range(1, nb):
                a_copy(b).start()

        def finish(put):
            for b in range(1, nb):
                a_copy(b).wait_recv()
            for j in range(nb):
                put(j, ga[j].astype(F32))
            for d in range(nz):
                for b in range(1, nb):
                    x_copy(d, b).wait_send()
                if d:
                    z_copy(d).wait_send()
            for b in range(1, nb):
                a_copy(b).wait_send()

        return f_send, x_send, z_send, a_send, finish

    far_first = list(range(1, nz)) + [0]
    if inside:
        tall, small = base // nb, 2 * share // nb

        def dwd_get(c, j):
            return dwd[pl.ds(pl.multiple_of(c * base + j * tall, 8), tall), :]

        def dwp_get(c, j):
            rows = pl.ds(pl.multiple_of(c * share + lax.rem(j, 2) * small, 8), small)
            if isinstance(j, int):
                return dwp[rows, j // 2 * hid : (j // 2 + 1) * hid]
            return dwp[rows, pl.ds(pl.multiple_of(j // 2 * hid, 128), hid)]

        wide_f, wide_x, wide_z, wide_a, wide_end = reduction(0, dwd_red, dwd_get)
        point_f, point_x, point_z, point_a, point_end = reduction(1, dwp_red, dwp_get)

    def sums_x(s, acc):
        load_x(s).wait()
        for r in range(pieces):
            xx = xin[s, r * CHUNK : (r + 1) * CHUNK, :].astype(F32)
            acc = acc + fold(xx * mask(s, r, wide))
        return acc

    acc = lax.fori_loop(0, seqs, sums_x, jnp.zeros((8, chans), F32))
    count_wide = jnp.concatenate([own_count] * wide, axis=1)
    count_narrow = jnp.concatenate([own_count] * narrow, axis=1)
    sum_one = jnp.sum(acc, axis=0, keepdims=True)
    local_one = sum_one / jnp.maximum(count_wide, 1.0)

    def squares_x(s, acc):
        for r in range(pieces):
            xx = xin[s, r * CHUNK : (r + 1) * CHUNK, :].astype(F32) - local_one
            acc = acc + fold(xx * xx * mask(s, r, wide))
        return acc

    acc = lax.fori_loop(0, seqs, squares_x, jnp.zeros((8, chans), F32))
    fs1[0:1, :] = sum_one
    fs1[1:2, :] = jnp.sum(acc, axis=0, keepdims=True)
    fs1[2:3, :] = count_wide
    fs1[3:4, :] = count_wide

    def triple(ref):
        return ref[0:1, :], ref[1:2, :], ref[2:3, :]

    mine = mate_copies(0, fs1, fr1)
    start(mine)

    def side_work(h):
        w_far[h].wait_recv()
        start(w_side[h])
        w_near[h][0].start()

    for h in hops[:2] if inside else ():
        pl.when(receives(h))(functools.partial(side_work, h))
    wait(mine)
    s_, q_, n_ = merge([triple(fs1)] + [triple(fr1.at[j]) for j in range(len(mates))])
    cs1[0:1, :] = s_
    cs1[1:2, :] = q_
    cs1[2:3, :] = n_
    cs1[3:4, :] = n_
    far = chip_copies(0, cs1, cr1)
    start(far)
    for h in hops[2:] if inside else ():
        pl.when(receives(h))(functools.partial(side_work, h))

    def mask_grad(s, acc):
        load_g(s).wait()
        for r in range(pieces):
            rows = slice(r * CHUNK, (r + 1) * CHUNK)
            g = grad[s, rows, :].astype(F32) * mask(s, r, wide)
            acc = acc + fold(g)
            grad[s, rows, :] = g.astype(BF)
        return acc

    acc = lax.fori_loop(0, seqs, mask_grad, jnp.zeros((8, chans), F32))
    own_bias = jnp.sum(acc, axis=0, keepdims=True)

    for k in range(1, nz):
        par_far[k - 1].wait_recv()
        start(par_near[k])
    for k in range(nz):
        for c in par_near[k]:
            c.wait_recv()

    rows = jnp.zeros((8, chans + 256), F32)
    cols = jnp.zeros((8, hid + 256), F32)

    def laid(into, tile, width, index):
        at = index * width
        first, turn = at // 128 * 128, at % 128
        tile = jnp.concatenate([tile, jnp.zeros((8, 128), F32)], axis=1)
        tile = pltpu.roll(tile, turn, 1) if turn else tile
        return jnp.concatenate(
            [t for t in (into[:, :first], into[:, first : first + 256] + tile, into[:, first + 256 :]) if t.shape[1]],
            axis=1,
        )

    for c in range(nz * nf):
        rows = laid(rows, pall[c], bias_in.shape[0], c)
        cols = laid(cols, pall[c], g2_in.shape[0], c)
    par[0:3, :] = rows[0:3, :chans]
    par[3:5, 0:hid] = cols[3:5, :hid]

    wait(far)
    s_, q_, count = merge([triple(cs1)] + [triple(cr1.at[j]) for j in range(len(chips))])
    mean_one = s_ / count
    scale_one = lax.rsqrt(q_ / count + EPS)
    gain_one = par[1:2, :] * scale_one
    shift_one = par[2:3, :]

    h1[:, 0:PAD, :] = jnp.zeros((seqs, PAD, chans), BF)
    h1[:, PAD + bins : PAD + bins + PAD, :] = jnp.zeros((seqs, PAD, chans), BF)

    def first_act(s, acc):
        for r in range(pieces):
            rows = slice(PAD + r * CHUNK, PAD + (r + 1) * CHUNK)
            v = (xin[s, r * CHUNK : (r + 1) * CHUNK, :].astype(F32) - mean_one) * gain_one + shift_one
            v = 0.5 * v + (0.5 * v) * jnp.tanh(0.851 * v)
            h1[s, rows, :] = v.astype(BF)
            acc = acc + fold(v)
        return acc

    acc = lax.fori_loop(0, seqs, first_act, jnp.zeros((8, chans), F32))
    act_sum = jnp.sum(acc, axis=0, keepdims=True)

    def near_work(h):
        for b in range(1, nb):
            w_side[h][b - 1].wait_recv()
            w_near[h][b].start()

    def near_end(h):
        for c in w_near[h]:
            c.wait_recv()

    for_hops(receives, near_work)
    for_hops(receives, near_end)
    if inside:
        for c in w_own:
            c.wait_recv()
        for c in range(nz * nf):
            wd[c * base : (c + 1) * base, :] = wall[c, 0:base, :]
            wp[c * share : (c + 1) * share, 0:hid] = wall[c, base : base + share, :]
            wp[c * share : (c + 1) * share, hid:] = wall[c, base + share : base + 2 * share, :]

    def tap(k):
        return wd[k * chans : (k + 1) * chans, :]

    over = h1[:, PAD + bins - STEP : PAD + bins - STEP + PAD, :].reshape(seqs * PAD, chans)
    over = dot(over, tap(0), 1, 0).astype(BF)
    under = h1[:, STEP : STEP + PAD, :].reshape(seqs * PAD, chans)
    under = dot(under, tap(2), 1, 0).astype(BF)
    for s in range(seqs):
        es[(1,) + packed(s)] = over[s * PAD : s * PAD + STEP, :]
        es[(0,) + packed(s)] = under[s * PAD + PAD - STEP : s * PAD + PAD, :]
    e_first, e_onward, e_last = edges(es, er, mid_e, hsem)
    e_first()

    group = seqs // 2

    def conv(i, _):
        some = pl.ds(i * group, group)
        z = None
        for k in range(3):
            first = PAD + (k - 1) * STEP
            left = h1[some, first : first + bins, :].reshape(group * bins, chans)
            part = dot(left, tap(k), 1, 0)
            z = part if z is None else z + part
        z1[some] = z.reshape(group, bins, hid)
        return 0

    lax.fori_loop(0, 1, conv, 0)
    e_onward()
    lax.fori_loop(1, 2, conv, 0)

    e_last()

    @pl.when(bi > 0)
    def _():
        for s in range(seqs):
            z1[s, 0:STEP, :] = z1[s, 0:STEP, :] + er[(1,) + packed(s)].astype(F32)

    @pl.when(bi < nb - 1)
    def _():
        for s in range(seqs):
            z1[s, bins - STEP :, :] = z1[s, bins - STEP :, :] + er[(0,) + packed(s)].astype(F32)

    def sums_z(s, acc):
        for r in range(pieces):
            acc = acc + fold(z1[s, r * CHUNK : (r + 1) * CHUNK, :] * mask(s, r, narrow))
        return acc

    acc = lax.fori_loop(0, seqs, sums_z, jnp.zeros((8, hid), F32))
    sum_two = jnp.sum(acc, axis=0, keepdims=True)
    local_two = sum_two / jnp.maximum(count_narrow, 1.0)

    def squares_z(s, acc):
        for r in range(pieces):
            z = z1[s, r * CHUNK : (r + 1) * CHUNK, :] - local_two
            acc = acc + fold(z * z * mask(s, r, narrow))
        return acc

    acc = lax.fori_loop(0, seqs, squares_z, jnp.zeros((8, hid), F32))
    fs2[0:1, :] = sum_two
    fs2[1:2, :] = jnp.sum(acc, axis=0, keepdims=True)
    fs2[2:3, :] = own_bias[:, :hid]
    fs2[3:4, :] = own_bias[:, hid:]

    def pair(ref, n):
        return ref[0:1, :], ref[1:2, :], n[2:3, :hid]

    mine = mate_copies(1, fs2, fr2)
    start(mine)
    wait(mine)
    entries = [pair(fs2, fs1)] + [pair(fr2.at[j], fr1.at[j]) for j in range(len(mates))]
    s_, q_, _ = merge(entries)
    bias_part = fs2[2:4, :]
    for j in range(len(mates)):
        bias_part = bias_part + fr2[j, 2:4, :]
    cs2[0:1, :] = s_
    cs2[1:2, :] = q_
    cs2[2:4, :] = bias_part
    far = chip_copies(1, cs2, cr2)
    start(far)

    def grad_point(i, _):
        some = pl.ds(i * group, group)
        left = grad[some].reshape(group * bins, chans)
        gw[some] = dot(left, wp[...], 1, 1).reshape(group, bins, hid)
        return 0

    lax.fori_loop(0, 2, grad_point, 0)
    for k in range(3):
        wt[k * hid : (k + 1) * hid, :] = jnp.transpose(tap(k))

    wait(far)
    entries = [pair(cs2, cs1)] + [pair(cr2.at[j], cr1.at[j]) for j in range(len(chips))]
    s_, q_, _ = merge(entries)
    for j in range(len(chips)):
        bias_part = bias_part + cr2[j, 2:4, :]
    bias_total = jnp.concatenate([bias_part[0:1, :], bias_part[1:2, :]], axis=1)

    def owned(r, n, row):
        row = jnp.concatenate([row, jnp.zeros((1, 256), F32)], axis=1)
        row = jnp.broadcast_to(row, (8, row.shape[1]))
        mine = jnp.zeros((8, 128), F32)
        for c in range(nz * nf):
            first, turn = c * n // 128 * 128, c * n % 128
            piece_ = row[:, first : first + 256]
            piece_ = (pltpu.roll(piece_, 256 - turn, 1) if turn else piece_)[:, :128]
            mine = jnp.where(own == c, piece_, mine)
        tile_out[r : r + 1, :] = mine[0:1, :]

    wide_row, narrow_row = bias_in.shape[0], g2_in.shape[0]
    owned(0, wide_row, bias_total)
    mean_two = s_ / count[:, :hid]
    scale_two = lax.rsqrt(q_ / count[:, :hid] + EPS)
    gain_two = par[3:4, :hid]
    shift_two = par[4:5, :hid]

    def second_act(s, acc):
        a, b = acc
        for r in range(pieces):
            rows = slice(r * CHUNK, (r + 1) * CHUNK)
            xh = (z1[s, rows, :] - mean_two) * scale_two
            v = xh * gain_two + shift_two
            t = jnp.tanh(0.851 * v)
            h2[s, rows, :] = (0.5 * v + (0.5 * v) * t).astype(BF)
            d = gw[s, rows, :] * (0.5 + 0.5 * t + (0.4255 * v) * (1.0 - t * t))
            z1[s, rows, :] = xh
            gw[s, rows, :] = d
            a = a + fold(d)
            b = b + fold(d * xh)
        return a, b

    zero = jnp.zeros((8, hid), F32)
    a, b = lax.fori_loop(0, seqs, second_act, (zero, zero))
    fs3[0:1, :] = jnp.sum(a, axis=0, keepdims=True)
    fs3[1:2, :] = jnp.sum(b, axis=0, keepdims=True)
    fs3[2:3, :] = act_sum[:, :hid]
    fs3[3:4, :] = act_sum[:, hid:]

    def point_work():
        def branch(s, _):
            out[s] = (
                xin[s].astype(F32) + dot(h2[s], wp[...], 1, 0) + par[0:1, :]
            ).astype(BF)
            return 0

        lax.fori_loop(0, seqs, branch, 0)
        flat = grad[...].reshape(seqs * bins, chans)
        dwp[...] = dot(h2[...].reshape(seqs * bins, hid), flat, 0, 0)

    both = plain_sum(2, fs3, fr3, cs3, cr3, point_work)
    shift_total, gain_total = both[0:1, :], both[1:2, :]
    owned(3, narrow_row, gain_total)
    owned(4, narrow_row, shift_total)
    if inside:
        for d in far_first:
            point_f(d)
    outer = scale_two * gain_two
    level = shift_total / count[:, :hid]
    slant = gain_total / count[:, :hid]

    typical = jnp.concatenate([both[2:3, :], both[3:4, :]], axis=1) / (nb * nz * nf * seqs * bins)
    typical = jnp.concatenate([typical, jnp.zeros((7, chans), F32)], axis=0)
    middle_act = lax.dot_general(
        typical, jnp.ones((8, 128), F32), (((0,), (0,)), ((), ())),
        precision=lax.Precision.HIGHEST, preferred_element_type=F32,
    )
    for k in range(3):
        mcol[k * chans : (k + 1) * chans, :] = middle_act

    def conv_grad(s, acc):
        for r in range(pieces):
            rows = slice(r * CHUNK, (r + 1) * CHUNK)
            d = outer * (gw[s, rows, :] - mask(s, r, narrow) * (level + z1[s, rows, :] * slant))
            dz[s, PAD + r * CHUNK : PAD + (r + 1) * CHUNK, :] = d.astype(BF)
            acc = acc + fold(d)
        return acc

    acc = lax.fori_loop(0, seqs, conv_grad, jnp.zeros((8, hid), F32))
    dz_sum = jnp.sum(acc, axis=0, keepdims=True)

    def rank_one(first, count, row):
        m = mcol[pl.ds(pl.multiple_of(first, 8), count), :]
        return jnp.concatenate([m] * narrow, axis=1) * row

    for s in range(seqs):
        zs_out[(0,) + packed(s)] = dz[s, PAD : PAD + STEP, :]
        zs_out[(1,) + packed(s)] = dz[s, PAD + bins - STEP : PAD + bins, :]
    z_first, z_onward, z_last = edges(zs_out, zs_in, mid_z, zsem)
    z_first()

    def shift_taps(s, _):
        for k in range(3):
            first = PAD - (k - 1) * STEP
            taps[s, :, k * hid : (k + 1) * hid] = dz[s, first : first + bins, :]
        return 0

    lax.fori_loop(0, seqs, shift_taps, 0)
    if inside:
        for d in far_first:
            point_x(d)

    def kernel_grad(m, _):
        cols = pl.ds(pl.multiple_of(m * hid, 128), hid)
        left = h1[:, PAD : PAD + bins, cols].reshape(seqs * bins, hid)
        g = dot(left, taps[...].reshape(seqs * bins, 3 * hid), 0, 0)
        for k in range(3):
            part = g[:, k * hid : (k + 1) * hid]
            if inside:
                part = part - rank_one(m * hid, hid, dz_sum)
            dwd[pl.ds(pl.multiple_of(k * chans + m * hid, 128), hid), :] = part
        return 0

    lax.fori_loop(0, 1, kernel_grad, 0)
    z_onward()
    lax.fori_loop(1, chans // hid, kernel_grad, 0)

    z_last()

    @pl.when(bi < nb - 1)
    def _():
        for s in range(seqs):
            upper[s, PAD - STEP :, :] = zs_in[(0,) + packed(s)]

    @pl.when(bi > 0)
    def _():
        for s in range(seqs):
            lower[s, 0:STEP, :] = zs_in[(1,) + packed(s)]

    after, ahead = upper[...], lower[...]
    taps[:, bins - PAD :, 0:hid] = taps[:, bins - PAD :, 0:hid] + after
    taps[:, 0:PAD, 2 * hid :] = taps[:, 0:PAD, 2 * hid :] + ahead
    after = after.reshape(seqs * PAD, hid)
    ahead = ahead.reshape(seqs * PAD, hid)

    def kernel_edge(m, _):
        cols = pl.ds(pl.multiple_of(m * 256, 256), 256)
        for k, rows, right in ((0, bins, after), (2, PAD, ahead)):
            left = h1[:, rows : rows + PAD, cols].reshape(seqs * PAD, 256)
            where = pl.ds(pl.multiple_of(k * chans + m * 256, 256), 256)
            dwd[where, :] = dwd[where, :] + dot(left, right, 0, 0)
        return 0

    lax.fori_loop(0, chans // 256, kernel_edge, 0)
    if inside:
        for d in far_first:
            wide_f(d)
        for d in far_first:
            point_z(d)
        wide_x(far_first[0])

    def back_conv(i):
        some = pl.ds(i * 2, 2)
        left = taps[some].reshape(2 * bins, 3 * hid)
        dg[some] = dot(left, wt[...], 1, 0).reshape(2, bins, chans)

    def back_act(i, acc):
        a, b = acc
        for s in (2 * i, 2 * i + 1):
            for r in range(pieces):
                rows = slice(r * CHUNK, (r + 1) * CHUNK)
                xc = xin[s, rows, :].astype(F32) - mean_one
                v = xc * gain_one + shift_one
                t = jnp.tanh(0.851 * v)
                d = dg[s, rows, :] * (0.5 + 0.5 * t + (0.4255 * v) * (1.0 - t * t))
                dg[s, rows, :] = d
                a = a + fold(d)
                b = b + fold(d * (xc * scale_one))
        return a, b

    def input_side(i, acc):
        acc = back_act(i - 1, acc)
        back_conv(i)
        return acc

    zero = jnp.zeros((8, chans), F32)
    back_conv(0)
    if inside:
        for d in far_first[1:]:
            wide_x(d)
        point_a()
    a, b = lax.fori_loop(1, seqs // 2, input_side, (zero, zero))
    a, b = back_act(seqs // 2 - 1, (a, b))
    if inside:
        wide_z(far_first[0])
    fs4[0:1, :] = jnp.sum(a, axis=0, keepdims=True)
    fs4[1:2, :] = jnp.sum(b, axis=0, keepdims=True)
    fs4[2:3, :] = jnp.concatenate([dz_sum, dz_sum], axis=1)
    fs4[3:4, :] = fs4[2:3, :]

    def weight_work():
        if inside:
            for d in far_first[1:]:
                wide_z(d)
            wide_a()

    both = plain_sum(3, fs4, fr4, cs4, cr4, weight_work)
    shift_total, gain_total = both[0:1, :], both[1:2, :]
    owned(1, wide_row, gain_total)
    owned(2, wide_row, shift_total)
    level = shift_total / count
    slant = gain_total / count

    def input_grad(s, _):
        for r in range(pieces):
            rows = slice(r * CHUNK, (r + 1) * CHUNK)
            xc = xin[s, r * CHUNK : (r + 1) * CHUNK, :].astype(F32) - mean_one
            d = dg[s, rows, :] - mask(s, r, wide) * (level + (xc * scale_one) * slant)
            gin[s, rows, :] = (grad[s, rows, :].astype(F32) + gain_one * d).astype(BF)
        return 0

    lax.fori_loop(0, seqs, input_grad, 0)

    if inside:

        def put_wide(j, v):
            more = rank_one(own * base + j * tall, tall, both[2:3, :hid])
            dwd_out[j * tall : (j + 1) * tall, :] = v + more

        def put_point(j, v):
            dwp_out[j % 2 * small : (j % 2 + 1) * small, j // 2 * hid : (j // 2 + 1) * hid] = v

        point_end(put_point)
        wide_end(put_wide)
    for c in par_far:
        c.wait_send()
    for k in range(nz):
        for c in par_near[k]:
            c.wait_send()

    def sent(h):
        for c in w_side[h] + w_near[h]:
            c.wait_send()

    for_hops(sends, lambda h: w_far[h].wait_send())
    for_hops(receives, sent)
    if inside:
        for c in w_own:
            c.wait_send()


def call(sizes, inside, *refs):
    refs = list(refs)
    first = 17 + 17 + 16 + 9
    if inside:
        red = first + 5
        refs[red : red + 14] = [refs[red : red + 7], refs[red + 7 : red + 14]]
    else:
        refs[first:first] = [refs[first - 7], refs[first - 6], None, refs[14], refs[15], None, None]
    block(sizes, *refs)


def write_out(out, gin, dwd, dwp, tile, *refs):
    sem = refs[9]
    copies = [
        pltpu.make_async_copy(src, dst, sem.at[i])
        for i, (src, dst) in enumerate(zip((out, gin, dwd, dwp), refs[:4]))
    ]
    for c in copies:
        c.start()
    for r, ref in enumerate(refs[4:9]):
        n = ref.shape[0]
        ref[...] = tile[r : r + 1, 0:n].reshape(n)
    for c in copies:
        c.wait()


def local(sizes, x, black, unmap, limit, wd, wp, bias, g1, s1, g2, s2, og):
    nb, nz, nf = sizes
    seqs, bins, chans = x.shape
    hid = wd.shape[1]
    groups = ("batch", "fsdp")
    inside = (
        nf == 2
        and nb == 4
        and wd.shape[0] % (8 * nb) == 0
        and wp.shape[0] % 16 == 0
        and (wd.shape[0] + 2 * wp.shape[0]) % (16 * nb) == 0
        and chans == 2 * hid
    )
    if not inside:
        wd = lax.all_gather(wd.astype(BF), groups, axis=0, tiled=True)
        wp = lax.all_gather(wp.astype(BF), groups, axis=0, tiled=True)
    near, far = nf - 1, nb * nz - 1
    vmem = pl.BlockSpec(memory_space=pltpu.VMEM)
    hbm = pl.BlockSpec(memory_space=pl.ANY)
    dma = pltpu.SemaphoreType.DMA

    def sums(rows, width):
        return [
            pltpu.VMEM((rows, width), F32),
            pltpu.VMEM((near, rows, width), F32),
            pltpu.VMEM((rows, width), F32),
            pltpu.VMEM((far, rows, width), F32),
        ]

    tall = bins + 2 * PAD
    scratch = [
        pltpu.VMEM(black.shape, jnp.int32),
        pltpu.VMEM(black.shape, jnp.int32),
        pltpu.VMEM(wd.shape, wd.dtype),
        pltpu.VMEM(wp.shape, wp.dtype),
        pltpu.VMEM((nz * nf, 8, 128), F32),
        pltpu.VMEM((8, chans), F32),
        pltpu.VMEM((2, 2, seqs // 2 * STEP, hid), BF),
        pltpu.VMEM((2, 2, seqs // 2 * STEP, hid), BF),
    ]
    scratch.append(pltpu.VMEM((3 * hid, chans), BF))
    if inside:
        scratch += [
            pltpu.VMEM((3 * chans, hid), BF),
            pltpu.VMEM((hid, chans), BF),
            pltpu.VMEM((nz * nf, wd.shape[0] + 2 * wp.shape[0], hid), BF),
            pltpu.VMEM((3 * chans, hid), F32),
            pltpu.VMEM((hid, chans), F32),
        ]
        for p in (wd.shape[0] // nb, 2 * wp.shape[0] // nb):
            scratch += [
                pltpu.VMEM((nz, nb, p, hid), BF),
                pltpu.VMEM((nz, nb, p, hid), BF),
                pltpu.VMEM((nb - 1, nz, p, hid), BF),
                pltpu.VMEM((nz, p, hid), F32),
                pltpu.VMEM((nz - 1, p, hid), BF),
                pltpu.VMEM((nz - 1, p, hid), BF),
                pltpu.VMEM((nb, p, hid), BF),
            ]
    out, gin, dwd, dwp, tile = pl.pallas_call(
        functools.partial(call, sizes, inside),
        out_shape=(
            pltpu.VMEM(x.shape, BF),
            pltpu.VMEM(x.shape, BF),
            pltpu.VMEM(wd.shape if inside else (3 * chans, hid), F32),
            pltpu.VMEM(wp.shape if inside else (hid, chans), F32),
            pltpu.VMEM((8, 128), F32),
        ),
        in_specs=[hbm] * 4 + [pl.BlockSpec(memory_space=pltpu.SMEM)] + [hbm] * 2 + [vmem] * 5,
        out_specs=(vmem,) * 5,
        scratch_shapes=[
            pltpu.VMEM((seqs, bins, chans), BF),
            pltpu.VMEM((seqs, bins, chans), BF),
            pltpu.VMEM((seqs, bins, 128), F32),
            pltpu.VMEM((seqs, tall, chans), BF),
            pltpu.VMEM((seqs, bins, hid), F32),
            pltpu.VMEM((seqs, bins, hid), F32),
            pltpu.VMEM((seqs, bins, hid), BF),
            pltpu.VMEM((seqs, tall, hid), BF),
            pltpu.VMEM((seqs, bins, 3 * hid), BF),
            pltpu.VMEM((seqs, bins, chans), F32),
            pltpu.VMEM((2, 2, seqs // 2 * STEP, hid), BF),
            pltpu.VMEM((2, 2, seqs // 2 * STEP, hid), BF),
            pltpu.VMEM((seqs // 2 * STEP, hid), BF),
            pltpu.VMEM((seqs // 2 * STEP, hid), BF),
            pltpu.VMEM((seqs, PAD, hid), BF),
            pltpu.VMEM((seqs, PAD, hid), BF),
            pltpu.VMEM((3 * chans, 128), F32),
        ]
        + sums(4, chans) + sums(4, hid) + sums(4, hid) + sums(4, chans)
        + scratch
        + [
            dma((seqs,)), dma((seqs,)), dma((4,)),
            dma((2, 5)), dma((2, 5)),
            dma((4, near)), dma((4, near)), dma((4, far)), dma((4, far)),
            dma((2 * nz,)), dma((2 * nz,)), dma((2 * nz, nb)), dma((2 * nz, nb)),
            dma((2 * nz, nb)), dma((2 * nz, nb)),
            dma((nz,)), dma((nz,)), dma((near, nz)), dma((near, nz)),
            dma((2, nz)), dma((2, nz)), dma((2, nb, nz)), dma((2, nb, nz)),
            dma((2, nz)), dma((2, nz)), dma((2, nb)), dma((2, nb)),
        ],
        compiler_params=pltpu.CompilerParams(
            collective_id=0, has_side_effects=True, vmem_limit_bytes=(54 if inside else 50) * 2**20
        ),
    )(x, og, black, unmap, limit, wd, wp, bias, g1, s1, g2, s2)
    if not inside:
        dwd, dwp = lax.psum((dwd, dwp), "bins")
        dwd = lax.psum_scatter(dwd, groups, scatter_dimension=0, tiled=True)
        dwp = lax.psum_scatter(dwp, groups, scatter_dimension=0, tiled=True)
    results = (x, x, dwd, dwp, bias, g1, s1, g2, s2)
    kinds = (BF, BF) + (F32,) * 7
    return pl.pallas_call(
        write_out,
        out_shape=tuple(jax.ShapeDtypeStruct(r.shape, t) for r, t in zip(results, kinds)),
        in_specs=[vmem] * 5,
        out_specs=(hbm,) * 4 + (vmem,) * 5,
        scratch_shapes=[dma((4,))],
        compiler_params=pltpu.CompilerParams(vmem_limit_bytes=2**20),
    )(*(pltpu.with_memory_space_constraint(v, pltpu.VMEM) for v in (out, gin, dwd, dwp, tile)))


def solution(mesh):
    sizes = (mesh.shape["bins"], mesh.shape["batch"], mesh.shape["fsdp"])
    rows = P(("batch", "fsdp"))
    track = P(("batch", "fsdp"), "bins", None)
    table = P(("batch", "fsdp"), None)
    return jax.shard_map(
        functools.partial(local, sizes),
        mesh=mesh,
        in_specs=(track, P(("batch", "fsdp"), "bins"), P(("batch", "fsdp"), "bins"), rows,
                  table, table, rows, rows, rows, rows, rows, track),
        out_specs=(track, track, table, table, rows, rows, rows, rows, rows),
        check_vma=False,
    )
```

```python
import functools

import jax
import jax.numpy as jnp
from jax import lax
from jax.experimental import pallas as pl
from jax.experimental.pallas import tpu as pltpu
from jax.sharding import PartitionSpec as P

STEP = 26
EPS = 1e-5
PAD = 32
CHUNK = 32
MESH = pl.DeviceIdType.MESH
BF = jnp.bfloat16
F32 = jnp.float32


def dot(a, b, ca, cb):
    return lax.dot_general(a, b, (((ca,), (cb,)), ((), ())), preferred_element_type=F32)


def fold(v):
    rows, width = v.shape
    return jnp.sum(v.reshape(rows // 8, 8, width), axis=0)


def merge(entries):
    total = functools.reduce(jnp.add, [e[0] for e in entries])
    count = functools.reduce(jnp.add, [e[2] for e in entries])
    mean = total / jnp.maximum(count, 1.0)
    square = functools.reduce(jnp.add, [e[1] for e in entries])
    for s, _, n in entries:
        gap = s / jnp.maximum(n, 1.0) - mean
        square = square + n * gap * gap
    return total, square, count


def block(
    sizes,
    x_hbm, og_hbm, black_hbm, unmap_hbm, limit, wd_hbm, wp_hbm, bias_in, g1_in, s1_in, g2_in, s2_in,
    out, gin, dwd_out, dwp_out, tile_out,
    xin, grad, vm, h1, z1, gw, h2, dz, taps, dg, zs_out, zs_in, mid_e, mid_z, upper, lower, mcol,
    fs1, fr1, cs1, cr1, fs2, fr2, cs2, cr2, fs3, fr3, cs3, cr3, fs4, fr4, cs4, cr4,
    black, unmap, wd_own, wp_own, pall, par, es, er,
    wt, wd, wp, wall_d, wall_p, dwd, dwp, dwd_red, dwp_red,
    xsem, gsem, lsem, hsem, zsem, fss, frs, css, crs,
    wzs, wzr, wcs, wcr, wfs, wfr, pzs, pzr, pfs, pfr,
    rfs, rfr, rxs, rxr, rzs, rzr, ras, rar,
):
    nb, nz, nf = sizes
    inside = wall_d is not None
    seqs, bins, chans = grad.shape
    hid = z1.shape[2]
    wide, narrow = chans // 128, hid // 128
    pieces = bins // CHUNK
    bi, zi, fi = lax.axis_index("bins"), lax.axis_index("batch"), lax.axis_index("fsdp")

    def load_x(s):
        return pltpu.make_async_copy(x_hbm.at[s], xin.at[s], xsem.at[s])

    def load_g(s):
        return pltpu.make_async_copy(og_hbm.at[s], grad.at[s], gsem.at[s])

    small_loads = [
        pltpu.make_async_copy(src, dst, lsem.at[i])
        for i, (src, dst) in enumerate(
            [(black_hbm, black), (unmap_hbm, unmap), (wd_hbm, wd_own), (wp_hbm, wp_own)]
        )
    ]

    for c in small_loads:
        c.start()
    for s in range(seqs):
        load_x(s).start()
    for s in range(seqs):
        load_g(s).start()

    mates = [(k,) for k in range(1, nf)]
    chips = [(b, z) for z in range(nz) for b in range(nb) if (b, z) != (0, 0)]

    def mate(k):
        return {"fsdp": lax.rem(fi + k, nf)}

    def chip(b, z):
        return {"bins": lax.rem(bi + b, nb), "batch": lax.rem(zi + z, nz)}

    upper[...] = jnp.zeros_like(upper)
    lower[...] = jnp.zeros_like(lower)
    dz[:, 0:PAD, :] = jnp.zeros((seqs, PAD, hid), BF)
    dz[:, PAD + bins : PAD + bins + PAD, :] = jnp.zeros((seqs, PAD, hid), BF)
    barrier = pltpu.get_barrier_semaphore()
    for (k,) in mates:
        pl.semaphore_signal(barrier, inc=1, device_id=mate(k), device_id_type=MESH)
    for b, z in chips:
        pl.semaphore_signal(barrier, inc=1, device_id=chip(b, z), device_id_type=MESH)

    def start(copies):
        for c in copies:
            c.start()

    def wait(copies):
        for c in copies:
            c.wait_recv()
        for c in copies:
            c.wait_send()

    own = zi * nf + fi
    pall[own] = jnp.zeros((8, 128), F32)
    for r, ref in enumerate((bias_in, g1_in, s1_in, g2_in, s2_in)):
        n = ref.shape[0]
        pall[own, r : r + 1, 0:n] = ref[...].astype(BF).astype(F32).reshape(1, n)
    small_loads[2].wait()
    small_loads[3].wait()
    share = wp_own.shape[0]
    if inside:
        base = wd_own.shape[0]
        tall, small = base // nb, 2 * share // nb
        for j in range(nb):
            wall_d[own, j] = wd_own[j * tall : (j + 1) * tall, :].astype(BF)
            first, col = j % 2 * small, j // 2 * hid
            wall_p[own, j] = wp_own[first : first + small, col : col + hid].astype(BF)

    def before(i, k, n):
        return lax.rem(i + n - k, n)

    hops = [h for k in range(1, nz) for h in (k, -k)]

    def sends(h):
        return (zi + h >= 0) & (zi + h < nz)

    def receives(h):
        return (zi - h >= 0) & (zi - h < nz)

    def send_to(src, dst, ssem, rsem, where):
        return pltpu.make_async_remote_copy(
            src_ref=src, dst_ref=dst, send_sem=ssem, recv_sem=rsem,
            device_id=where, device_id_type=MESH,
        )

    def send(ref, ssem, rsem, where):
        return send_to(ref, ref, ssem, rsem, where)

    def along(k):
        return {"batch": lax.rem(zi + k, nz)}

    def slot(z, f):
        return z * nf + f

    par_far = [send(pall.at[own], pzs.at[k], pzr.at[k], along(k)) for k in range(1, nz)]
    par_near = [
        [
            send(pall.at[slot(before(zi, k, nz), fi)], pfs.at[j, k], pfr.at[j, k], mate(m))
            for j, (m,) in enumerate(mates)
        ]
        for k in range(nz)
    ]

    class Spread:
        def __init__(self, i, ref):
            def part(h, b):
                return ref.at[slot(zi - h, fi), before(bi, b, nb)]

            n = len(hops)
            self.far = {
                h: send(part(0, 0), wzs.at[i, k], wzr.at[i, k], {"batch": zi + h})
                for k, h in enumerate(hops)
            }
            self.side = {
                h: [
                    send(part(h, 0), wcs.at[i, k, b], wcr.at[i, k, b], {"bins": lax.rem(bi + b, nb)})
                    for b in range(1, nb)
                ]
                for k, h in enumerate(hops)
            }
            self.own = send(ref.at[own], wfs.at[i, n, 0], wfr.at[i, n, 0], mate(1))
            self.near = {
                h: [send(part(h, b), wfs.at[i, k, b], wfr.at[i, k, b], mate(1)) for b in range(nb)]
                for k, h in enumerate(hops)
            }

        def begin(self):
            for_hops(sends, lambda h: self.far[h].start())
            self.own.start()

        def arrive(self, h):
            self.far[h].wait_recv()
            self.near[h][0].start()

        def across(self, h):
            start(self.side[h])

        def hand_on(self):
            def near_work(h):
                for b in range(1, nb):
                    self.side[h][b - 1].wait_recv()
                    self.near[h][b].start()

            def near_end(h):
                for c in self.near[h]:
                    c.wait_recv()

            for_hops(receives, near_work)
            for_hops(receives, near_end)
            self.own.wait_recv()

        def end(self):
            def sent(h):
                for c in self.side[h] + self.near[h]:
                    c.wait_send()

            for_hops(sends, lambda h: self.far[h].wait_send())
            for_hops(receives, sent)
            self.own.wait_send()

    if inside:
        spread_d, spread_p = Spread(0, wall_d), Spread(1, wall_p)

    def for_hops(test, do):
        for h in hops if inside else ():
            pl.when(test(h))(functools.partial(do, h))

    pl.semaphore_wait(barrier, len(mates) + len(chips))
    if inside:
        spread_d.begin()
    start(par_far)
    start(par_near[0])

    small_loads[0].wait()
    small_loads[1].wait()
    ends = jnp.zeros((seqs, bins), jnp.int32)
    for s in range(seqs):
        row = lax.broadcasted_iota(jnp.int32, (seqs, bins), 0)
        ends = jnp.where(row == s, limit[s], ends)
    place = bi * bins + lax.broadcasted_iota(jnp.int32, (seqs, bins), 1)
    keep = (black[...] == 0) & (unmap[...] == 0) & (place < ends)
    columns = jnp.transpose(keep.astype(F32))
    tally = jnp.zeros((8, 128), F32)
    for s in range(seqs):
        lanes = jnp.broadcast_to(columns[:, s : s + 1], (bins, 128))
        vm[s] = lanes
        tally = tally + fold(lanes)
    own_count = jnp.sum(tally, axis=0, keepdims=True)

    def mask(s, r, copies):
        m = vm[s, r * CHUNK : (r + 1) * CHUNK, :]
        return jnp.concatenate([m] * copies, axis=1)

    low, high = lax.rem(bi + nb - 1, nb), lax.rem(bi + 1, nb)

    relay = nb == 4
    half = seqs // 2

    def edge_copy(src, dst, sems, i, where):
        return pltpu.make_async_remote_copy(
            src_ref=src, dst_ref=dst, send_sem=sems.at[0, i], recv_sem=sems.at[1, i],
            device_id={"bins": where}, device_id_type=MESH,
        )

    def edges(src, dst, mid, sems):
        to_low = [edge_copy(src.at[0, i], dst.at[0, i], sems, i, low) for i in range(2)]
        to_high = [edge_copy(src.at[1, i], dst.at[1, i], sems, 2 + i, high) for i in range(2)]
        by_0 = [edge_copy(src.at[0, 1], mid, sems, 4, 0), edge_copy(mid, dst.at[0, 1], sems, 1, 1)]
        by_3 = [edge_copy(src.at[1, 1], mid, sems, 4, nb - 1), edge_copy(mid, dst.at[1, 1], sems, 3, nb - 2)]

        def sides(do_low, do_high):
            pl.when(bi > 0)(do_low)
            pl.when(bi < nb - 1)(do_high)

        def first():
            def _low():
                to_low[0].start()
                if not relay:
                    to_low[1].start()

            def _high():
                to_high[0].start()
                if not relay:
                    to_high[1].start()

            sides(_low, _high)
            if relay:
                pl.when((bi == 1) | (bi == 3))(to_low[1].start)
                pl.when((bi == 0) | (bi == 2))(to_high[1].start)
                pl.when(bi == 2)(by_0[0].start)
                pl.when(bi == 1)(by_3[0].start)

        def onward():
            def _pass(copies):
                copies[0].wait_recv()
                copies[1].start()

            if relay:
                pl.when(bi == 0)(functools.partial(_pass, by_0))
                pl.when(bi == nb - 1)(functools.partial(_pass, by_3))

        def last():
            def _from_low():
                for c in to_high:
                    c.wait_recv()
                to_low[0].wait_send()
                if not relay:
                    to_low[1].wait_send()

            def _from_high():
                for c in to_low:
                    c.wait_recv()
                to_high[0].wait_send()
                if not relay:
                    to_high[1].wait_send()

            sides(_from_low, _from_high)
            if relay:
                pl.when((bi == 1) | (bi == 3))(to_low[1].wait_send)
                pl.when((bi == 0) | (bi == 2))(to_high[1].wait_send)
                pl.when(bi == 2)(by_0[0].wait_send)
                pl.when(bi == 1)(by_3[0].wait_send)
                pl.when(bi == 0)(by_0[1].wait_send)
                pl.when(bi == nb - 1)(by_3[1].wait_send)

        return first, onward, last

    def packed(s):
        first = s % half * STEP
        return s // half, slice(first, first + STEP), slice(None)

    def mate_copies(i, src, dst):
        return [
            pltpu.make_async_remote_copy(
                src_ref=src, dst_ref=dst.at[j], send_sem=fss.at[i, j], recv_sem=frs.at[i, j],
                device_id=mate(k), device_id_type=MESH,
            )
            for j, (k,) in enumerate(mates)
        ]

    def chip_copies(i, src, dst):
        return [
            pltpu.make_async_remote_copy(
                src_ref=src, dst_ref=dst.at[j], send_sem=css.at[i, j], recv_sem=crs.at[i, j],
                device_id=chip(b, z), device_id_type=MESH,
            )
            for j, (b, z) in enumerate(chips)
        ]

    def plain_sum(i, fs, fr, cs, cr, filler):
        mine = mate_copies(i, fs, fr)
        start(mine)
        wait(mine)
        both = fs[...]
        for j in range(len(mates)):
            both = both + fr[j]
        cs[...] = both
        far = chip_copies(i, cs, cr)
        start(far)
        filler()
        wait(far)
        total = cs[...]
        for j in range(len(chips)):
            total = total + cr[j]
        return total

    def reduction(i, bufs, get):
        fs, fr, xr, acc, zs, zr, ga = bufs
        xs = fs
        other = lax.rem(fi + 1, 2)

        def f_copy(d):
            return send_to(fs.at[d], fr.at[d], rfs.at[i, d], rfr.at[i, d], mate(1))

        def x_copy(d, b):
            j = lax.rem(bi + b, nb)
            return send_to(
                xs.at[d, j], xr.at[b - 1, d], rxs.at[i, b - 1, d], rxr.at[i, b - 1, d], {"bins": j}
            )

        def z_copy(d):
            return send_to(zs.at[d - 1], zr.at[d - 1], rzs.at[i, d], rzr.at[i, d], along(d))

        def a_copy(b):
            return send_to(
                ga.at[bi], ga.at[bi], ras.at[i, b], rar.at[i, b], {"bins": lax.rem(bi + b, nb)}
            )

        def f_send(d):
            z = lax.rem(zi + d, nz)
            for j in range(nb):
                fs[d, j] = get(slot(z, other), j).astype(BF)
            f_copy(d).start()

        def x_send(d):
            z = lax.rem(zi + d, nz)
            f_copy(d).wait()
            for j in range(nb):
                xs[d, j] = (get(slot(z, fi), j) + fr[d, j].astype(F32)).astype(BF)
            acc[d] = get(slot(z, fi), bi) + fr[d, bi].astype(F32)
            for b in range(1, nb):
                x_copy(d, b).start()

        def z_send(d):
            total = acc[d]
            for b in range(1, nb):
                x_copy(d, b).wait_recv()
                total = total + xr[b - 1, d].astype(F32)
            if d:
                zs[d - 1] = total.astype(BF)
                z_copy(d).start()
            else:
                acc[0] = total

        def a_send():
            total = acc[0]
            for d in range(1, nz):
                z_copy(d).wait_recv()
                total = total + zr[d - 1].astype(F32)
            ga[bi] = total.astype(BF)
            for b in range(1, nb):
                a_copy(b).start()

        def finish(put):
            for b in range(1, nb):
                a_copy(b).wait_recv()
            for j in range(nb):
                put(j, ga[j].astype(F32))
            for d in range(nz):
                for b in range(1, nb):
                    x_copy(d, b).wait_send()
                if d:
                    z_copy(d).wait_send()
            for b in range(1, nb):
                a_copy(b).wait_send()

        return f_send, x_send, z_send, a_send, finish

    far_first = list(range(1, nz)) + [0]
    if inside:

        def dwd_get(c, j):
            return dwd[pl.ds(pl.multiple_of(c * base + j * tall, 8), tall), :]

        def dwp_get(c, j):
            rows = pl.ds(pl.multiple_of(c * share + lax.rem(j, 2) * small, 8), small)
            if isinstance(j, int):
                return dwp[rows, j // 2 * hid : (j // 2 + 1) * hid]
            return dwp[rows, pl.ds(pl.multiple_of(j // 2 * hid, 128), hid)]

        wide_f, wide_x, wide_z, wide_a, wide_end = reduction(0, dwd_red, dwd_get)
        point_f, point_x, point_z, point_a, point_end = reduction(1, dwp_red, dwp_get)

    def sums_x(s, acc):
        load_x(s).wait()
        for r in range(pieces):
            xx = xin[s, r * CHUNK : (r + 1) * CHUNK, :].astype(F32)
            acc = acc + fold(xx * mask(s, r, wide))
        return acc

    acc = lax.fori_loop(0, seqs, sums_x, jnp.zeros((8, chans), F32))
    count_wide = jnp.concatenate([own_count] * wide, axis=1)
    count_narrow = jnp.concatenate([own_count] * narrow, axis=1)
    sum_one = jnp.sum(acc, axis=0, keepdims=True)
    local_one = sum_one / jnp.maximum(count_wide, 1.0)

    def squares_x(s, acc):
        for r in range(pieces):
            xx = xin[s, r * CHUNK : (r + 1) * CHUNK, :].astype(F32) - local_one
            acc = acc + fold(xx * xx * mask(s, r, wide))
        return acc

    acc = lax.fori_loop(0, seqs, squares_x, jnp.zeros((8, chans), F32))
    fs1[0:1, :chans] = sum_one
    fs1[1:2, :chans] = jnp.sum(acc, axis=0, keepdims=True)
    fs1[0:1, chans:] = own_count
    fs1[1:2, chans:] = own_count

    def triple(ref):
        n = jnp.concatenate([ref[0:1, chans:]] * wide, axis=1)
        return ref[0:1, :chans], ref[1:2, :chans], n

    mine = mate_copies(0, fs1, fr1)
    start(mine)

    def side_work(h):
        spread_d.arrive(h)
        spread_d.across(h)

    wait(mine)
    s_, q_, n_ = merge([triple(fs1)] + [triple(fr1.at[j]) for j in range(len(mates))])
    cs1[0:1, :chans] = s_
    cs1[1:2, :chans] = q_
    cs1[0:1, chans:] = n_[:, :128]
    cs1[1:2, chans:] = n_[:, :128]
    far = chip_copies(0, cs1, cr1)
    start(far)
    for h in hops if inside else ():
        pl.when(receives(h))(functools.partial(side_work, h))

    def mask_grad(s, acc):
        load_g(s).wait()
        for r in range(pieces):
            rows = slice(r * CHUNK, (r + 1) * CHUNK)
            g = grad[s, rows, :].astype(F32) * mask(s, r, wide)
            acc = acc + fold(g)
            grad[s, rows, :] = g.astype(BF)
        return acc

    acc = lax.fori_loop(0, seqs, mask_grad, jnp.zeros((8, chans), F32))
    own_bias = jnp.sum(acc, axis=0, keepdims=True)

    for k in range(1, nz):
        par_far[k - 1].wait_recv()
        start(par_near[k])
    for k in range(nz):
        for c in par_near[k]:
            c.wait_recv()

    rows = jnp.zeros((8, chans + 256), F32)
    cols = jnp.zeros((8, hid + 256), F32)

    def laid(into, tile, width, index):
        at = index * width
        first, turn = at // 128 * 128, at % 128
        tile = jnp.concatenate([tile, jnp.zeros((8, 128), F32)], axis=1)
        tile = pltpu.roll(tile, turn, 1) if turn else tile
        return jnp.concatenate(
            [t for t in (into[:, :first], into[:, first : first + 256] + tile, into[:, first + 256 :]) if t.shape[1]],
            axis=1,
        )

    for c in range(nz * nf):
        rows = laid(rows, pall[c], bias_in.shape[0], c)
        cols = laid(cols, pall[c], g2_in.shape[0], c)
    par[0:3, :] = rows[0:3, :chans]
    par[3:5, 0:hid] = cols[3:5, :hid]

    wait(far)
    s_, q_, count = merge([triple(cs1)] + [triple(cr1.at[j]) for j in range(len(chips))])
    mean_one = s_ / count
    scale_one = lax.rsqrt(q_ / count + EPS)
    gain_one = par[1:2, :] * scale_one
    shift_one = par[2:3, :]

    h1[:, 0:PAD, :] = jnp.zeros((seqs, PAD, chans), BF)
    h1[:, PAD + bins : PAD + bins + PAD, :] = jnp.zeros((seqs, PAD, chans), BF)

    def first_act(s, acc):
        for r in range(pieces):
            rows = slice(PAD + r * CHUNK, PAD + (r + 1) * CHUNK)
            v = (xin[s, r * CHUNK : (r + 1) * CHUNK, :].astype(F32) - mean_one) * gain_one + shift_one
            v = 0.5 * v + (0.5 * v) * jnp.tanh(0.851 * v)
            h1[s, rows, :] = v.astype(BF)
            acc = acc + fold(v)
        return acc

    acc = lax.fori_loop(0, seqs, first_act, jnp.zeros((8, chans), F32))
    act_sum = jnp.sum(acc, axis=0, keepdims=True)

    if inside:
        spread_p.begin()

    if inside:
        spread_d.hand_on()
        for c in range(nz * nf):
            for j in range(nb):
                first = c * base + j * tall
                wd[first : first + tall, :] = wall_d[c, j]

    def tap(k):
        return wd[k * chans : (k + 1) * chans, :]

    over = h1[:, PAD + bins - STEP : PAD + bins - STEP + PAD, :].reshape(seqs * PAD, chans)
    over = dot(over, tap(0), 1, 0).astype(BF)
    under = h1[:, STEP : STEP + PAD, :].reshape(seqs * PAD, chans)
    under = dot(under, tap(2), 1, 0).astype(BF)
    for s in range(seqs):
        es[(1,) + packed(s)] = over[s * PAD : s * PAD + STEP, :]
        es[(0,) + packed(s)] = under[s * PAD + PAD - STEP : s * PAD + PAD, :]
    e_first, e_onward, e_last = edges(es, er, mid_e, hsem)
    e_first()

    group = seqs // 2

    def conv(i, _):
        some = pl.ds(i * group, group)
        z = None
        for k in range(3):
            first = PAD + (k - 1) * STEP
            left = h1[some, first : first + bins, :].reshape(group * bins, chans)
            part = dot(left, tap(k), 1, 0)
            z = part if z is None else z + part
        z1[some] = z.reshape(group, bins, hid)
        return 0

    lax.fori_loop(0, 1, conv, 0)
    e_onward()
    if inside:
        for_hops(receives, spread_p.arrive)
        for_hops(receives, spread_p.across)
    lax.fori_loop(1, 2, conv, 0)

    e_last()

    @pl.when(bi > 0)
    def _():
        for s in range(seqs):
            z1[s, 0:STEP, :] = z1[s, 0:STEP, :] + er[(1,) + packed(s)].astype(F32)

    @pl.when(bi < nb - 1)
    def _():
        for s in range(seqs):
            z1[s, bins - STEP :, :] = z1[s, bins - STEP :, :] + er[(0,) + packed(s)].astype(F32)

    def sums_z(s, acc):
        for r in range(pieces):
            acc = acc + fold(z1[s, r * CHUNK : (r + 1) * CHUNK, :] * mask(s, r, narrow))
        return acc

    acc = lax.fori_loop(0, seqs, sums_z, jnp.zeros((8, hid), F32))
    sum_two = jnp.sum(acc, axis=0, keepdims=True)
    local_two = sum_two / jnp.maximum(count_narrow, 1.0)

    def squares_z(s, acc):
        for r in range(pieces):
            z = z1[s, r * CHUNK : (r + 1) * CHUNK, :] - local_two
            acc = acc + fold(z * z * mask(s, r, narrow))
        return acc

    acc = lax.fori_loop(0, seqs, squares_z, jnp.zeros((8, hid), F32))
    fs2[0:1, :] = sum_two
    fs2[1:2, :] = jnp.sum(acc, axis=0, keepdims=True)
    fs2[2:3, :] = own_bias[:, :hid]
    fs2[3:4, :] = own_bias[:, hid:]

    def pair(ref, n):
        return ref[0:1, :], ref[1:2, :], jnp.concatenate([n[0:1, chans:]] * narrow, axis=1)

    mine = mate_copies(1, fs2, fr2)
    start(mine)
    wait(mine)
    entries = [pair(fs2, fs1)] + [pair(fr2.at[j], fr1.at[j]) for j in range(len(mates))]
    s_, q_, _ = merge(entries)
    bias_part = fs2[2:4, :]
    for j in range(len(mates)):
        bias_part = bias_part + fr2[j, 2:4, :]
    cs2[0:1, :] = s_
    cs2[1:2, :] = q_
    cs2[2:4, :] = bias_part
    far = chip_copies(1, cs2, cr2)
    start(far)

    def grad_point(i, _):
        some = pl.ds(i * group, group)
        left = grad[some].reshape(group * bins, chans)
        gw[some] = dot(left, wp[...], 1, 1).reshape(group, bins, hid)
        return 0

    for k in range(3):
        wt[k * hid : (k + 1) * hid, :] = jnp.transpose(tap(k))
    if inside:
        spread_p.hand_on()
        for c in range(nz * nf):
            for j in range(nb):
                first, col = c * share + j % 2 * small, j // 2 * hid
                wp[first : first + small, col : col + hid] = wall_p[c, j]
    lax.fori_loop(0, 2, grad_point, 0)

    wait(far)
    entries = [pair(cs2, cs1)] + [pair(cr2.at[j], cr1.at[j]) for j in range(len(chips))]
    s_, q_, _ = merge(entries)
    for j in range(len(chips)):
        bias_part = bias_part + cr2[j, 2:4, :]
    bias_total = jnp.concatenate([bias_part[0:1, :], bias_part[1:2, :]], axis=1)

    def owned(r, n, row):
        row = jnp.concatenate([row, jnp.zeros((1, 256), F32)], axis=1)
        row = jnp.broadcast_to(row, (8, row.shape[1]))
        mine = jnp.zeros((8, 128), F32)
        for c in range(nz * nf):
            first, turn = c * n // 128 * 128, c * n % 128
            piece_ = row[:, first : first + 256]
            piece_ = (pltpu.roll(piece_, 256 - turn, 1) if turn else piece_)[:, :128]
            mine = jnp.where(own == c, piece_, mine)
        tile_out[r : r + 1, :] = mine[0:1, :]

    wide_row, narrow_row = bias_in.shape[0], g2_in.shape[0]
    owned(0, wide_row, bias_total)
    mean_two = s_ / count[:, :hid]
    scale_two = lax.rsqrt(q_ / count[:, :hid] + EPS)
    gain_two = par[3:4, :hid]
    shift_two = par[4:5, :hid]

    def second_act(s, acc):
        a, b = acc
        for r in range(pieces):
            rows = slice(r * CHUNK, (r + 1) * CHUNK)
            xh = (z1[s, rows, :] - mean_two) * scale_two
            v = xh * gain_two + shift_two
            t = jnp.tanh(0.851 * v)
            h2[s, rows, :] = (0.5 * v + (0.5 * v) * t).astype(BF)
            d = gw[s, rows, :] * (0.5 + 0.5 * t + (0.4255 * v) * (1.0 - t * t))
            z1[s, rows, :] = xh
            gw[s, rows, :] = d
            a = a + fold(d)
            b = b + fold(d * xh)
        return a, b

    zero = jnp.zeros((8, hid), F32)
    a, b = lax.fori_loop(0, seqs, second_act, (zero, zero))
    fs3[0:1, :] = jnp.sum(a, axis=0, keepdims=True)
    fs3[1:2, :] = jnp.sum(b, axis=0, keepdims=True)
    fs3[2:3, :] = act_sum[:, :hid]
    fs3[3:4, :] = act_sum[:, hid:]

    def point_work():
        flat = grad[...].reshape(seqs * bins, chans)
        dwp[...] = dot(h2[...].reshape(seqs * bins, hid), flat, 0, 0)
        if inside:
            for d in far_first:
                point_f(d)

        def branch(i, _):
            some = pl.ds(i * 2, 2)
            more = dot(h2[some].reshape(2 * bins, hid), wp[...], 1, 0) + par[0:1, :]
            out[some] = (xin[some].astype(F32) + more.reshape(2, bins, chans)).astype(BF)
            return 0

        lax.fori_loop(0, seqs // 2, branch, 0)
        if inside:
            for d in far_first:
                point_x(d)

    both = plain_sum(2, fs3, fr3, cs3, cr3, point_work)
    shift_total, gain_total = both[0:1, :], both[1:2, :]
    owned(3, narrow_row, gain_total)
    owned(4, narrow_row, shift_total)
    outer = scale_two * gain_two
    level = shift_total / count[:, :hid]
    slant = gain_total / count[:, :hid]

    dz_sum = outer * (
        fs3[0:1, :] - level * count_narrow - slant * (sum_two - count_narrow * mean_two) * scale_two
    )
    typical = jnp.concatenate([both[2:3, :], both[3:4, :]], axis=1) / (nb * nz * nf * seqs * bins)
    typical = jnp.concatenate([typical, jnp.zeros((7, chans), F32)], axis=0)
    middle_act = lax.dot_general(
        typical, jnp.ones((8, 128), F32), (((0,), (0,)), ((), ())),
        precision=lax.Precision.HIGHEST, preferred_element_type=F32,
    )
    mcol[...] = middle_act

    def conv_grad(s, _):
        for r in range(pieces):
            rows = slice(r * CHUNK, (r + 1) * CHUNK)
            d = outer * (gw[s, rows, :] - mask(s, r, narrow) * (level + z1[s, rows, :] * slant))
            dz[s, PAD + r * CHUNK : PAD + (r + 1) * CHUNK, :] = d.astype(BF)
        return 0

    lax.fori_loop(0, seqs, conv_grad, 0)

    def rank_one(first, count, row):
        m = mcol[pl.ds(pl.multiple_of(first, 8), count), :]
        return jnp.concatenate([m] * narrow, axis=1) * row

    for s in range(seqs):
        zs_out[(0,) + packed(s)] = dz[s, PAD : PAD + STEP, :]
        zs_out[(1,) + packed(s)] = dz[s, PAD + bins - STEP : PAD + bins, :]
    z_first, z_onward, z_last = edges(zs_out, zs_in, mid_z, zsem)
    z_first()

    def shift_taps(s, _):
        for k in range(3):
            first = PAD - (k - 1) * STEP
            taps[s, :, k * hid : (k + 1) * hid] = dz[s, first : first + bins, :]
        return 0

    lax.fori_loop(0, seqs, shift_taps, 0)

    def kernel_grad(m, _):
        cols = pl.ds(pl.multiple_of(m * hid, 128), hid)
        left = h1[:, PAD : PAD + bins, cols].reshape(seqs * bins, hid)
        g = dot(left, taps[...].reshape(seqs * bins, 3 * hid), 0, 0)
        for k in range(3):
            part = g[:, k * hid : (k + 1) * hid]
            if inside:
                part = part - rank_one(m * hid, hid, dz_sum)
            dwd[pl.ds(pl.multiple_of(k * chans + m * hid, 128), hid), :] = part
        return 0

    lax.fori_loop(0, 1, kernel_grad, 0)
    z_onward()
    if inside:
        for d in far_first:
            point_z(d)
    lax.fori_loop(1, chans // hid, kernel_grad, 0)
    if inside:
        point_a()

    z_last()

    @pl.when(bi < nb - 1)
    def _():
        for s in range(seqs):
            upper[s, PAD - STEP :, :] = zs_in[(0,) + packed(s)]

    @pl.when(bi > 0)
    def _():
        for s in range(seqs):
            lower[s, 0:STEP, :] = zs_in[(1,) + packed(s)]

    after, ahead = upper[...], lower[...]
    taps[:, bins - PAD :, 0:hid] = taps[:, bins - PAD :, 0:hid] + after
    taps[:, 0:PAD, 2 * hid :] = taps[:, 0:PAD, 2 * hid :] + ahead
    after = after.reshape(seqs * PAD, hid)
    ahead = ahead.reshape(seqs * PAD, hid)

    def kernel_edge(m, _):
        cols = pl.ds(pl.multiple_of(m * 256, 256), 256)
        for k, rows, right in ((0, bins, after), (2, PAD, ahead)):
            left = h1[:, rows : rows + PAD, cols].reshape(seqs * PAD, 256)
            where = pl.ds(pl.multiple_of(k * chans + m * 256, 256), 256)
            dwd[where, :] = dwd[where, :] + dot(left, right, 0, 0)
        return 0

    lax.fori_loop(0, chans // 256, kernel_edge, 0)
    if inside:
        for d in far_first:
            wide_f(d)
        wide_x(far_first[0])

    def back_conv(i):
        some = pl.ds(i * 2, 2)
        left = taps[some].reshape(2 * bins, 3 * hid)
        dg[some] = dot(left, wt[...], 1, 0).reshape(2, bins, chans)

    def back_act(i, acc):
        a, b = acc
        for s in (2 * i, 2 * i + 1):
            for r in range(pieces):
                rows = slice(r * CHUNK, (r + 1) * CHUNK)
                xc = xin[s, rows, :].astype(F32) - mean_one
                v = xc * gain_one + shift_one
                t = jnp.tanh(0.851 * v)
                d = dg[s, rows, :] * (0.5 + 0.5 * t + (0.4255 * v) * (1.0 - t * t))
                dg[s, rows, :] = d
                a = a + fold(d)
                b = b + fold(d * (xc * scale_one))
        return a, b

    def input_side(i, acc):
        acc = back_act(i - 1, acc)
        back_conv(i)
        return acc

    zero = jnp.zeros((8, chans), F32)
    back_conv(0)
    if inside:
        for d in far_first[1:]:
            wide_x(d)
    a, b = lax.fori_loop(1, seqs // 2, input_side, (zero, zero))
    a, b = back_act(seqs // 2 - 1, (a, b))
    if inside:
        wide_z(far_first[0])
    fs4[0:1, :] = jnp.sum(a, axis=0, keepdims=True)
    fs4[1:2, :] = jnp.sum(b, axis=0, keepdims=True)

    def weight_work():
        if inside:
            for d in far_first[1:]:
                wide_z(d)
            wide_a()

    both = plain_sum(3, fs4, fr4, cs4, cr4, weight_work)
    shift_total, gain_total = both[0:1, :], both[1:2, :]
    owned(1, wide_row, gain_total)
    owned(2, wide_row, shift_total)
    level = shift_total / count
    slant = gain_total / count

    def input_grad(s, _):
        for r in range(pieces):
            rows = slice(r * CHUNK, (r + 1) * CHUNK)
            xc = xin[s, r * CHUNK : (r + 1) * CHUNK, :].astype(F32) - mean_one
            d = dg[s, rows, :] - mask(s, r, wide) * (level + (xc * scale_one) * slant)
            gin[s, rows, :] = (grad[s, rows, :].astype(F32) + gain_one * d).astype(BF)
        return 0

    lax.fori_loop(0, seqs, input_grad, 0)

    if inside:

        def put_wide(j, v):
            dwd_out[j * tall : (j + 1) * tall, :] = v

        def put_point(j, v):
            dwp_out[j % 2 * small : (j % 2 + 1) * small, j // 2 * hid : (j // 2 + 1) * hid] = v

        point_end(put_point)
        wide_end(put_wide)
    for c in par_far:
        c.wait_send()
    for k in range(nz):
        for c in par_near[k]:
            c.wait_send()
    if inside:
        spread_d.end()
        spread_p.end()


def call(sizes, inside, *refs):
    refs = list(refs)
    first = 17 + 17 + 16 + 9
    if inside:
        red = first + 6
        refs[red : red + 14] = [refs[red : red + 7], refs[red + 7 : red + 14]]
    else:
        refs[first:first] = [refs[first - 7], refs[first - 6], None, None, refs[14], refs[15], None, None]
    block(sizes, *refs)


def write_out(out, gin, dwd, dwp, tile, *refs):
    sem = refs[9]
    copies = [
        pltpu.make_async_copy(src, dst, sem.at[i])
        for i, (src, dst) in enumerate(zip((out, gin, dwd, dwp), refs[:4]))
    ]
    for c in copies:
        c.start()
    for r, ref in enumerate(refs[4:9]):
        n = ref.shape[0]
        ref[...] = tile[r : r + 1, 0:n].reshape(n)
    for c in copies:
        c.wait()


def local(sizes, x, black, unmap, limit, wd, wp, bias, g1, s1, g2, s2, og):
    nb, nz, nf = sizes
    seqs, bins, chans = x.shape
    hid = wd.shape[1]
    groups = ("batch", "fsdp")
    inside = (
        nf == 2
        and nb == 4
        and wd.shape[0] % (8 * nb) == 0
        and 2 * wp.shape[0] % (8 * nb) == 0
        and chans == 2 * hid
    )
    if not inside:
        wd = lax.all_gather(wd.astype(BF), groups, axis=0, tiled=True)
        wp = lax.all_gather(wp.astype(BF), groups, axis=0, tiled=True)
    near, far = nf - 1, nb * nz - 1
    steps = 2 * nz if inside else 1
    vmem = pl.BlockSpec(memory_space=pltpu.VMEM)
    hbm = pl.BlockSpec(memory_space=pl.ANY)
    dma = pltpu.SemaphoreType.DMA

    def sums(rows, width):
        return [
            pltpu.VMEM((rows, width), F32),
            pltpu.VMEM((near, rows, width), F32),
            pltpu.VMEM((rows, width), F32),
            pltpu.VMEM((far, rows, width), F32),
        ]

    tall = bins + 2 * PAD
    scratch = [
        pltpu.VMEM(black.shape, jnp.int32),
        pltpu.VMEM(black.shape, jnp.int32),
        pltpu.VMEM(wd.shape, wd.dtype),
        pltpu.VMEM(wp.shape, wp.dtype),
        pltpu.VMEM((nz * nf, 8, 128), F32),
        pltpu.VMEM((8, chans), F32),
        pltpu.VMEM((2, 2, seqs // 2 * STEP, hid), BF),
        pltpu.VMEM((2, 2, seqs // 2 * STEP, hid), BF),
    ]
    scratch.append(pltpu.VMEM((3 * hid, chans), BF))
    if inside:
        scratch += [
            pltpu.VMEM((3 * chans, hid), BF),
            pltpu.VMEM((hid, chans), BF),
            pltpu.VMEM((nz * nf, nb, wd.shape[0] // nb, hid), BF),
            pltpu.VMEM((nz * nf, nb, 2 * wp.shape[0] // nb, hid), BF),
            pltpu.VMEM((3 * chans, hid), F32),
            pltpu.VMEM((hid, chans), F32),
        ]
        for p in (wd.shape[0] // nb, 2 * wp.shape[0] // nb):
            scratch += [
                pltpu.VMEM((nz, nb, p, hid), BF),
                pltpu.VMEM((nz, nb, p, hid), BF),
                pltpu.VMEM((nb - 1, nz, p, hid), BF),
                pltpu.VMEM((nz, p, hid), F32),
                pltpu.VMEM((nz - 1, p, hid), BF),
                pltpu.VMEM((nz - 1, p, hid), BF),
                pltpu.VMEM((nb, p, hid), BF),
            ]
    out, gin, dwd, dwp, tile = pl.pallas_call(
        functools.partial(call, sizes, inside),
        out_shape=(
            pltpu.VMEM(x.shape, BF),
            pltpu.VMEM(x.shape, BF),
            pltpu.VMEM(wd.shape if inside else (3 * chans, hid), F32),
            pltpu.VMEM(wp.shape if inside else (hid, chans), F32),
            pltpu.VMEM((8, 128), F32),
        ),
        in_specs=[hbm] * 4 + [pl.BlockSpec(memory_space=pltpu.SMEM)] + [hbm] * 2 + [vmem] * 5,
        out_specs=(vmem,) * 5,
        scratch_shapes=[
            pltpu.VMEM((seqs, bins, chans), BF),
            pltpu.VMEM((seqs, bins, chans), BF),
            pltpu.VMEM((seqs, bins, 128), F32),
            pltpu.VMEM((seqs, tall, chans), BF),
            pltpu.VMEM((seqs, bins, hid), F32),
            pltpu.VMEM((seqs, bins, hid), F32),
            pltpu.VMEM((seqs, bins, hid), BF),
            pltpu.VMEM((seqs, tall, hid), BF),
            pltpu.VMEM((seqs, bins, 3 * hid), BF),
            pltpu.VMEM((seqs, bins, chans), F32),
            pltpu.VMEM((2, 2, seqs // 2 * STEP, hid), BF),
            pltpu.VMEM((2, 2, seqs // 2 * STEP, hid), BF),
            pltpu.VMEM((seqs // 2 * STEP, hid), BF),
            pltpu.VMEM((seqs // 2 * STEP, hid), BF),
            pltpu.VMEM((seqs, PAD, hid), BF),
            pltpu.VMEM((seqs, PAD, hid), BF),
            pltpu.VMEM((chans, 128), F32),
        ]
        + sums(2, chans + 128) + sums(4, hid) + sums(4, hid) + sums(2, chans)
        + scratch
        + [
            dma((seqs,)), dma((seqs,)), dma((4,)),
            dma((2, 5)), dma((2, 5)),
            dma((4, near)), dma((4, near)), dma((4, far)), dma((4, far)),
            dma((2, steps)), dma((2, steps)), dma((2, steps, nb)), dma((2, steps, nb)),
            dma((2, steps, nb)), dma((2, steps, nb)),
            dma((nz,)), dma((nz,)), dma((near, nz)), dma((near, nz)),
            dma((2, steps)), dma((2, steps)), dma((2, nb, steps)), dma((2, nb, steps)),
            dma((2, steps)), dma((2, steps)), dma((2, nb)), dma((2, nb)),
        ],
        compiler_params=pltpu.CompilerParams(
            collective_id=0, has_side_effects=True, vmem_limit_bytes=(54 if inside else 50) * 2**20
        ),
    )(x, og, black, unmap, limit, wd, wp, bias, g1, s1, g2, s2)
    if not inside:
        dwd, dwp = lax.psum((dwd, dwp), "bins")
        dwd = lax.psum_scatter(dwd, groups, scatter_dimension=0, tiled=True)
        dwp = lax.psum_scatter(dwp, groups, scatter_dimension=0, tiled=True)
    results = (x, x, dwd, dwp, bias, g1, s1, g2, s2)
    kinds = (BF, BF) + (F32,) * 7
    return pl.pallas_call(
        write_out,
        out_shape=tuple(jax.ShapeDtypeStruct(r.shape, t) for r, t in zip(results, kinds)),
        in_specs=[vmem] * 5,
        out_specs=(hbm,) * 4 + (vmem,) * 5,
        scratch_shapes=[dma((4,))],
        compiler_params=pltpu.CompilerParams(vmem_limit_bytes=2**20),
    )(*(pltpu.with_memory_space_constraint(v, pltpu.VMEM) for v in (out, gin, dwd, dwp, tile)))


def solution(mesh):
    sizes = (mesh.shape["bins"], mesh.shape["batch"], mesh.shape["fsdp"])
    rows = P(("batch", "fsdp"))
    track = P(("batch", "fsdp"), "bins", None)
    table = P(("batch", "fsdp"), None)
    return jax.shard_map(
        functools.partial(local, sizes),
        mesh=mesh,
        in_specs=(track, P(("batch", "fsdp"), "bins"), P(("batch", "fsdp"), "bins"), rows,
                  table, table, rows, rows, rows, rows, rows, track),
        out_specs=(track, track, table, table, rows, rows, rows, rows, rows),
        check_vma=False,
    )
```

```python
import functools

import jax
import jax.numpy as jnp
from jax import lax
from jax.experimental import pallas as pl
from jax.experimental.pallas import tpu as pltpu
from jax.sharding import PartitionSpec as P

STEP = 26
EPS = 1e-5
PAD = 32
CHUNK = 16
MESH = pl.DeviceIdType.MESH
BF = jnp.bfloat16
F32 = jnp.float32


def dot(a, b, ca, cb):
    return lax.dot_general(a, b, (((ca,), (cb,)), ((), ())), preferred_element_type=F32)


def fold(v):
    rows, width = v.shape
    return jnp.sum(v.reshape(rows // 8, 8, width), axis=0)


def merge(entries):
    total = functools.reduce(jnp.add, [e[0] for e in entries])
    count = functools.reduce(jnp.add, [e[2] for e in entries])
    mean = total / jnp.maximum(count, 1.0)
    square = functools.reduce(jnp.add, [e[1] for e in entries])
    for s, _, n in entries:
        gap = s / jnp.maximum(n, 1.0) - mean
        square = square + n * gap * gap
    return total, square, count


def block(
    sizes,
    x_hbm, og_hbm, black_hbm, unmap_hbm, limit, wd_hbm, wp_hbm, bias_in, g1_in, s1_in, g2_in, s2_in,
    out, gin, dwd_out, dwp_out, tile_out,
    xin, grad, vm, h1, z1, gw, h2, dz, taps, dg, zs_out, zs_in, mid_e, mid_z, upper, lower, mcol,
    fs1, fr1, cs1, cr1, fs2, fr2, cs2, cr2, fs3, fr3, cs3, cr3, fs4, fr4, cs4, cr4,
    black, unmap, wd_own, wp_own, pall, par, es, er,
    wt, wd, wp, wall_d, wall_p, dwd, dwp, dwd_red, dwp_red,
    xsem, gsem, lsem, hsem, zsem, fss, frs, css, crs,
    wzs, wzr, wcs, wcr, wfs, wfr, pzs, pzr, pfs, pfr,
    rfs, rfr, rxs, rxr, rzs, rzr, ras, rar,
):
    nb, nz, nf = sizes
    inside = wall_d is not None
    seqs, bins, chans = grad.shape
    hid = z1.shape[2]
    wide, narrow = chans // 128, hid // 128
    pieces = bins // CHUNK
    bi, zi, fi = lax.axis_index("bins"), lax.axis_index("batch"), lax.axis_index("fsdp")

    def load_x(s):
        return pltpu.make_async_copy(x_hbm.at[s], xin.at[s], xsem.at[s])

    def load_g(s):
        return pltpu.make_async_copy(og_hbm.at[s], grad.at[s], gsem.at[s])

    small_loads = [
        pltpu.make_async_copy(src, dst, lsem.at[i])
        for i, (src, dst) in enumerate(
            [(black_hbm, black), (unmap_hbm, unmap), (wd_hbm, wd_own), (wp_hbm, wp_own)]
        )
    ]

    for c in small_loads:
        c.start()
    for s in range(seqs):
        load_x(s).start()
    for s in range(seqs):
        load_g(s).start()

    mates = [(k,) for k in range(1, nf)]
    chips = [(b, z) for z in range(nz) for b in range(nb) if (b, z) != (0, 0)]

    def mate(k):
        return {"fsdp": lax.rem(fi + k, nf)}

    def chip(b, z):
        return {"bins": lax.rem(bi + b, nb), "batch": lax.rem(zi + z, nz)}

    upper[...] = jnp.zeros_like(upper)
    lower[...] = jnp.zeros_like(lower)
    dz[:, 0:PAD, :] = jnp.zeros((seqs, PAD, hid), BF)
    dz[:, PAD + bins : PAD + bins + PAD, :] = jnp.zeros((seqs, PAD, hid), BF)
    barrier = pltpu.get_barrier_semaphore()
    for (k,) in mates:
        pl.semaphore_signal(barrier, inc=1, device_id=mate(k), device_id_type=MESH)
    for b, z in chips:
        pl.semaphore_signal(barrier, inc=1, device_id=chip(b, z), device_id_type=MESH)

    def start(copies):
        for c in copies:
            c.start()

    def wait(copies):
        for c in copies:
            c.wait_recv()
        for c in copies:
            c.wait_send()

    own = zi * nf + fi
    pall[own] = jnp.zeros((8, 128), F32)
    for r, ref in enumerate((bias_in, g1_in, s1_in, g2_in, s2_in)):
        n = ref.shape[0]
        pall[own, r : r + 1, 0:n] = ref[...].astype(BF).astype(F32).reshape(1, n)
    small_loads[2].wait()
    small_loads[3].wait()
    share = wp_own.shape[0]
    if inside:
        base = wd_own.shape[0]
        tall, small = base // nb, 2 * share // nb
        for j in range(nb):
            wall_d[own, j] = wd_own[j * tall : (j + 1) * tall, :].astype(BF)
            first, col = j % 2 * small, j // 2 * hid
            wall_p[own, j] = wp_own[first : first + small, col : col + hid].astype(BF)

    def before(i, k, n):
        return lax.rem(i + n - k, n)

    hops = [h for k in range(1, nz) for h in (k, -k)]

    def sends(h):
        return (zi + h >= 0) & (zi + h < nz)

    def receives(h):
        return (zi - h >= 0) & (zi - h < nz)

    def send_to(src, dst, ssem, rsem, where):
        return pltpu.make_async_remote_copy(
            src_ref=src, dst_ref=dst, send_sem=ssem, recv_sem=rsem,
            device_id=where, device_id_type=MESH,
        )

    def send(ref, ssem, rsem, where):
        return send_to(ref, ref, ssem, rsem, where)

    def along(k):
        return {"batch": lax.rem(zi + k, nz)}

    def slot(z, f):
        return z * nf + f

    par_far = [send(pall.at[own], pzs.at[k], pzr.at[k], along(k)) for k in range(1, nz)]
    par_near = [
        [
            send(pall.at[slot(before(zi, k, nz), fi)], pfs.at[j, k], pfr.at[j, k], mate(m))
            for j, (m,) in enumerate(mates)
        ]
        for k in range(nz)
    ]

    class Spread:
        def __init__(self, i, ref):
            def part(h, b):
                return ref.at[slot(zi - h, fi), before(bi, b, nb)]

            n = len(hops)
            self.far = {
                h: send(part(0, 0), wzs.at[i, k], wzr.at[i, k], {"batch": zi + h})
                for k, h in enumerate(hops)
            }
            self.side = {
                h: [
                    send(part(h, 0), wcs.at[i, k, b], wcr.at[i, k, b], {"bins": lax.rem(bi + b, nb)})
                    for b in range(1, nb)
                ]
                for k, h in enumerate(hops)
            }
            self.own = send(ref.at[own], wfs.at[i, n, 0], wfr.at[i, n, 0], mate(1))
            self.near = {
                h: [send(part(h, b), wfs.at[i, k, b], wfr.at[i, k, b], mate(1)) for b in range(nb)]
                for k, h in enumerate(hops)
            }

        def begin(self):
            for_hops(sends, lambda h: self.far[h].start())
            self.own.start()

        def arrive(self, h):
            self.far[h].wait_recv()
            self.near[h][0].start()

        def across(self, h):
            start(self.side[h])

        def hand_on(self):
            def near_work(h):
                for b in range(1, nb):
                    self.side[h][b - 1].wait_recv()
                    self.near[h][b].start()

            def near_end(h):
                for c in self.near[h]:
                    c.wait_recv()

            for_hops(receives, near_work)
            for_hops(receives, near_end)
            self.own.wait_recv()

        def end(self):
            def sent(h):
                for c in self.side[h] + self.near[h]:
                    c.wait_send()

            for_hops(sends, lambda h: self.far[h].wait_send())
            for_hops(receives, sent)
            self.own.wait_send()

    if inside:
        spread_d, spread_p = Spread(0, wall_d), Spread(1, wall_p)

    def for_hops(test, do):
        for h in hops if inside else ():
            pl.when(test(h))(functools.partial(do, h))

    pl.semaphore_wait(barrier, len(mates) + len(chips))
    if inside:
        spread_d.begin()
    start(par_far)
    start(par_near[0])

    small_loads[0].wait()
    small_loads[1].wait()
    ends = jnp.zeros((seqs, bins), jnp.int32)
    for s in range(seqs):
        row = lax.broadcasted_iota(jnp.int32, (seqs, bins), 0)
        ends = jnp.where(row == s, limit[s], ends)
    place = bi * bins + lax.broadcasted_iota(jnp.int32, (seqs, bins), 1)
    keep = (black[...] == 0) & (unmap[...] == 0) & (place < ends)
    columns = jnp.transpose(keep.astype(F32))
    tally = jnp.zeros((8, 128), F32)
    for s in range(seqs):
        lanes = jnp.broadcast_to(columns[:, s : s + 1], (bins, 128))
        vm[s] = lanes
        tally = tally + fold(lanes)
    own_count = jnp.sum(tally, axis=0, keepdims=True)

    def mask(s, r, copies):
        m = vm[s, r * CHUNK : (r + 1) * CHUNK, :]
        return jnp.concatenate([m] * copies, axis=1)

    low, high = lax.rem(bi + nb - 1, nb), lax.rem(bi + 1, nb)

    relay = nb == 4
    half = seqs // 2

    def edge_copy(src, dst, sems, i, where):
        return pltpu.make_async_remote_copy(
            src_ref=src, dst_ref=dst, send_sem=sems.at[0, i], recv_sem=sems.at[1, i],
            device_id={"bins": where}, device_id_type=MESH,
        )

    def edges(src, dst, mid, sems):
        to_low = [edge_copy(src.at[0, i], dst.at[0, i], sems, i, low) for i in range(2)]
        to_high = [edge_copy(src.at[1, i], dst.at[1, i], sems, 2 + i, high) for i in range(2)]
        by_0 = [edge_copy(src.at[0, 1], mid, sems, 4, 0), edge_copy(mid, dst.at[0, 1], sems, 1, 1)]
        by_3 = [edge_copy(src.at[1, 1], mid, sems, 4, nb - 1), edge_copy(mid, dst.at[1, 1], sems, 3, nb - 2)]

        def sides(do_low, do_high):
            pl.when(bi > 0)(do_low)
            pl.when(bi < nb - 1)(do_high)

        def first():
            def _low():
                to_low[0].start()
                if not relay:
                    to_low[1].start()

            def _high():
                to_high[0].start()
                if not relay:
                    to_high[1].start()

            sides(_low, _high)
            if relay:
                pl.when((bi == 1) | (bi == 3))(to_low[1].start)
                pl.when((bi == 0) | (bi == 2))(to_high[1].start)
                pl.when(bi == 2)(by_0[0].start)
                pl.when(bi == 1)(by_3[0].start)

        def onward():
            def _pass(copies):
                copies[0].wait_recv()
                copies[1].start()

            if relay:
                pl.when(bi == 0)(functools.partial(_pass, by_0))
                pl.when(bi == nb - 1)(functools.partial(_pass, by_3))

        def last():
            def _from_low():
                for c in to_high:
                    c.wait_recv()
                to_low[0].wait_send()
                if not relay:
                    to_low[1].wait_send()

            def _from_high():
                for c in to_low:
                    c.wait_recv()
                to_high[0].wait_send()
                if not relay:
                    to_high[1].wait_send()

            sides(_from_low, _from_high)
            if relay:
                pl.when((bi == 1) | (bi == 3))(to_low[1].wait_send)
                pl.when((bi == 0) | (bi == 2))(to_high[1].wait_send)
                pl.when(bi == 2)(by_0[0].wait_send)
                pl.when(bi == 1)(by_3[0].wait_send)
                pl.when(bi == 0)(by_0[1].wait_send)
                pl.when(bi == nb - 1)(by_3[1].wait_send)

        return first, onward, last

    def packed(s):
        first = s % half * STEP
        return s // half, slice(first, first + STEP), slice(None)

    def mate_copies(i, src, dst):
        return [
            pltpu.make_async_remote_copy(
                src_ref=src, dst_ref=dst.at[j], send_sem=fss.at[i, j], recv_sem=frs.at[i, j],
                device_id=mate(k), device_id_type=MESH,
            )
            for j, (k,) in enumerate(mates)
        ]

    def chip_copies(i, src, dst, only=lambda b, z: True):
        return [
            pltpu.make_async_remote_copy(
                src_ref=src, dst_ref=dst.at[j], send_sem=css.at[i, j], recv_sem=crs.at[i, j],
                device_id=chip(b, z), device_id_type=MESH,
            )
            for j, (b, z) in enumerate(chips)
            if only(b, z)
        ]

    def plain_sum(i, fs, fr, cs, cr, filler):
        mine = mate_copies(i, fs, fr)
        start(mine)
        wait(mine)
        both = fs[...]
        for j in range(len(mates)):
            both = both + fr[j]
        cs[...] = both
        far = chip_copies(i, cs, cr)
        start(far)
        filler()
        wait(far)
        total = cs[...]
        for j in range(len(chips)):
            total = total + cr[j]
        return total

    def reduction(i, bufs, get):
        fs, fr, xr, acc, zs, zr, ga = bufs
        xs = fs
        other = lax.rem(fi + 1, 2)

        def f_copy(d):
            return send_to(fs.at[d], fr.at[d], rfs.at[i, d], rfr.at[i, d], mate(1))

        def x_copy(d, b):
            j = lax.rem(bi + b, nb)
            return send_to(
                xs.at[d, j], xr.at[b - 1, d], rxs.at[i, b - 1, d], rxr.at[i, b - 1, d], {"bins": j}
            )

        def z_copy(d):
            return send_to(zs.at[d - 1], zr.at[d - 1], rzs.at[i, d], rzr.at[i, d], along(d))

        def a_copy(b):
            return send_to(
                ga.at[bi], ga.at[bi], ras.at[i, b], rar.at[i, b], {"bins": lax.rem(bi + b, nb)}
            )

        def f_send(d):
            z = lax.rem(zi + d, nz)
            for j in range(nb):
                fs[d, j] = get(slot(z, other), j).astype(BF)
            f_copy(d).start()

        def x_send(d):
            z = lax.rem(zi + d, nz)
            f_copy(d).wait()
            for j in range(nb):
                xs[d, j] = (get(slot(z, fi), j) + fr[d, j].astype(F32)).astype(BF)
            acc[d] = get(slot(z, fi), bi) + fr[d, bi].astype(F32)
            for b in range(1, nb):
                x_copy(d, b).start()

        def z_send(d):
            total = acc[d]
            for b in range(1, nb):
                x_copy(d, b).wait_recv()
                total = total + xr[b - 1, d].astype(F32)
            if d:
                zs[d - 1] = total.astype(BF)
                z_copy(d).start()
            else:
                acc[0] = total

        def a_send():
            total = acc[0]
            for d in range(1, nz):
                z_copy(d).wait_recv()
                total = total + zr[d - 1].astype(F32)
            ga[bi] = total.astype(BF)
            for b in range(1, nb):
                a_copy(b).start()

        def finish(put):
            for b in range(1, nb):
                a_copy(b).wait_recv()
            for j in range(nb):
                put(j, ga[j].astype(F32))
            for d in range(nz):
                for b in range(1, nb):
                    x_copy(d, b).wait_send()
                if d:
                    z_copy(d).wait_send()
            for b in range(1, nb):
                a_copy(b).wait_send()

        return f_send, x_send, z_send, a_send, finish

    far_first = list(range(1, nz)) + [0]
    if inside:

        def dwd_get(c, j):
            return dwd[pl.ds(pl.multiple_of(c * base + j * tall, 8), tall), :]

        def dwp_get(c, j):
            rows = pl.ds(pl.multiple_of(c * share + lax.rem(j, 2) * small, 8), small)
            if isinstance(j, int):
                return dwp[rows, j // 2 * hid : (j // 2 + 1) * hid]
            return dwp[rows, pl.ds(pl.multiple_of(j // 2 * hid, 128), hid)]

        wide_f, wide_x, wide_z, wide_a, wide_end = reduction(0, dwd_red, dwd_get)
        point_f, point_x, point_z, point_a, point_end = reduction(1, dwp_red, dwp_get)

    def sums_x(s, acc):
        load_x(s).wait()
        for r in range(pieces):
            xx = xin[s, r * CHUNK : (r + 1) * CHUNK, :].astype(F32)
            acc = acc + fold(xx * mask(s, r, wide))
        return acc

    acc = lax.fori_loop(0, seqs, sums_x, jnp.zeros((8, chans), F32))
    count_wide = jnp.concatenate([own_count] * wide, axis=1)
    count_narrow = jnp.concatenate([own_count] * narrow, axis=1)
    sum_one = jnp.sum(acc, axis=0, keepdims=True)
    local_one = sum_one / jnp.maximum(count_wide, 1.0)

    def squares_x(s, acc):
        for r in range(pieces):
            xx = xin[s, r * CHUNK : (r + 1) * CHUNK, :].astype(F32) - local_one
            acc = acc + fold(xx * xx * mask(s, r, wide))
        return acc

    acc = lax.fori_loop(0, seqs, squares_x, jnp.zeros((8, chans), F32))
    fs1[0:1, :chans] = sum_one
    fs1[1:2, :chans] = jnp.sum(acc, axis=0, keepdims=True)
    fs1[0:1, chans:] = own_count
    fs1[1:2, chans:] = own_count

    def triple(ref):
        n = jnp.concatenate([ref[0:1, chans:]] * wide, axis=1)
        return ref[0:1, :chans], ref[1:2, :chans], n

    mine = mate_copies(0, fs1, fr1)
    start(mine)

    def side_work(h):
        spread_d.arrive(h)
        spread_d.across(h)

    wait(mine)
    s_, q_, n_ = merge([triple(fs1)] + [triple(fr1.at[j]) for j in range(len(mates))])
    cs1[0:1, :chans] = s_
    cs1[1:2, :chans] = q_
    cs1[0:1, chans:] = n_[:, :128]
    cs1[1:2, chans:] = n_[:, :128]
    far = chip_copies(0, cs1, cr1)
    start(far)
    for h in hops if inside else ():
        pl.when(receives(h))(functools.partial(side_work, h))

    def mask_grad(s, acc):
        load_g(s).wait()
        for r in range(pieces):
            rows = slice(r * CHUNK, (r + 1) * CHUNK)
            g = grad[s, rows, :].astype(F32) * mask(s, r, wide)
            acc = acc + fold(g)
            grad[s, rows, :] = g.astype(BF)
        return acc

    acc = lax.fori_loop(0, seqs, mask_grad, jnp.zeros((8, chans), F32))
    own_bias = jnp.sum(acc, axis=0, keepdims=True)

    for k in range(1, nz):
        par_far[k - 1].wait_recv()
        start(par_near[k])
    for k in range(nz):
        for c in par_near[k]:
            c.wait_recv()

    rows = jnp.zeros((8, chans + 256), F32)
    cols = jnp.zeros((8, hid + 256), F32)

    def laid(into, tile, width, index):
        at = index * width
        first, turn = at // 128 * 128, at % 128
        tile = jnp.concatenate([tile, jnp.zeros((8, 128), F32)], axis=1)
        tile = pltpu.roll(tile, turn, 1) if turn else tile
        return jnp.concatenate(
            [t for t in (into[:, :first], into[:, first : first + 256] + tile, into[:, first + 256 :]) if t.shape[1]],
            axis=1,
        )

    for c in range(nz * nf):
        rows = laid(rows, pall[c], bias_in.shape[0], c)
        cols = laid(cols, pall[c], g2_in.shape[0], c)
    par[0:3, :] = rows[0:3, :chans]
    par[3:5, 0:hid] = cols[3:5, :hid]

    wait(far)
    s_, q_, count = merge([triple(cs1)] + [triple(cr1.at[j]) for j in range(len(chips))])
    mean_one = s_ / count
    scale_one = lax.rsqrt(q_ / count + EPS)
    gain_one = par[1:2, :] * scale_one
    shift_one = par[2:3, :]

    h1[:, 0:PAD, :] = jnp.zeros((seqs, PAD, chans), BF)
    h1[:, PAD + bins : PAD + bins + PAD, :] = jnp.zeros((seqs, PAD, chans), BF)

    def first_act(s, acc):
        for r in range(pieces):
            rows = slice(PAD + r * CHUNK, PAD + (r + 1) * CHUNK)
            v = (xin[s, r * CHUNK : (r + 1) * CHUNK, :].astype(F32) - mean_one) * gain_one + shift_one
            v = 0.5 * v + (0.5 * v) * jnp.tanh(0.851 * v)
            h1[s, rows, :] = v.astype(BF)
            acc = acc + fold(v)
        return acc

    acc = lax.fori_loop(0, seqs, first_act, jnp.zeros((8, chans), F32))
    act_sum = jnp.sum(acc, axis=0, keepdims=True)

    if inside:
        spread_p.begin()

    if inside:
        spread_d.hand_on()
        for c in range(nz * nf):
            for j in range(nb):
                first = c * base + j * tall
                wd[first : first + tall, :] = wall_d[c, j]

    def tap(k):
        return wd[k * chans : (k + 1) * chans, :]

    over = h1[:, PAD + bins - STEP : PAD + bins - STEP + PAD, :].reshape(seqs * PAD, chans)
    over = dot(over, tap(0), 1, 0).astype(BF)
    under = h1[:, STEP : STEP + PAD, :].reshape(seqs * PAD, chans)
    under = dot(under, tap(2), 1, 0).astype(BF)
    for s in range(seqs):
        es[(1,) + packed(s)] = over[s * PAD : s * PAD + STEP, :]
        es[(0,) + packed(s)] = under[s * PAD + PAD - STEP : s * PAD + PAD, :]
    e_first, e_onward, e_last = edges(es, er, mid_e, hsem)
    e_first()

    group = seqs // 2

    def conv(i, _):
        some = pl.ds(i * group, group)
        z = None
        for k in range(3):
            first = PAD + (k - 1) * STEP
            left = h1[some, first : first + bins, :].reshape(group * bins, chans)
            part = dot(left, tap(k), 1, 0)
            z = part if z is None else z + part
        z1[some] = z.reshape(group, bins, hid)
        return 0

    lax.fori_loop(0, 1, conv, 0)
    e_onward()
    if inside:
        for_hops(receives, spread_p.arrive)
        for_hops(receives, spread_p.across)
    lax.fori_loop(1, 2, conv, 0)

    e_last()

    @pl.when(bi > 0)
    def _():
        for s in range(seqs):
            z1[s, 0:STEP, :] = z1[s, 0:STEP, :] + er[(1,) + packed(s)].astype(F32)

    @pl.when(bi < nb - 1)
    def _():
        for s in range(seqs):
            z1[s, bins - STEP :, :] = z1[s, bins - STEP :, :] + er[(0,) + packed(s)].astype(F32)

    def sums_z(s, acc):
        for r in range(pieces):
            acc = acc + fold(z1[s, r * CHUNK : (r + 1) * CHUNK, :] * mask(s, r, narrow))
        return acc

    acc = lax.fori_loop(0, seqs, sums_z, jnp.zeros((8, hid), F32))
    sum_two = jnp.sum(acc, axis=0, keepdims=True)
    local_two = sum_two / jnp.maximum(count_narrow, 1.0)

    def squares_z(s, acc):
        for r in range(pieces):
            z = z1[s, r * CHUNK : (r + 1) * CHUNK, :] - local_two
            acc = acc + fold(z * z * mask(s, r, narrow))
        return acc

    acc = lax.fori_loop(0, seqs, squares_z, jnp.zeros((8, hid), F32))
    fs2[0:1, :] = sum_two
    fs2[1:2, :] = jnp.sum(acc, axis=0, keepdims=True)
    fs2[2:3, :] = own_bias[:, :hid]
    fs2[3:4, :] = own_bias[:, hid:]

    def pair(ref, n):
        return ref[0:1, :], ref[1:2, :], jnp.concatenate([n[0:1, chans:]] * narrow, axis=1)

    mine = mate_copies(1, fs2, fr2)
    start(mine)
    wait(mine)
    entries = [pair(fs2, fs1)] + [pair(fr2.at[j], fr1.at[j]) for j in range(len(mates))]
    s_, q_, _ = merge(entries)
    bias_part = fs2[2:4, :]
    for j in range(len(mates)):
        bias_part = bias_part + fr2[j, 2:4, :]
    cs2[0:1, :] = s_
    cs2[1:2, :] = q_
    cs2[2:4, :] = bias_part
    far = chip_copies(1, cs2, cr2)
    start(far)

    def grad_point(i, _):
        some = pl.ds(i * group, group)
        left = grad[some].reshape(group * bins, chans)
        gw[some] = dot(left, wp[...], 1, 1).reshape(group, bins, hid)
        return 0

    for k in range(3):
        wt[k * hid : (k + 1) * hid, :] = jnp.transpose(tap(k))
    if inside:
        spread_p.hand_on()
        for c in range(nz * nf):
            for j in range(nb):
                first, col = c * share + j % 2 * small, j // 2 * hid
                wp[first : first + small, col : col + hid] = wall_p[c, j]
    lax.fori_loop(0, 2, grad_point, 0)

    wait(far)
    entries = [pair(cs2, cs1)] + [pair(cr2.at[j], cr1.at[j]) for j in range(len(chips))]
    s_, q_, _ = merge(entries)
    for j in range(len(chips)):
        bias_part = bias_part + cr2[j, 2:4, :]
    bias_total = jnp.concatenate([bias_part[0:1, :], bias_part[1:2, :]], axis=1)

    def owned(r, n, row):
        row = jnp.concatenate([row, jnp.zeros((1, 256), F32)], axis=1)
        row = jnp.broadcast_to(row, (8, row.shape[1]))
        mine = jnp.zeros((8, 128), F32)
        for c in range(nz * nf):
            first, turn = c * n // 128 * 128, c * n % 128
            piece_ = row[:, first : first + 256]
            piece_ = (pltpu.roll(piece_, 256 - turn, 1) if turn else piece_)[:, :128]
            mine = jnp.where(own == c, piece_, mine)
        tile_out[r : r + 1, :] = mine[0:1, :]

    wide_row, narrow_row = bias_in.shape[0], g2_in.shape[0]
    owned(0, wide_row, bias_total)
    mean_two = s_ / count[:, :hid]
    scale_two = lax.rsqrt(q_ / count[:, :hid] + EPS)
    gain_two = par[3:4, :hid]
    shift_two = par[4:5, :hid]

    def second_act(s, acc):
        a, b = acc
        for r in range(pieces):
            rows = slice(r * CHUNK, (r + 1) * CHUNK)
            xh = (z1[s, rows, :] - mean_two) * scale_two
            v = xh * gain_two + shift_two
            t = jnp.tanh(0.851 * v)
            h2[s, rows, :] = (0.5 * v + (0.5 * v) * t).astype(BF)
            d = gw[s, rows, :] * (0.5 + 0.5 * t + (0.4255 * v) * (1.0 - t * t))
            z1[s, rows, :] = xh
            gw[s, rows, :] = d
            a = a + fold(d)
            b = b + fold(d * xh)
        return a, b

    zero = jnp.zeros((8, hid), F32)
    a, b = lax.fori_loop(0, seqs, second_act, (zero, zero))
    fs3[0:1, :] = jnp.sum(a, axis=0, keepdims=True)
    fs3[1:2, :] = jnp.sum(b, axis=0, keepdims=True)
    fs3[2:3, :] = act_sum[:, :hid]
    fs3[3:4, :] = act_sum[:, hid:]

    def point_work():
        flat = grad[...].reshape(seqs * bins, chans)
        dwp[...] = dot(h2[...].reshape(seqs * bins, hid), flat, 0, 0)
        if inside:
            for d in far_first:
                point_f(d)

        def branch(i, _):
            some = pl.ds(i * 2, 2)
            more = dot(h2[some].reshape(2 * bins, hid), wp[...], 1, 0) + par[0:1, :]
            out[some] = (xin[some].astype(F32) + more.reshape(2, bins, chans)).astype(BF)
            return 0

        lax.fori_loop(0, seqs // 2, branch, 0)
        if inside:
            for d in far_first:
                point_x(d)

    both = plain_sum(2, fs3, fr3, cs3, cr3, point_work)
    shift_total, gain_total = both[0:1, :], both[1:2, :]
    owned(3, narrow_row, gain_total)
    owned(4, narrow_row, shift_total)
    outer = scale_two * gain_two
    level = shift_total / count[:, :hid]
    slant = gain_total / count[:, :hid]

    dz_sum = outer * (
        fs3[0:1, :] - level * count_narrow - slant * (sum_two - count_narrow * mean_two) * scale_two
    )
    typical = jnp.concatenate([both[2:3, :], both[3:4, :]], axis=1) / (nb * nz * nf * seqs * bins)
    typical = jnp.concatenate([typical, jnp.zeros((7, chans), F32)], axis=0)
    middle_act = lax.dot_general(
        typical, jnp.ones((8, 128), F32), (((0,), (0,)), ((), ())),
        precision=lax.Precision.HIGHEST, preferred_element_type=F32,
    )
    mcol[...] = middle_act

    def conv_grad(some, s, _):
        for r in some:
            rows = slice(r * CHUNK, (r + 1) * CHUNK)
            d = outer * (gw[s, rows, :] - mask(s, r, narrow) * (level + z1[s, rows, :] * slant))
            dz[s, PAD + r * CHUNK : PAD + (r + 1) * CHUNK, :] = d.astype(BF)
        return 0

    ends_of = -(-STEP // CHUNK)
    outside = [*range(ends_of), *range(pieces - ends_of, pieces)]
    lax.fori_loop(0, seqs, functools.partial(conv_grad, outside), 0)
    for s in range(seqs):
        zs_out[(0,) + packed(s)] = dz[s, PAD : PAD + STEP, :]
        zs_out[(1,) + packed(s)] = dz[s, PAD + bins - STEP : PAD + bins, :]
    z_first, z_onward, z_last = edges(zs_out, zs_in, mid_z, zsem)
    z_first()

    lax.fori_loop(0, seqs, functools.partial(conv_grad, range(ends_of, pieces - ends_of)), 0)

    def rank_one(first, count, row):
        m = mcol[pl.ds(pl.multiple_of(first, 8), count), :]
        return jnp.concatenate([m] * narrow, axis=1) * row

    def shift_taps(s, _):
        for k in range(3):
            first = PAD - (k - 1) * STEP
            taps[s, :, k * hid : (k + 1) * hid] = dz[s, first : first + bins, :]
        return 0

    lax.fori_loop(0, seqs, shift_taps, 0)

    def kernel_grad(m, _):
        cols = pl.ds(pl.multiple_of(m * hid, 128), hid)
        left = h1[:, PAD : PAD + bins, cols].reshape(seqs * bins, hid)
        g = dot(left, taps[...].reshape(seqs * bins, 3 * hid), 0, 0)
        for k in range(3):
            part = g[:, k * hid : (k + 1) * hid]
            if inside:
                part = part - rank_one(m * hid, hid, dz_sum)
            dwd[pl.ds(pl.multiple_of(k * chans + m * hid, 128), hid), :] = part
        return 0

    lax.fori_loop(0, 1, kernel_grad, 0)
    z_onward()
    if inside:
        for d in far_first:
            point_z(d)
    lax.fori_loop(1, chans // hid, kernel_grad, 0)
    if inside:
        point_a()

    z_last()

    @pl.when(bi < nb - 1)
    def _():
        for s in range(seqs):
            upper[s, PAD - STEP :, :] = zs_in[(0,) + packed(s)]

    @pl.when(bi > 0)
    def _():
        for s in range(seqs):
            lower[s, 0:STEP, :] = zs_in[(1,) + packed(s)]

    after, ahead = upper[...], lower[...]
    taps[:, bins - PAD :, 0:hid] = taps[:, bins - PAD :, 0:hid] + after
    taps[:, 0:PAD, 2 * hid :] = taps[:, 0:PAD, 2 * hid :] + ahead
    after = after.reshape(seqs * PAD, hid)
    ahead = ahead.reshape(seqs * PAD, hid)

    def kernel_edge(m, _):
        cols = pl.ds(pl.multiple_of(m * 256, 256), 256)
        for k, rows, right in ((0, bins, after), (2, PAD, ahead)):
            left = h1[:, rows : rows + PAD, cols].reshape(seqs * PAD, 256)
            where = pl.ds(pl.multiple_of(k * chans + m * 256, 256), 256)
            dwd[where, :] = dwd[where, :] + dot(left, right, 0, 0)
        return 0

    lax.fori_loop(0, chans // 256, kernel_edge, 0)
    if inside:
        for d in far_first:
            wide_f(d)
        wide_x(far_first[0])

    def back_conv(i):
        some = pl.ds(i * 2, 2)
        left = taps[some].reshape(2 * bins, 3 * hid)
        dg[some] = dot(left, wt[...], 1, 0).reshape(2, bins, chans)

    def back_act(i, acc):
        a, b = acc
        for s in (2 * i, 2 * i + 1):
            for r in range(pieces):
                rows = slice(r * CHUNK, (r + 1) * CHUNK)
                xc = xin[s, rows, :].astype(F32) - mean_one
                v = xc * gain_one + shift_one
                t = jnp.tanh(0.851 * v)
                d = dg[s, rows, :] * (0.5 + 0.5 * t + (0.4255 * v) * (1.0 - t * t))
                dg[s, rows, :] = d
                a = a + fold(d)
                b = b + fold(d * (xc * scale_one))
        return a, b

    def input_side(i, acc):
        acc = back_act(i - 1, acc)
        back_conv(i)
        return acc

    zero = jnp.zeros((8, chans), F32)
    back_conv(0)
    if inside:
        for d in far_first[1:]:
            wide_x(d)
    a, b = lax.fori_loop(1, seqs // 2, input_side, (zero, zero))
    a, b = back_act(seqs // 2 - 1, (a, b))
    if inside:
        wide_z(far_first[0])
    fs4[0:1, :] = jnp.sum(a, axis=0, keepdims=True)
    fs4[1:2, :] = jnp.sum(b, axis=0, keepdims=True)

    def weight_work():
        if inside:
            for d in far_first[1:]:
                wide_z(d)

    mine = mate_copies(3, fs4, fr4)
    start(mine)
    wait(mine)
    total = fs4[...]
    for j in range(len(mates)):
        total = total + fr4[j]
    cs4[...] = total
    far = chip_copies(3, cs4, cr4, lambda b, z: z == 0)
    side = [j for j, (b, z) in enumerate(chips) if z == 0]
    start(far)
    weight_work()
    wait(far)
    for j in side:
        total = total + cr4[j]
    fs4[...] = total
    far = chip_copies(3, fs4, cr4, lambda b, z: b == 0)
    side = [j for j, (b, z) in enumerate(chips) if b == 0]
    start(far)
    if inside:
        wide_a()
    wait(far)
    for j in side:
        total = total + cr4[j]
    both = total
    shift_total, gain_total = both[0:1, :], both[1:2, :]
    owned(1, wide_row, gain_total)
    owned(2, wide_row, shift_total)
    level = shift_total / count
    slant = gain_total / count

    def input_grad(s, _):
        for r in range(pieces):
            rows = slice(r * CHUNK, (r + 1) * CHUNK)
            xc = xin[s, r * CHUNK : (r + 1) * CHUNK, :].astype(F32) - mean_one
            d = dg[s, rows, :] - mask(s, r, wide) * (level + (xc * scale_one) * slant)
            gin[s, rows, :] = (grad[s, rows, :].astype(F32) + gain_one * d).astype(BF)
        return 0

    lax.fori_loop(0, seqs, input_grad, 0)

    if inside:

        def put_wide(j, v):
            dwd_out[j * tall : (j + 1) * tall, :] = v

        def put_point(j, v):
            dwp_out[j % 2 * small : (j % 2 + 1) * small, j // 2 * hid : (j // 2 + 1) * hid] = v

        point_end(put_point)
        wide_end(put_wide)
    for c in par_far:
        c.wait_send()
    for k in range(nz):
        for c in par_near[k]:
            c.wait_send()
    if inside:
        spread_d.end()
        spread_p.end()


def call(sizes, inside, *refs):
    refs = list(refs)
    first = 17 + 17 + 16 + 9
    if inside:
        red = first + 6
        refs[red : red + 14] = [refs[red : red + 7], refs[red + 7 : red + 14]]
    else:
        refs[first:first] = [refs[first - 7], refs[first - 6], None, None, refs[14], refs[15], None, None]
    block(sizes, *refs)


def write_out(out, gin, dwd, dwp, tile, *refs):
    sem = refs[9]
    copies = [
        pltpu.make_async_copy(src, dst, sem.at[i])
        for i, (src, dst) in enumerate(zip((out, gin, dwd, dwp), refs[:4]))
    ]
    for c in copies:
        c.start()
    for r, ref in enumerate(refs[4:9]):
        n = ref.shape[0]
        ref[...] = tile[r : r + 1, 0:n].reshape(n)
    for c in copies:
        c.wait()


def local(sizes, x, black, unmap, limit, wd, wp, bias, g1, s1, g2, s2, og):
    nb, nz, nf = sizes
    seqs, bins, chans = x.shape
    hid = wd.shape[1]
    groups = ("batch", "fsdp")
    inside = (
        nf == 2
        and nb == 4
        and wd.shape[0] % (8 * nb) == 0
        and 2 * wp.shape[0] % (8 * nb) == 0
        and chans == 2 * hid
    )
    if not inside:
        wd = lax.all_gather(wd.astype(BF), groups, axis=0, tiled=True)
        wp = lax.all_gather(wp.astype(BF), groups, axis=0, tiled=True)
    near, far = nf - 1, nb * nz - 1
    steps = 2 * nz if inside else 1
    vmem = pl.BlockSpec(memory_space=pltpu.VMEM)
    hbm = pl.BlockSpec(memory_space=pl.ANY)
    dma = pltpu.SemaphoreType.DMA

    def sums(rows, width):
        return [
            pltpu.VMEM((rows, width), F32),
            pltpu.VMEM((near, rows, width), F32),
            pltpu.VMEM((rows, width), F32),
            pltpu.VMEM((far, rows, width), F32),
        ]

    tall = bins + 2 * PAD
    scratch = [
        pltpu.VMEM(black.shape, jnp.int32),
        pltpu.VMEM(black.shape, jnp.int32),
        pltpu.VMEM(wd.shape, wd.dtype),
        pltpu.VMEM(wp.shape, wp.dtype),
        pltpu.VMEM((nz * nf, 8, 128), F32),
        pltpu.VMEM((8, chans), F32),
        pltpu.VMEM((2, 2, seqs // 2 * STEP, hid), BF),
        pltpu.VMEM((2, 2, seqs // 2 * STEP, hid), BF),
    ]
    scratch.append(pltpu.VMEM((3 * hid, chans), BF))
    if inside:
        scratch += [
            pltpu.VMEM((3 * chans, hid), BF),
            pltpu.VMEM((hid, chans), BF),
            pltpu.VMEM((nz * nf, nb, wd.shape[0] // nb, hid), BF),
            pltpu.VMEM((nz * nf, nb, 2 * wp.shape[0] // nb, hid), BF),
            pltpu.VMEM((3 * chans, hid), F32),
            pltpu.VMEM((hid, chans), F32),
        ]
        for p in (wd.shape[0] // nb, 2 * wp.shape[0] // nb):
            scratch += [
                pltpu.VMEM((nz, nb, p, hid), BF),
                pltpu.VMEM((nz, nb, p, hid), BF),
                pltpu.VMEM((nb - 1, nz, p, hid), BF),
                pltpu.VMEM((nz, p, hid), F32),
                pltpu.VMEM((nz - 1, p, hid), BF),
                pltpu.VMEM((nz - 1, p, hid), BF),
                pltpu.VMEM((nb, p, hid), BF),
            ]
    out, gin, dwd, dwp, tile = pl.pallas_call(
        functools.partial(call, sizes, inside),
        out_shape=(
            pltpu.VMEM(x.shape, BF),
            pltpu.VMEM(x.shape, BF),
            pltpu.VMEM(wd.shape if inside else (3 * chans, hid), F32),
            pltpu.VMEM(wp.shape if inside else (hid, chans), F32),
            pltpu.VMEM((8, 128), F32),
        ),
        in_specs=[hbm] * 4 + [pl.BlockSpec(memory_space=pltpu.SMEM)] + [hbm] * 2 + [vmem] * 5,
        out_specs=(vmem,) * 5,
        scratch_shapes=[
            pltpu.VMEM((seqs, bins, chans), BF),
            pltpu.VMEM((seqs, bins, chans), BF),
            pltpu.VMEM((seqs, bins, 128), F32),
            pltpu.VMEM((seqs, tall, chans), BF),
            pltpu.VMEM((seqs, bins, hid), F32),
            pltpu.VMEM((seqs, bins, hid), F32),
            pltpu.VMEM((seqs, bins, hid), BF),
            pltpu.VMEM((seqs, tall, hid), BF),
            pltpu.VMEM((seqs, bins, 3 * hid), BF),
            pltpu.VMEM((seqs, bins, chans), F32),
            pltpu.VMEM((2, 2, seqs // 2 * STEP, hid), BF),
            pltpu.VMEM((2, 2, seqs // 2 * STEP, hid), BF),
            pltpu.VMEM((seqs // 2 * STEP, hid), BF),
            pltpu.VMEM((seqs // 2 * STEP, hid), BF),
            pltpu.VMEM((seqs, PAD, hid), BF),
            pltpu.VMEM((seqs, PAD, hid), BF),
            pltpu.VMEM((chans, 128), F32),
        ]
        + sums(2, chans + 128) + sums(4, hid) + sums(4, hid) + sums(2, chans)
        + scratch
        + [
            dma((seqs,)), dma((seqs,)), dma((4,)),
            dma((2, 5)), dma((2, 5)),
            dma((4, near)), dma((4, near)), dma((4, far)), dma((4, far)),
            dma((2, steps)), dma((2, steps)), dma((2, steps, nb)), dma((2, steps, nb)),
            dma((2, steps, nb)), dma((2, steps, nb)),
            dma((nz,)), dma((nz,)), dma((near, nz)), dma((near, nz)),
            dma((2, steps)), dma((2, steps)), dma((2, nb, steps)), dma((2, nb, steps)),
            dma((2, steps)), dma((2, steps)), dma((2, nb)), dma((2, nb)),
        ],
        compiler_params=pltpu.CompilerParams(
            collective_id=0, has_side_effects=True, vmem_limit_bytes=(54 if inside else 50) * 2**20
        ),
    )(x, og, black, unmap, limit, wd, wp, bias, g1, s1, g2, s2)
    if not inside:
        dwd, dwp = lax.psum((dwd, dwp), "bins")
        dwd = lax.psum_scatter(dwd, groups, scatter_dimension=0, tiled=True)
        dwp = lax.psum_scatter(dwp, groups, scatter_dimension=0, tiled=True)
    results = (x, x, dwd, dwp, bias, g1, s1, g2, s2)
    kinds = (BF, BF) + (F32,) * 7
    return pl.pallas_call(
        write_out,
        out_shape=tuple(jax.ShapeDtypeStruct(r.shape, t) for r, t in zip(results, kinds)),
        in_specs=[vmem] * 5,
        out_specs=(hbm,) * 4 + (vmem,) * 5,
        scratch_shapes=[dma((4,))],
        compiler_params=pltpu.CompilerParams(vmem_limit_bytes=2**20),
    )(*(pltpu.with_memory_space_constraint(v, pltpu.VMEM) for v in (out, gin, dwd, dwp, tile)))


def solution(mesh):
    sizes = (mesh.shape["bins"], mesh.shape["batch"], mesh.shape["fsdp"])
    rows = P(("batch", "fsdp"))
    track = P(("batch", "fsdp"), "bins", None)
    table = P(("batch", "fsdp"), None)
    return jax.shard_map(
        functools.partial(local, sizes),
        mesh=mesh,
        in_specs=(track, P(("batch", "fsdp"), "bins"), P(("batch", "fsdp"), "bins"), rows,
                  table, table, rows, rows, rows, rows, rows, track),
        out_specs=(track, track, table, table, rows, rows, rows, rows, rows),
        check_vma=False,
    )
```

```python
import functools

import jax
import jax.numpy as jnp
from jax import lax
from jax.experimental import pallas as pl
from jax.experimental.pallas import tpu as pltpu
from jax.sharding import PartitionSpec as P

STEP = 26
EPS = 1e-5
PAD = 32
CHUNK = 16
MESH = pl.DeviceIdType.MESH
BF = jnp.bfloat16
F32 = jnp.float32


def dot(a, b, ca, cb):
    return lax.dot_general(a, b, (((ca,), (cb,)), ((), ())), preferred_element_type=F32)


def fold(v):
    rows, width = v.shape
    return jnp.sum(v.reshape(rows // 8, 8, width), axis=0)


def merge(entries):
    total = functools.reduce(jnp.add, [e[0] for e in entries])
    count = functools.reduce(jnp.add, [e[2] for e in entries])
    mean = total / jnp.maximum(count, 1.0)
    square = functools.reduce(jnp.add, [e[1] for e in entries])
    for s, _, n in entries:
        gap = s / jnp.maximum(n, 1.0) - mean
        square = square + n * gap * gap
    return total, square, count


def block(
    sizes,
    x_hbm, og_hbm, black_hbm, unmap_hbm, limit, wd_hbm, wp_hbm, bias_in, g1_in, s1_in, g2_in, s2_in,
    out, gin, dwd_out, dwp_out, tile_out,
    xin, grad, vm, h1, z1, gw, h2, dz, taps, dg, zs_out, zs_in, mid_e, mid_z, upper, lower, mcol,
    fs1, fr1, cs1, cr1, fs2, fr2, cs2, cr2, fs3, fr3, cs3, cr3, fs4, fr4, cs4, cr4,
    black, unmap, wd_own, wp_own, pall, par, es, er,
    wt, wd, wp, wall_d, wall_p, dwd, dwp, dwd_red, dwp_red,
    xsem, gsem, lsem, hsem, zsem, fss, frs, css, crs,
    wzs, wzr, wcs, wcr, wfs, wfr, pzs, pzr, pfs, pfr,
    rfs, rfr, rxs, rxr, rzs, rzr, ras, rar,
):
    nb, nz, nf = sizes
    inside = wall_d is not None
    seqs, bins, chans = grad.shape
    hid = z1.shape[2]
    wide, narrow = chans // 128, hid // 128
    pieces = bins // CHUNK
    bi, zi, fi = lax.axis_index("bins"), lax.axis_index("batch"), lax.axis_index("fsdp")

    def load_x(s):
        return pltpu.make_async_copy(x_hbm.at[s], xin.at[s], xsem.at[s])

    def load_g(s):
        return pltpu.make_async_copy(og_hbm.at[s], grad.at[s], gsem.at[s])

    small_loads = [
        pltpu.make_async_copy(src, dst, lsem.at[i])
        for i, (src, dst) in enumerate(
            [(black_hbm, black), (unmap_hbm, unmap), (wd_hbm, wd_own), (wp_hbm, wp_own)]
        )
    ]

    for c in small_loads:
        c.start()
    for s in range(seqs):
        load_x(s).start()
    for s in range(seqs):
        load_g(s).start()

    mates = [(k,) for k in range(1, nf)]
    chips = [(b, z) for z in range(nz) for b in range(nb) if (b, z) != (0, 0)]

    def mate(k):
        return {"fsdp": lax.rem(fi + k, nf)}

    def chip(b, z):
        return {"bins": lax.rem(bi + b, nb), "batch": lax.rem(zi + z, nz)}

    upper[...] = jnp.zeros_like(upper)
    lower[...] = jnp.zeros_like(lower)
    dz[:, 0:PAD, :] = jnp.zeros((seqs, PAD, hid), BF)
    dz[:, PAD + bins : PAD + bins + PAD, :] = jnp.zeros((seqs, PAD, hid), BF)
    barrier = pltpu.get_barrier_semaphore()
    for (k,) in mates:
        pl.semaphore_signal(barrier, inc=1, device_id=mate(k), device_id_type=MESH)
    for b, z in chips:
        pl.semaphore_signal(barrier, inc=1, device_id=chip(b, z), device_id_type=MESH)

    def start(copies):
        for c in copies:
            c.start()

    def wait(copies):
        for c in copies:
            c.wait_recv()
        for c in copies:
            c.wait_send()

    own = zi * nf + fi
    pall[own] = jnp.zeros((8, 128), F32)
    for r, ref in enumerate((bias_in, g1_in, s1_in, g2_in, s2_in)):
        n = ref.shape[0]
        pall[own, r : r + 1, 0:n] = ref[...].astype(BF).astype(F32).reshape(1, n)
    small_loads[2].wait()
    small_loads[3].wait()
    share = wp_own.shape[0]
    if inside:
        base = wd_own.shape[0]
        tall, small = base // nb, 2 * share // nb
        for j in range(nb):
            wall_d[own, j] = wd_own[j * tall : (j + 1) * tall, :].astype(BF)
            first, col = j % 2 * small, j // 2 * hid
            wall_p[own, j] = wp_own[first : first + small, col : col + hid].astype(BF)

    def before(i, k, n):
        return lax.rem(i + n - k, n)

    hops = [h for k in range(1, nz) for h in (k, -k)]

    def sends(h):
        return (zi + h >= 0) & (zi + h < nz)

    def receives(h):
        return (zi - h >= 0) & (zi - h < nz)

    def send_to(src, dst, ssem, rsem, where):
        return pltpu.make_async_remote_copy(
            src_ref=src, dst_ref=dst, send_sem=ssem, recv_sem=rsem,
            device_id=where, device_id_type=MESH,
        )

    def send(ref, ssem, rsem, where):
        return send_to(ref, ref, ssem, rsem, where)

    def along(k):
        return {"batch": lax.rem(zi + k, nz)}

    def slot(z, f):
        return z * nf + f

    par_far = [send(pall.at[own], pzs.at[k], pzr.at[k], along(k)) for k in range(1, nz)]
    par_near = [
        [
            send(pall.at[slot(before(zi, k, nz), fi)], pfs.at[j, k], pfr.at[j, k], mate(m))
            for j, (m,) in enumerate(mates)
        ]
        for k in range(nz)
    ]

    class Spread:
        def __init__(self, i, ref):
            def part(h, b):
                return ref.at[slot(zi - h, fi), before(bi, b, nb)]

            n = len(hops)
            self.far = {
                h: send(part(0, 0), wzs.at[i, k], wzr.at[i, k], {"batch": zi + h})
                for k, h in enumerate(hops)
            }
            self.side = {
                h: [
                    send(part(h, 0), wcs.at[i, k, b], wcr.at[i, k, b], {"bins": lax.rem(bi + b, nb)})
                    for b in range(1, nb)
                ]
                for k, h in enumerate(hops)
            }
            self.own = send(ref.at[own], wfs.at[i, n, 0], wfr.at[i, n, 0], mate(1))
            self.near = {
                h: [send(part(h, b), wfs.at[i, k, b], wfr.at[i, k, b], mate(1)) for b in range(nb)]
                for k, h in enumerate(hops)
            }

        def begin(self):
            for_hops(sends, lambda h: self.far[h].start())
            self.own.start()

        def arrive(self, h):
            self.far[h].wait_recv()
            self.near[h][0].start()

        def across(self, h):
            start(self.side[h])

        def hand_on(self):
            def near_work(h):
                for b in range(1, nb):
                    self.side[h][b - 1].wait_recv()
                    self.near[h][b].start()

            def near_end(h):
                for c in self.near[h]:
                    c.wait_recv()

            for_hops(receives, near_work)
            for_hops(receives, near_end)
            self.own.wait_recv()

        def end(self):
            def sent(h):
                for c in self.side[h] + self.near[h]:
                    c.wait_send()

            for_hops(sends, lambda h: self.far[h].wait_send())
            for_hops(receives, sent)
            self.own.wait_send()

    if inside:
        spread_d, spread_p = Spread(0, wall_d), Spread(1, wall_p)

    def for_hops(test, do):
        for h in hops if inside else ():
            pl.when(test(h))(functools.partial(do, h))

    pl.semaphore_wait(barrier, len(mates) + len(chips))
    if inside:
        spread_d.begin()
    start(par_far)
    start(par_near[0])

    small_loads[0].wait()
    small_loads[1].wait()
    ends = jnp.zeros((seqs, bins), jnp.int32)
    for s in range(seqs):
        row = lax.broadcasted_iota(jnp.int32, (seqs, bins), 0)
        ends = jnp.where(row == s, limit[s], ends)
    place = bi * bins + lax.broadcasted_iota(jnp.int32, (seqs, bins), 1)
    keep = (black[...] == 0) & (unmap[...] == 0) & (place < ends)
    columns = jnp.transpose(keep.astype(F32))
    tally = jnp.zeros((8, 128), F32)
    for s in range(seqs):
        lanes = jnp.broadcast_to(columns[:, s : s + 1], (bins, 128))
        vm[s] = lanes
        tally = tally + fold(lanes)
    own_count = jnp.sum(tally, axis=0, keepdims=True)

    def mask(s, r, copies):
        m = vm[s, r * CHUNK : (r + 1) * CHUNK, :]
        return jnp.concatenate([m] * copies, axis=1)

    low, high = lax.rem(bi + nb - 1, nb), lax.rem(bi + 1, nb)

    relay = nb == 4
    half = seqs // 2

    def edge_copy(src, dst, sems, i, where):
        return pltpu.make_async_remote_copy(
            src_ref=src, dst_ref=dst, send_sem=sems.at[0, i], recv_sem=sems.at[1, i],
            device_id={"bins": where}, device_id_type=MESH,
        )

    def edges(src, dst, mid, sems):
        to_low = [edge_copy(src.at[0, i], dst.at[0, i], sems, i, low) for i in range(2)]
        to_high = [edge_copy(src.at[1, i], dst.at[1, i], sems, 2 + i, high) for i in range(2)]
        by_0 = [edge_copy(src.at[0, 1], mid, sems, 4, 0), edge_copy(mid, dst.at[0, 1], sems, 1, 1)]
        by_3 = [edge_copy(src.at[1, 1], mid, sems, 4, nb - 1), edge_copy(mid, dst.at[1, 1], sems, 3, nb - 2)]

        def sides(do_low, do_high):
            pl.when(bi > 0)(do_low)
            pl.when(bi < nb - 1)(do_high)

        def first():
            def _low():
                to_low[0].start()
                if not relay:
                    to_low[1].start()

            def _high():
                to_high[0].start()
                if not relay:
                    to_high[1].start()

            sides(_low, _high)
            if relay:
                pl.when((bi == 1) | (bi == 3))(to_low[1].start)
                pl.when((bi == 0) | (bi == 2))(to_high[1].start)
                pl.when(bi == 2)(by_0[0].start)
                pl.when(bi == 1)(by_3[0].start)

        def onward():
            def _pass(copies):
                copies[0].wait_recv()
                copies[1].start()

            if relay:
                pl.when(bi == 0)(functools.partial(_pass, by_0))
                pl.when(bi == nb - 1)(functools.partial(_pass, by_3))

        def last():
            def _from_low():
                for c in to_high:
                    c.wait_recv()
                to_low[0].wait_send()
                if not relay:
                    to_low[1].wait_send()

            def _from_high():
                for c in to_low:
                    c.wait_recv()
                to_high[0].wait_send()
                if not relay:
                    to_high[1].wait_send()

            sides(_from_low, _from_high)
            if relay:
                pl.when((bi == 1) | (bi == 3))(to_low[1].wait_send)
                pl.when((bi == 0) | (bi == 2))(to_high[1].wait_send)
                pl.when(bi == 2)(by_0[0].wait_send)
                pl.when(bi == 1)(by_3[0].wait_send)
                pl.when(bi == 0)(by_0[1].wait_send)
                pl.when(bi == nb - 1)(by_3[1].wait_send)

        return first, onward, last

    def packed(s):
        first = s % half * STEP
        return s // half, slice(first, first + STEP), slice(None)

    def mate_copies(i, src, dst):
        return [
            pltpu.make_async_remote_copy(
                src_ref=src, dst_ref=dst.at[j], send_sem=fss.at[i, j], recv_sem=frs.at[i, j],
                device_id=mate(k), device_id_type=MESH,
            )
            for j, (k,) in enumerate(mates)
        ]

    def chip_copies(i, src, dst, only=lambda b, z: True):
        return [
            pltpu.make_async_remote_copy(
                src_ref=src, dst_ref=dst.at[j], send_sem=css.at[i, j], recv_sem=crs.at[i, j],
                device_id=chip(b, z), device_id_type=MESH,
            )
            for j, (b, z) in enumerate(chips)
            if only(b, z)
        ]

    def plain_sum(i, fs, fr, cs, cr, filler):
        mine = mate_copies(i, fs, fr)
        start(mine)
        wait(mine)
        both = fs[...]
        for j in range(len(mates)):
            both = both + fr[j]
        cs[...] = both
        far = chip_copies(i, cs, cr)
        start(far)
        filler()
        wait(far)
        total = cs[...]
        for j in range(len(chips)):
            total = total + cr[j]
        return total

    def reduction(i, bufs, get):
        fs, fr, xr, acc, zs, zr, ga = bufs
        xs = fs
        other = lax.rem(fi + 1, 2)

        def f_copy(d):
            return send_to(fs.at[d], fr.at[d], rfs.at[i, d], rfr.at[i, d], mate(1))

        def x_copy(d, b):
            j = lax.rem(bi + b, nb)
            return send_to(
                xs.at[d, j], xr.at[b - 1, d], rxs.at[i, b - 1, d], rxr.at[i, b - 1, d], {"bins": j}
            )

        def z_copy(d):
            return send_to(zs.at[d - 1], zr.at[d - 1], rzs.at[i, d], rzr.at[i, d], along(d))

        def a_copy(b):
            return send_to(
                ga.at[bi], ga.at[bi], ras.at[i, b], rar.at[i, b], {"bins": lax.rem(bi + b, nb)}
            )

        def f_send(d):
            z = lax.rem(zi + d, nz)
            for j in range(nb):
                fs[d, j] = get(slot(z, other), j).astype(BF)
            f_copy(d).start()

        def x_send(d):
            z = lax.rem(zi + d, nz)
            f_copy(d).wait()
            for j in range(nb):
                xs[d, j] = (get(slot(z, fi), j) + fr[d, j].astype(F32)).astype(BF)
            acc[d] = get(slot(z, fi), bi) + fr[d, bi].astype(F32)
            for b in range(1, nb):
                x_copy(d, b).start()

        def z_send(d):
            total = acc[d]
            for b in range(1, nb):
                x_copy(d, b).wait_recv()
                total = total + xr[b - 1, d].astype(F32)
            if d:
                zs[d - 1] = total.astype(BF)
                z_copy(d).start()
            else:
                acc[0] = total

        def a_send():
            total = acc[0]
            for d in range(1, nz):
                z_copy(d).wait_recv()
                total = total + zr[d - 1].astype(F32)
            ga[bi] = total.astype(BF)
            for b in range(1, nb):
                a_copy(b).start()

        def finish(put):
            for b in range(1, nb):
                a_copy(b).wait_recv()
            for j in range(nb):
                put(j, ga[j].astype(F32))
            for d in range(nz):
                for b in range(1, nb):
                    x_copy(d, b).wait_send()
                if d:
                    z_copy(d).wait_send()
            for b in range(1, nb):
                a_copy(b).wait_send()

        return f_send, x_send, z_send, a_send, finish

    far_first = list(range(1, nz)) + [0]
    if inside:

        def dwd_get(c, j):
            return dwd[pl.ds(pl.multiple_of(c * base + j * tall, 8), tall), :]

        def dwp_get(c, j):
            rows = pl.ds(pl.multiple_of(c * share + lax.rem(j, 2) * small, 8), small)
            if isinstance(j, int):
                return dwp[rows, j // 2 * hid : (j // 2 + 1) * hid]
            return dwp[rows, pl.ds(pl.multiple_of(j // 2 * hid, 128), hid)]

        wide_f, wide_x, wide_z, wide_a, wide_end = reduction(0, dwd_red, dwd_get)
        point_f, point_x, point_z, point_a, point_end = reduction(1, dwp_red, dwp_get)

    def sums_x(s, acc):
        load_x(s).wait()
        for r in range(pieces):
            xx = xin[s, r * CHUNK : (r + 1) * CHUNK, :].astype(F32)
            acc = acc + fold(xx * mask(s, r, wide))
        return acc

    acc = lax.fori_loop(0, seqs, sums_x, jnp.zeros((8, chans), F32))
    count_wide = jnp.concatenate([own_count] * wide, axis=1)
    count_narrow = jnp.concatenate([own_count] * narrow, axis=1)
    sum_one = jnp.sum(acc, axis=0, keepdims=True)
    local_one = sum_one / jnp.maximum(count_wide, 1.0)

    def squares_x(s, acc):
        for r in range(pieces):
            xx = xin[s, r * CHUNK : (r + 1) * CHUNK, :].astype(F32) - local_one
            acc = acc + fold(xx * xx * mask(s, r, wide))
        return acc

    acc = lax.fori_loop(0, seqs, squares_x, jnp.zeros((8, chans), F32))
    fs1[0:1, :chans] = sum_one
    fs1[1:2, :chans] = jnp.sum(acc, axis=0, keepdims=True)
    fs1[0:1, chans:] = own_count
    fs1[1:2, chans:] = own_count

    def triple(ref):
        n = jnp.concatenate([ref[0:1, chans:]] * wide, axis=1)
        return ref[0:1, :chans], ref[1:2, :chans], n

    mine = mate_copies(0, fs1, fr1)
    start(mine)

    def side_work(h):
        spread_d.arrive(h)
        spread_d.across(h)

    wait(mine)
    s_, q_, n_ = merge([triple(fs1)] + [triple(fr1.at[j]) for j in range(len(mates))])
    cs1[0:1, :chans] = s_
    cs1[1:2, :chans] = q_
    cs1[0:1, chans:] = n_[:, :128]
    cs1[1:2, chans:] = n_[:, :128]
    far = chip_copies(0, cs1, cr1)
    start(far)
    for h in hops if inside else ():
        pl.when(receives(h))(functools.partial(side_work, h))

    def mask_grad(s, acc):
        load_g(s).wait()
        for r in range(pieces):
            rows = slice(r * CHUNK, (r + 1) * CHUNK)
            g = grad[s, rows, :].astype(F32) * mask(s, r, wide)
            acc = acc + fold(g)
            grad[s, rows, :] = g.astype(BF)
        return acc

    acc = lax.fori_loop(0, seqs, mask_grad, jnp.zeros((8, chans), F32))
    own_bias = jnp.sum(acc, axis=0, keepdims=True)

    for k in range(1, nz):
        par_far[k - 1].wait_recv()
        start(par_near[k])
    for k in range(nz):
        for c in par_near[k]:
            c.wait_recv()

    rows = jnp.zeros((8, chans + 256), F32)
    cols = jnp.zeros((8, hid + 256), F32)

    def laid(into, tile, width, index):
        at = index * width
        first, turn = at // 128 * 128, at % 128
        tile = jnp.concatenate([tile, jnp.zeros((8, 128), F32)], axis=1)
        tile = pltpu.roll(tile, turn, 1) if turn else tile
        return jnp.concatenate(
            [t for t in (into[:, :first], into[:, first : first + 256] + tile, into[:, first + 256 :]) if t.shape[1]],
            axis=1,
        )

    for c in range(nz * nf):
        rows = laid(rows, pall[c], bias_in.shape[0], c)
        cols = laid(cols, pall[c], g2_in.shape[0], c)
    par[0:3, :] = rows[0:3, :chans]
    par[3:5, 0:hid] = cols[3:5, :hid]

    wait(far)
    s_, q_, count = merge([triple(cs1)] + [triple(cr1.at[j]) for j in range(len(chips))])
    mean_one = s_ / count
    scale_one = lax.rsqrt(q_ / count + EPS)
    gain_one = par[1:2, :] * scale_one
    shift_one = par[2:3, :]

    h1[:, 0:PAD, :] = jnp.zeros((seqs, PAD, chans), BF)
    h1[:, PAD + bins : PAD + bins + PAD, :] = jnp.zeros((seqs, PAD, chans), BF)

    def first_act(s, acc):
        for r in range(pieces):
            rows = slice(PAD + r * CHUNK, PAD + (r + 1) * CHUNK)
            v = (xin[s, r * CHUNK : (r + 1) * CHUNK, :].astype(F32) - mean_one) * gain_one + shift_one
            v = 0.5 * v + (0.5 * v) * jnp.tanh(0.851 * v)
            h1[s, rows, :] = v.astype(BF)
            acc = acc + fold(v)
        return acc

    acc = lax.fori_loop(0, seqs, first_act, jnp.zeros((8, chans), F32))
    act_sum = jnp.sum(acc, axis=0, keepdims=True)

    if inside:
        spread_p.begin()

    if inside:
        spread_d.hand_on()
        for c in range(nz * nf):
            for j in range(nb):
                first = c * base + j * tall
                wd[first : first + tall, :] = wall_d[c, j]

    def tap(k):
        return wd[k * chans : (k + 1) * chans, :]

    over = h1[:, PAD + bins - STEP : PAD + bins - STEP + PAD, :].reshape(seqs * PAD, chans)
    over = dot(over, tap(0), 1, 0).astype(BF)
    under = h1[:, STEP : STEP + PAD, :].reshape(seqs * PAD, chans)
    under = dot(under, tap(2), 1, 0).astype(BF)
    for s in range(seqs):
        es[(1,) + packed(s)] = over[s * PAD : s * PAD + STEP, :]
        es[(0,) + packed(s)] = under[s * PAD + PAD - STEP : s * PAD + PAD, :]
    e_first, e_onward, e_last = edges(es, er, mid_e, hsem)
    e_first()

    group = seqs // 2

    def conv(i, _):
        some = pl.ds(i * group, group)
        z = None
        for k in range(3):
            first = PAD + (k - 1) * STEP
            left = h1[some, first : first + bins, :].reshape(group * bins, chans)
            part = dot(left, tap(k), 1, 0)
            z = part if z is None else z + part
        z1[some] = z.reshape(group, bins, hid)
        return 0

    lax.fori_loop(0, 1, conv, 0)
    e_onward()
    if inside:
        for_hops(receives, spread_p.arrive)
        for_hops(receives, spread_p.across)
    lax.fori_loop(1, 2, conv, 0)

    e_last()

    @pl.when(bi > 0)
    def _():
        for s in range(seqs):
            z1[s, 0:STEP, :] = z1[s, 0:STEP, :] + er[(1,) + packed(s)].astype(F32)

    @pl.when(bi < nb - 1)
    def _():
        for s in range(seqs):
            z1[s, bins - STEP :, :] = z1[s, bins - STEP :, :] + er[(0,) + packed(s)].astype(F32)

    def sums_z(s, acc):
        for r in range(pieces):
            acc = acc + fold(z1[s, r * CHUNK : (r + 1) * CHUNK, :] * mask(s, r, narrow))
        return acc

    acc = lax.fori_loop(0, seqs, sums_z, jnp.zeros((8, hid), F32))
    sum_two = jnp.sum(acc, axis=0, keepdims=True)
    local_two = sum_two / jnp.maximum(count_narrow, 1.0)

    def squares_z(s, acc):
        for r in range(pieces):
            z = z1[s, r * CHUNK : (r + 1) * CHUNK, :] - local_two
            acc = acc + fold(z * z * mask(s, r, narrow))
        return acc

    acc = lax.fori_loop(0, seqs, squares_z, jnp.zeros((8, hid), F32))
    fs2[0:1, :] = sum_two
    fs2[1:2, :] = jnp.sum(acc, axis=0, keepdims=True)
    fs2[2:3, :] = own_bias[:, :hid]
    fs2[3:4, :] = own_bias[:, hid:]

    def pair(ref, n):
        return ref[0:1, :], ref[1:2, :], jnp.concatenate([n[0:1, chans:]] * narrow, axis=1)

    mine = mate_copies(1, fs2, fr2)
    start(mine)
    wait(mine)
    entries = [pair(fs2, fs1)] + [pair(fr2.at[j], fr1.at[j]) for j in range(len(mates))]
    s_, q_, _ = merge(entries)
    bias_part = fs2[2:4, :]
    for j in range(len(mates)):
        bias_part = bias_part + fr2[j, 2:4, :]
    cs2[0:1, :] = s_
    cs2[1:2, :] = q_
    cs2[2:4, :] = bias_part
    far = chip_copies(1, cs2, cr2)
    start(far)

    def grad_point(i, _):
        some = pl.ds(i * group, group)
        left = grad[some].reshape(group * bins, chans)
        gw[some] = dot(left, wp[...], 1, 1).reshape(group, bins, hid)
        return 0

    for k in range(3):
        wt[k * hid : (k + 1) * hid, :] = jnp.transpose(tap(k))
    if inside:
        spread_p.hand_on()
        for c in range(nz * nf):
            for j in range(nb):
                first, col = c * share + j % 2 * small, j // 2 * hid
                wp[first : first + small, col : col + hid] = wall_p[c, j]
    lax.fori_loop(0, 2, grad_point, 0)

    wait(far)
    entries = [pair(cs2, cs1)] + [pair(cr2.at[j], cr1.at[j]) for j in range(len(chips))]
    s_, q_, _ = merge(entries)
    for j in range(len(chips)):
        bias_part = bias_part + cr2[j, 2:4, :]
    bias_total = jnp.concatenate([bias_part[0:1, :], bias_part[1:2, :]], axis=1)

    def owned(r, n, row):
        row = jnp.concatenate([row, jnp.zeros((1, 256), F32)], axis=1)
        row = jnp.broadcast_to(row, (8, row.shape[1]))
        mine = jnp.zeros((8, 128), F32)
        for c in range(nz * nf):
            first, turn = c * n // 128 * 128, c * n % 128
            piece_ = row[:, first : first + 256]
            piece_ = (pltpu.roll(piece_, 256 - turn, 1) if turn else piece_)[:, :128]
            mine = jnp.where(own == c, piece_, mine)
        tile_out[r : r + 1, :] = mine[0:1, :]

    wide_row, narrow_row = bias_in.shape[0], g2_in.shape[0]
    owned(0, wide_row, bias_total)
    mean_two = s_ / count[:, :hid]
    scale_two = lax.rsqrt(q_ / count[:, :hid] + EPS)
    gain_two = par[3:4, :hid]
    shift_two = par[4:5, :hid]

    def second_act(s, acc):
        a, b = acc
        for r in range(pieces):
            rows = slice(r * CHUNK, (r + 1) * CHUNK)
            xh = (z1[s, rows, :] - mean_two) * scale_two
            v = xh * gain_two + shift_two
            t = jnp.tanh(0.851 * v)
            h2[s, rows, :] = (0.5 * v + (0.5 * v) * t).astype(BF)
            d = gw[s, rows, :] * (0.5 + 0.5 * t + (0.4255 * v) * (1.0 - t * t))
            z1[s, rows, :] = xh
            gw[s, rows, :] = d
            a = a + fold(d)
            b = b + fold(d * xh)
        return a, b

    zero = jnp.zeros((8, hid), F32)
    a, b = lax.fori_loop(0, seqs, second_act, (zero, zero))
    fs3[0:1, :] = jnp.sum(a, axis=0, keepdims=True)
    fs3[1:2, :] = jnp.sum(b, axis=0, keepdims=True)
    fs3[2:3, :] = act_sum[:, :hid]
    fs3[3:4, :] = act_sum[:, hid:]

    def point_work():
        flat = grad[...].reshape(seqs * bins, chans)
        dwp[...] = dot(h2[...].reshape(seqs * bins, hid), flat, 0, 0)
        if inside:
            for d in far_first:
                point_f(d)

        def branch(i, _):
            some = pl.ds(i * 2, 2)
            more = dot(h2[some].reshape(2 * bins, hid), wp[...], 1, 0) + par[0:1, :]
            out[some] = (xin[some].astype(F32) + more.reshape(2, bins, chans)).astype(BF)
            return 0

        lax.fori_loop(0, seqs // 2, branch, 0)
        if inside:
            for d in far_first:
                point_x(d)

    both = plain_sum(2, fs3, fr3, cs3, cr3, point_work)
    shift_total, gain_total = both[0:1, :], both[1:2, :]
    owned(3, narrow_row, gain_total)
    owned(4, narrow_row, shift_total)
    outer = scale_two * gain_two
    level = shift_total / count[:, :hid]
    slant = gain_total / count[:, :hid]

    dz_sum = outer * (
        fs3[0:1, :] - level * count_narrow - slant * (sum_two - count_narrow * mean_two) * scale_two
    )
    typical = jnp.concatenate([both[2:3, :], both[3:4, :]], axis=1) / (nb * nz * nf * seqs * bins)
    typical = jnp.concatenate([typical, jnp.zeros((7, chans), F32)], axis=0)
    middle_act = lax.dot_general(
        typical, jnp.ones((8, 128), F32), (((0,), (0,)), ((), ())),
        precision=lax.Precision.HIGHEST, preferred_element_type=F32,
    )
    mcol[...] = middle_act

    def conv_grad(some, s, _):
        for r in some:
            rows = slice(r * CHUNK, (r + 1) * CHUNK)
            d = outer * (gw[s, rows, :] - mask(s, r, narrow) * (level + z1[s, rows, :] * slant))
            dz[s, PAD + r * CHUNK : PAD + (r + 1) * CHUNK, :] = d.astype(BF)
        return 0

    ends_of = -(-STEP // CHUNK)
    outside = [*range(ends_of), *range(pieces - ends_of, pieces)]
    lax.fori_loop(0, seqs, functools.partial(conv_grad, outside), 0)
    for s in range(seqs):
        zs_out[(0,) + packed(s)] = dz[s, PAD : PAD + STEP, :]
        zs_out[(1,) + packed(s)] = dz[s, PAD + bins - STEP : PAD + bins, :]
    z_first, z_onward, z_last = edges(zs_out, zs_in, mid_z, zsem)
    z_first()

    lax.fori_loop(0, seqs, functools.partial(conv_grad, range(ends_of, pieces - ends_of)), 0)

    def rank_one(first, count, row):
        m = mcol[pl.ds(pl.multiple_of(first, 8), count), :]
        return jnp.concatenate([m] * narrow, axis=1) * row

    def shift_taps(s, _):
        for k in range(3):
            first = PAD - (k - 1) * STEP
            taps[s, :, k * hid : (k + 1) * hid] = dz[s, first : first + bins, :]
        return 0

    lax.fori_loop(0, seqs, shift_taps, 0)

    def kernel_grad(m, _):
        cols = pl.ds(pl.multiple_of(m * hid, 128), hid)
        left = h1[:, PAD : PAD + bins, cols].reshape(seqs * bins, hid)
        g = dot(left, taps[...].reshape(seqs * bins, 3 * hid), 0, 0)
        for k in range(3):
            part = g[:, k * hid : (k + 1) * hid]
            if inside:
                part = part - rank_one(m * hid, hid, dz_sum)
            dwd[pl.ds(pl.multiple_of(k * chans + m * hid, 128), hid), :] = part
        return 0

    lax.fori_loop(0, 1, kernel_grad, 0)
    z_onward()
    if inside:
        for d in far_first:
            point_z(d)
    lax.fori_loop(1, chans // hid, kernel_grad, 0)
    if inside:
        point_a()

    z_last()

    @pl.when(bi < nb - 1)
    def _():
        for s in range(seqs):
            upper[s, PAD - STEP :, :] = zs_in[(0,) + packed(s)]

    @pl.when(bi > 0)
    def _():
        for s in range(seqs):
            lower[s, 0:STEP, :] = zs_in[(1,) + packed(s)]

    after, ahead = upper[...], lower[...]
    taps[:, bins - PAD :, 0:hid] = taps[:, bins - PAD :, 0:hid] + after
    taps[:, 0:PAD, 2 * hid :] = taps[:, 0:PAD, 2 * hid :] + ahead
    after = after.reshape(seqs * PAD, hid)
    ahead = ahead.reshape(seqs * PAD, hid)

    def kernel_edge(m, _):
        cols = pl.ds(pl.multiple_of(m * hid, 128), hid)
        for k, rows, right in ((0, bins, after), (2, PAD, ahead)):
            left = h1[:, rows : rows + PAD, cols].reshape(seqs * PAD, hid)
            where = pl.ds(pl.multiple_of(k * chans + m * hid, 128), hid)
            dwd[where, :] = dwd[where, :] + dot(left, right, 0, 0)
        return 0

    lax.fori_loop(0, chans // hid, kernel_edge, 0)
    if inside:
        for d in far_first:
            wide_f(d)
        wide_x(far_first[0])

    def back_conv(i):
        some = pl.ds(i * 2, 2)
        left = taps[some].reshape(2 * bins, 3 * hid)
        dg[some] = dot(left, wt[...], 1, 0).reshape(2, bins, chans)

    def back_act(i, acc):
        a, b = acc
        for s in (2 * i, 2 * i + 1):
            for r in range(pieces):
                rows = slice(r * CHUNK, (r + 1) * CHUNK)
                xc = xin[s, rows, :].astype(F32) - mean_one
                v = xc * gain_one + shift_one
                t = jnp.tanh(0.851 * v)
                d = dg[s, rows, :] * (0.5 + 0.5 * t + (0.4255 * v) * (1.0 - t * t))
                dg[s, rows, :] = d
                a = a + fold(d)
                b = b + fold(d * (xc * scale_one))
        return a, b

    def input_side(i, acc):
        acc = back_act(i - 1, acc)
        back_conv(i)
        return acc

    zero = jnp.zeros((8, chans), F32)
    back_conv(0)
    if inside:
        for d in far_first[1:]:
            wide_x(d)
    a, b = lax.fori_loop(1, seqs // 2, input_side, (zero, zero))
    a, b = back_act(seqs // 2 - 1, (a, b))
    if inside:
        wide_z(far_first[0])
    fs4[0:1, :] = jnp.sum(a, axis=0, keepdims=True)
    fs4[1:2, :] = jnp.sum(b, axis=0, keepdims=True)

    def weight_work():
        if inside:
            for d in far_first[1:]:
                wide_z(d)

    mine = mate_copies(3, fs4, fr4)
    start(mine)
    wait(mine)
    total = fs4[...]
    for j in range(len(mates)):
        total = total + fr4[j]
    cs4[...] = total
    far = chip_copies(3, cs4, cr4, lambda b, z: z == 0)
    side = [j for j, (b, z) in enumerate(chips) if z == 0]
    start(far)
    weight_work()
    wait(far)
    for j in side:
        total = total + cr4[j]
    fs4[...] = total
    far = chip_copies(3, fs4, cr4, lambda b, z: b == 0)
    side = [j for j, (b, z) in enumerate(chips) if b == 0]
    start(far)
    if inside:
        wide_a()
    wait(far)
    for j in side:
        total = total + cr4[j]
    both = total
    shift_total, gain_total = both[0:1, :], both[1:2, :]
    owned(1, wide_row, gain_total)
    owned(2, wide_row, shift_total)
    level = shift_total / count
    slant = gain_total / count

    def input_grad(s, _):
        for r in range(pieces):
            rows = slice(r * CHUNK, (r + 1) * CHUNK)
            xc = xin[s, r * CHUNK : (r + 1) * CHUNK, :].astype(F32) - mean_one
            d = dg[s, rows, :] - mask(s, r, wide) * (level + (xc * scale_one) * slant)
            gin[s, rows, :] = (grad[s, rows, :].astype(F32) + gain_one * d).astype(BF)
        return 0

    lax.fori_loop(0, seqs, input_grad, 0)

    if inside:

        def put_wide(j, v):
            dwd_out[j * tall : (j + 1) * tall, :] = v

        def put_point(j, v):
            dwp_out[j % 2 * small : (j % 2 + 1) * small, j // 2 * hid : (j // 2 + 1) * hid] = v

        point_end(put_point)
        wide_end(put_wide)
    for c in par_far:
        c.wait_send()
    for k in range(nz):
        for c in par_near[k]:
            c.wait_send()
    if inside:
        spread_d.end()
        spread_p.end()


def call(sizes, inside, *refs):
    refs = list(refs)
    first = 17 + 17 + 16 + 9
    if inside:
        red = first + 6
        refs[red : red + 14] = [refs[red : red + 7], refs[red + 7 : red + 14]]
    else:
        refs[first:first] = [refs[first - 7], refs[first - 6], None, None, refs[14], refs[15], None, None]
    block(sizes, *refs)


def write_out(out, gin, dwd, dwp, tile, *refs):
    sem = refs[9]
    copies = [
        pltpu.make_async_copy(src, dst, sem.at[i])
        for i, (src, dst) in enumerate(zip((out, gin, dwd, dwp), refs[:4]))
    ]
    for c in copies:
        c.start()
    for r, ref in enumerate(refs[4:9]):
        n = ref.shape[0]
        ref[...] = tile[r : r + 1, 0:n].reshape(n)
    for c in copies:
        c.wait()


def local(sizes, x, black, unmap, limit, wd, wp, bias, g1, s1, g2, s2, og):
    nb, nz, nf = sizes
    seqs, bins, chans = x.shape
    hid = wd.shape[1]
    groups = ("batch", "fsdp")
    inside = (
        nf == 2
        and nb == 4
        and wd.shape[0] % (8 * nb) == 0
        and 2 * wp.shape[0] % (8 * nb) == 0
        and chans == 2 * hid
    )
    if not inside:
        wd = lax.all_gather(wd.astype(BF), groups, axis=0, tiled=True)
        wp = lax.all_gather(wp.astype(BF), groups, axis=0, tiled=True)
    near, far = nf - 1, nb * nz - 1
    steps = 2 * nz if inside else 1
    vmem = pl.BlockSpec(memory_space=pltpu.VMEM)
    hbm = pl.BlockSpec(memory_space=pl.ANY)
    dma = pltpu.SemaphoreType.DMA

    def sums(rows, width):
        return [
            pltpu.VMEM((rows, width), F32),
            pltpu.VMEM((near, rows, width), F32),
            pltpu.VMEM((rows, width), F32),
            pltpu.VMEM((far, rows, width), F32),
        ]

    tall = bins + 2 * PAD
    scratch = [
        pltpu.VMEM(black.shape, jnp.int32),
        pltpu.VMEM(black.shape, jnp.int32),
        pltpu.VMEM(wd.shape, wd.dtype),
        pltpu.VMEM(wp.shape, wp.dtype),
        pltpu.VMEM((nz * nf, 8, 128), F32),
        pltpu.VMEM((8, chans), F32),
        pltpu.VMEM((2, 2, seqs // 2 * STEP, hid), BF),
        pltpu.VMEM((2, 2, seqs // 2 * STEP, hid), BF),
    ]
    scratch.append(pltpu.VMEM((3 * hid, chans), BF))
    if inside:
        scratch += [
            pltpu.VMEM((3 * chans, hid), BF),
            pltpu.VMEM((hid, chans), BF),
            pltpu.VMEM((nz * nf, nb, wd.shape[0] // nb, hid), BF),
            pltpu.VMEM((nz * nf, nb, 2 * wp.shape[0] // nb, hid), BF),
            pltpu.VMEM((3 * chans, hid), F32),
            pltpu.VMEM((hid, chans), F32),
        ]
        for p in (wd.shape[0] // nb, 2 * wp.shape[0] // nb):
            scratch += [
                pltpu.VMEM((nz, nb, p, hid), BF),
                pltpu.VMEM((nz, nb, p, hid), BF),
                pltpu.VMEM((nb - 1, nz, p, hid), BF),
                pltpu.VMEM((nz, p, hid), F32),
                pltpu.VMEM((nz - 1, p, hid), BF),
                pltpu.VMEM((nz - 1, p, hid), BF),
                pltpu.VMEM((nb, p, hid), BF),
            ]
    out, gin, dwd, dwp, tile = pl.pallas_call(
        functools.partial(call, sizes, inside),
        out_shape=(
            pltpu.VMEM(x.shape, BF),
            pltpu.VMEM(x.shape, BF),
            pltpu.VMEM(wd.shape if inside else (3 * chans, hid), F32),
            pltpu.VMEM(wp.shape if inside else (hid, chans), F32),
            pltpu.VMEM((8, 128), F32),
        ),
        in_specs=[hbm] * 4 + [pl.BlockSpec(memory_space=pltpu.SMEM)] + [hbm] * 2 + [vmem] * 5,
        out_specs=(vmem,) * 5,
        scratch_shapes=[
            pltpu.VMEM((seqs, bins, chans), BF),
            pltpu.VMEM((seqs, bins, chans), BF),
            pltpu.VMEM((seqs, bins, 128), F32),
            pltpu.VMEM((seqs, tall, chans), BF),
            pltpu.VMEM((seqs, bins, hid), F32),
            pltpu.VMEM((seqs, bins, hid), F32),
            pltpu.VMEM((seqs, bins, hid), BF),
            pltpu.VMEM((seqs, tall, hid), BF),
            pltpu.VMEM((seqs, bins, 3 * hid), BF),
            pltpu.VMEM((seqs, bins, chans), F32),
            pltpu.VMEM((2, 2, seqs // 2 * STEP, hid), BF),
            pltpu.VMEM((2, 2, seqs // 2 * STEP, hid), BF),
            pltpu.VMEM((seqs // 2 * STEP, hid), BF),
            pltpu.VMEM((seqs // 2 * STEP, hid), BF),
            pltpu.VMEM((seqs, PAD, hid), BF),
            pltpu.VMEM((seqs, PAD, hid), BF),
            pltpu.VMEM((chans, 128), F32),
        ]
        + sums(2, chans + 128) + sums(4, hid) + sums(4, hid) + sums(2, chans)
        + scratch
        + [
            dma((seqs,)), dma((seqs,)), dma((4,)),
            dma((2, 5)), dma((2, 5)),
            dma((4, near)), dma((4, near)), dma((4, far)), dma((4, far)),
            dma((2, steps)), dma((2, steps)), dma((2, steps, nb)), dma((2, steps, nb)),
            dma((2, steps, nb)), dma((2, steps, nb)),
            dma((nz,)), dma((nz,)), dma((near, nz)), dma((near, nz)),
            dma((2, steps)), dma((2, steps)), dma((2, nb, steps)), dma((2, nb, steps)),
            dma((2, steps)), dma((2, steps)), dma((2, nb)), dma((2, nb)),
        ],
        compiler_params=pltpu.CompilerParams(
            collective_id=0, has_side_effects=True, vmem_limit_bytes=(54 if inside else 50) * 2**20
        ),
    )(x, og, black, unmap, limit, wd, wp, bias, g1, s1, g2, s2)
    if not inside:
        dwd, dwp = lax.psum((dwd, dwp), "bins")
        dwd = lax.psum_scatter(dwd, groups, scatter_dimension=0, tiled=True)
        dwp = lax.psum_scatter(dwp, groups, scatter_dimension=0, tiled=True)
    results = (x, x, dwd, dwp, bias, g1, s1, g2, s2)
    kinds = (BF, BF) + (F32,) * 7
    return pl.pallas_call(
        write_out,
        out_shape=tuple(jax.ShapeDtypeStruct(r.shape, t) for r, t in zip(results, kinds)),
        in_specs=[vmem] * 5,
        out_specs=(hbm,) * 4 + (vmem,) * 5,
        scratch_shapes=[dma((4,))],
        compiler_params=pltpu.CompilerParams(vmem_limit_bytes=2**20),
    )(*(pltpu.with_memory_space_constraint(v, pltpu.VMEM) for v in (out, gin, dwd, dwp, tile)))


def solution(mesh):
    sizes = (mesh.shape["bins"], mesh.shape["batch"], mesh.shape["fsdp"])
    rows = P(("batch", "fsdp"))
    track = P(("batch", "fsdp"), "bins", None)
    table = P(("batch", "fsdp"), None)
    return jax.shard_map(
        functools.partial(local, sizes),
        mesh=mesh,
        in_specs=(track, P(("batch", "fsdp"), "bins"), P(("batch", "fsdp"), "bins"), rows,
                  table, table, rows, rows, rows, rows, rows, track),
        out_specs=(track, track, table, table, rows, rows, rows, rows, rows),
        check_vma=False,
    )
```
